32 devices in a mesh: dp: 16 (over z, y, x), mp: 2 (over core).
Axes of the slice: x: 2, y: 2, z: 4, core: 2. Of those that a mesh axis runs over, the one named last changes fastest.
Arguments:
- layer_in: bfloat16 [8192, 2048], P(('dp', 'mp')), may hold values from -6 to 6
- out_grad: bfloat16 [8192, 2048], P(('dp', 'mp')), may hold values from -6 to 6
- parents: int32 [2, 7], replicated, may hold values from 0 to 5, as said below
- lengths: int32 [2, 7], replicated, may hold values from 1 to 2048, 4096 in all within a row
- attn_gain: bfloat16 [2048], P(('dp', 'mp')), may hold values from 0.099609375 to 1.8984375
- mlp_gain: bfloat16 [2048], P(('dp', 'mp')), may hold values from 0.099609375 to 1.8984375
- query_norm_gain: bfloat16 [128], P(('dp', 'mp')), may hold values from 0.099609375 to 1.8984375
- key_gain: bfloat16 [128], P(('dp', 'mp')), may hold values from 0.099609375 to 1.8984375
- query_weight: bfloat16 [2048, 2048], P('dp', 'mp'), may hold values from -0.125 to 0.125
- key_matrix: bfloat16 [2048, 1024], P('dp', 'mp'), may hold values from -0.125 to 0.125
- value_matrix: bfloat16 [2048, 1024], P('dp', 'mp'), may hold values from -0.125 to 0.125
- headgate_weight: bfloat16 [2048, 16], P('dp', 'mp'), may hold values from -0.125 to 0.125
- output_weight: bfloat16 [2048, 2048], P('mp', 'dp'), may hold values from -0.75 to 0.75
- gate_weight: bfloat16 [2048, 6144], P('dp', 'mp'), may hold values from -0.125 to 0.125
- up_weight: bfloat16 [2048, 6144], P('dp', 'mp'), may hold values from -0.125 to 0.125
- down_weight: bfloat16 [6144, 2048], P('mp', 'dp'), may hold values from -0.078125 to 0.078125
Outputs:
- layer_out: bfloat16 [8192, 2048], P(('dp', 'mp'))
- input_grad: bfloat16 [8192, 2048], P(('dp', 'mp'))
- attn_gain_grad: float32 [2048], P(('dp', 'mp'))
- mlp_gain_grad: float32 [2048], P(('dp', 'mp'))
- query_gain_grad: float32 [128], P(('dp', 'mp'))
- key_gain_grad: float32 [128], P(('dp', 'mp'))
- query_weight_grad: float32 [2048, 2048], P('dp', 'mp')
- key_weight_grad: float32 [2048, 1024], P('dp', 'mp')
- value_weight_grad: float32 [2048, 1024], P('dp', 'mp')
- headgate_weight_grad: float32 [2048, 16], P('dp', 'mp')
- output_weight_grad: float32 [2048, 2048], P('mp', 'dp')
- gate_weight_grad: float32 [2048, 6144], P('dp', 'mp')
- up_weight_grad: float32 [2048, 6144], P('dp', 'mp')
- down_weight_grad: float32 [6144, 2048], P('mp', 'dp')
The draws below stay inside these ranges and needn't reach their ends.
Inputs may be any that keep to these rules, and one draw needn't show every extreme that they name: Segments are numbered in token order and segment 0 is a tree's root: parents[t, s] is 0 for s <= 1 and s - 1 or s - 2 for s >= 2. `lengths`: each row sums to 4096.
All inputs are finite; a program needn't handle non-finite values.
Results may differ from the reference program's by a relative error of at most 0.035.
Values may be sent and summed in bfloat16 or wider, within the bound.
A program may use at most 256 MiB of HBM per device.

```python
import math
import jax
import jax.numpy as jnp
import numpy as np
from jax import lax

MODEL_WIDTH = 2048
QUERY_HEADS = 16
KEY_VALUE_HEADS = 8
HEAD_SIZE = 128
FF = 6144
SEGS = 7
TREE_TOKENS = 4096
TRUNK = 2048
TREES = 2
TOKENS = 8192


def draw_parents(key, part):
    back = jax.random.randint(key, (TREES, SEGS), 1, 3)
    order = jnp.arange(SEGS, dtype=jnp.int32)[None, :]
    return jnp.maximum(order - back, 0).astype(jnp.int32)


def level_of(stream_key, shape, pieces, smallest, top_value):
    def one(position, parts):
        steps = jax.random.uniform(jax.random.fold_in(jax.random.fold_in(stream_key, 6), position), (parts,), jnp.float32, smallest / len(pieces), top_value / len(pieces))
        return jnp.repeat(jnp.exp(steps), shape[position] // parts).reshape((-1,) + (1,) * (len(shape) - position - 1))

    level = one(*pieces[0])
    for cut in pieces[1:]:
        level = level * one(*cut)
    return level


def profile(number_of, total, most, slope):
    weights = [(1 << 20) // math.isqrt(standing ** slope) + 1 for standing in range(2, number_of + 1)]
    rest, counts = total - most - (number_of - 1), [1] * (number_of - 1)
    while rest > 0:
        free = [i for i in range(number_of - 1) if counts[i] < most]
        pool, left = sum([weights[i] for i in free]), rest
        for i in free:
            addition = min(most - counts[i], max(1, left * weights[i] // pool), rest)
            counts[i] = counts[i] + addition
            rest = rest - addition
    return np.array([most] + counts)


def ragged(own_key, count, total, most, slope):
    if count == 2:
        one = jax.random.randint(own_key, (), max(1, total - most), min(most, total - 1) + 1)
        return jnp.stack([one, total - one])
    tallies = jnp.asarray(profile(count, total, most, slope), jnp.int32)
    pairs = (count - 1) // 2
    source_of, sink = tallies[1:1 + 2 * pairs:2], tallies[2:2 + 2 * pairs:2]
    room = jnp.minimum(source_of - 1, most - sink)
    moved = jax.random.randint(jax.random.fold_in(own_key, 1), (pairs,), 0, 1 << 20) % (room + 1)
    tallies = tallies.at[1:1 + 2 * pairs:2].set(source_of - moved).at[2:2 + 2 * pairs:2].set(sink + moved)
    return tallies[jax.random.permutation(jax.random.fold_in(own_key, 2), count)]


def centred(rng, dims, scale, bound, split=(), kind=jnp.bfloat16):
    factor_of = level_of(rng, dims, split, -0.22, 0.18) if split else 1.0
    drawn = jax.random.normal(rng, dims, jnp.float32) * scale * factor_of
    return jnp.minimum(jnp.maximum(drawn, -bound), bound).astype(kind)


def setup_inputs(seed: int = 0) -> dict:
    splits = jax.random.split(jax.random.key(seed), 17)
    layer_in = centred(splits[0], (TOKENS, MODEL_WIDTH), 1.0, 6.0, ((0, 32),))
    out_grad = centred(splits[1], (TOKENS, MODEL_WIDTH), 1.0, 6.0, ((0, 32),))
    parents = draw_parents(jax.random.fold_in(splits[16], 71), 0)
    lengths = jax.vmap(lambda own: ragged(own, SEGS, TREE_TOKENS, TRUNK, 1))(jax.random.split(splits[3], TREES)).reshape((TREES, SEGS)).astype(jnp.int32)
    attn_gain = jnp.clip(1.0 + 0.18 * jax.random.normal(splits[4], (MODEL_WIDTH,), jnp.float32), 0.099609375, 1.8984375).astype(jnp.bfloat16)
    mlp_gain = jnp.clip(1.0 + 0.18 * jax.random.normal(splits[5], (MODEL_WIDTH,), jnp.float32), 0.099609375, 1.8984375).astype(jnp.bfloat16)
    query_norm_gain = jnp.clip(1.0 + 0.18 * jax.random.normal(splits[6], (HEAD_SIZE,), jnp.float32), 0.099609375, 1.8984375).astype(jnp.bfloat16)
    key_gain = jnp.clip(1.0 + 0.18 * jax.random.normal(splits[7], (HEAD_SIZE,), jnp.float32), 0.099609375, 1.8984375).astype(jnp.bfloat16)
    query_weight = centred(splits[8], (MODEL_WIDTH, QUERY_HEADS * HEAD_SIZE), MODEL_WIDTH ** -0.5, 0.125, ((0, 16), (1, 2)))
    key_matrix = centred(splits[9], (MODEL_WIDTH, KEY_VALUE_HEADS * HEAD_SIZE), MODEL_WIDTH ** -0.5, 0.125, ((0, 16), (1, 2)))
    value_matrix = centred(splits[10], (MODEL_WIDTH, KEY_VALUE_HEADS * HEAD_SIZE), MODEL_WIDTH ** -0.5, 0.125, ((0, 16), (1, 2)))
    headgate_weight = centred(splits[11], (MODEL_WIDTH, QUERY_HEADS), MODEL_WIDTH ** -0.5, 0.125, ((0, 16), (1, 2)))
    output_weight = centred(splits[12], (QUERY_HEADS * HEAD_SIZE, MODEL_WIDTH), (HEAD_SIZE // 2) ** -0.5, 0.75, ((0, 2), (1, 16)))
    gate_weight = centred(splits[13], (MODEL_WIDTH, FF), MODEL_WIDTH ** -0.5, 0.125, ((0, 16), (1, 2)))
    up_weight = centred(splits[14], (MODEL_WIDTH, FF), MODEL_WIDTH ** -0.5, 0.125, ((0, 16), (1, 2)))
    down_weight = centred(splits[15], (FF, MODEL_WIDTH), FF ** -0.5, 0.078125, ((0, 2), (1, 16)))
    return dict(layer_in=layer_in, out_grad=out_grad, parents=parents, lengths=lengths, attn_gain=attn_gain, mlp_gain=mlp_gain, query_norm_gain=query_norm_gain, key_gain=key_gain, query_weight=query_weight, key_matrix=key_matrix, value_matrix=value_matrix, headgate_weight=headgate_weight, output_weight=output_weight, gate_weight=gate_weight, up_weight=up_weight, down_weight=down_weight)


EPS = 1e-06
THETA = 1000000.0

@jax.custom_vjp
def lower_precision(v):
    return lax.optimization_barrier(v.astype(jnp.bfloat16)).astype(jnp.float32)

@jax.custom_vjp
def lower_precision_back(v):
    return v

def low_keep(v):
    return (lower_precision(v), None)

def low_pass(kept, grad):
    return (grad,)

def back_keep(v):
    return (v, None)

def back_low(kept, grad):
    return (lower_precision(grad),)
lower_precision.defvjp(low_keep, low_pass)
lower_precision_back.defvjp(back_keep, back_low)

def precise_product(left, right):
    return jnp.dot(left, right, precision=lax.Precision.HIGHEST, preferred_element_type=jnp.float32)

def row_norm(values, gain):
    scale = lax.rsqrt(lax.optimization_barrier(jnp.mean(values * values, axis=-1, keepdims=True)) + EPS)
    return values * scale * gain

def rotate(values):
    half = values.shape[-1] // 2
    return jnp.concatenate([-values[..., half:], values[..., :half]], axis=-1)

def rope_tables(positions, width):
    half = width // 2
    freqs = THETA ** (-(jnp.arange(half, dtype=jnp.float32) / half))
    angle = positions.astype(jnp.float32)[:, None] * freqs[None, :]
    angle = jnp.concatenate([angle, angle], axis=-1)
    return (jnp.cos(angle)[:, None, :], jnp.sin(angle)[:, None, :])

def prepare_heads(raw, gain, cosine_table, sine_table):
    normed = row_norm(raw, gain)
    return normed * cosine_table + rotate(normed) * sine_table

def swiglu(gate, up):
    return jax.nn.silu(gate) * up

def gating(attn, logit):
    return attn * jax.nn.sigmoid(logit)[..., None]

def ancestors(parent_row, count):
    table = jnp.eye(count, dtype=jnp.int32)
    for seg_index in range(1, count):
        joined = jnp.maximum(table[seg_index], table[parent_row[seg_index]])
        table = table.at[seg_index].set(joined)
    return table

def segment_onehot(offsets, starts, count):
    segment = lax.optimization_barrier(jnp.sum((offsets[:, None] >= starts[None, 1:]).astype(jnp.int32), axis=1))
    return (segment[:, None] == jnp.arange(count, dtype=jnp.int32)[None, :]).astype(jnp.int32)

def tree_layer(item, params):
    rows, parent_row, length_row = item
    attn_gain, mlp_gain, query_norm_gain, key_gain, query_weight, key_matrix, value_matrix, headgate_weight, output_weight, gate_weight, up_weight, down_weight = params
    starts = jnp.cumsum(length_row) - length_row
    table = ancestors(parent_row, SEGS)
    depth = lax.optimization_barrier(jnp.sum(table * length_row[None, :], axis=1)) - length_row
    offsets = jnp.arange(TREE_TOKENS, dtype=jnp.int32)
    onehot = segment_onehot(offsets, starts, SEGS)
    positions = lax.optimization_barrier(jnp.sum(onehot * (depth - starts)[None, :], axis=1)) + offsets
    reach = jnp.dot(onehot, table, preferred_element_type=jnp.int32)
    linked = jnp.dot(reach, onehot.T, preferred_element_type=jnp.int32) > 0
    visible = linked & (offsets[None, :] <= offsets[:, None])
    cosine_table, sine_table = rope_tables(positions, HEAD_SIZE)
    scale = HEAD_SIZE ** (-0.5)
    hidden_first = lower_precision(row_norm(rows, attn_gain))
    query_unnormed = lower_precision_back(precise_product(hidden_first, query_weight)).reshape(TREE_TOKENS, QUERY_HEADS, HEAD_SIZE)
    key_unnormed = lower_precision_back(precise_product(hidden_first, key_matrix)).reshape(TREE_TOKENS, KEY_VALUE_HEADS, HEAD_SIZE)
    value_rows = lower_precision(lower_precision_back(precise_product(hidden_first, value_matrix))).reshape(TREE_TOKENS, KEY_VALUE_HEADS, HEAD_SIZE)
    logit = lower_precision_back(precise_product(hidden_first, headgate_weight))
    query_rows = lower_precision(prepare_heads(query_unnormed, query_norm_gain, cosine_table, sine_table)).reshape(TREE_TOKENS, KEY_VALUE_HEADS, QUERY_HEADS // KEY_VALUE_HEADS, HEAD_SIZE)
    key = lower_precision(prepare_heads(key_unnormed, key_gain, cosine_table, sine_table))
    score = lower_precision_back(jnp.einsum('qkgd,tkd->kgqt', query_rows, key, precision=lax.Precision.HIGHEST) * scale)
    score = jnp.where(visible[None, None], score, -1e+30)
    prob = lower_precision(jax.nn.softmax(score, axis=-1))
    attn = lower_precision_back(jnp.einsum('kgqt,tkd->qkgd', prob, value_rows, precision=lax.Precision.HIGHEST))
    attn = attn.reshape(TREE_TOKENS, QUERY_HEADS, HEAD_SIZE)
    mixed = lower_precision(gating(attn, logit)).reshape(TREE_TOKENS, QUERY_HEADS * HEAD_SIZE)
    middle = rows + lower_precision_back(precise_product(mixed, output_weight))
    h_two = lower_precision(row_norm(middle, mlp_gain))
    gate = lower_precision_back(precise_product(h_two, gate_weight))
    up = lower_precision_back(precise_product(h_two, up_weight))
    hidden = lower_precision(swiglu(gate, up))
    return middle + lower_precision_back(precise_product(hidden, down_weight))

def reference(layer_in, out_grad, parents, lengths, attn_gain, mlp_gain, query_norm_gain, key_gain, query_weight, key_matrix, value_matrix, headgate_weight, output_weight, gate_weight, up_weight, down_weight):
    params = (attn_gain.astype(jnp.float32), mlp_gain.astype(jnp.float32), query_norm_gain.astype(jnp.float32), key_gain.astype(jnp.float32), query_weight.astype(jnp.float32), key_matrix.astype(jnp.float32), value_matrix.astype(jnp.float32), headgate_weight.astype(jnp.float32), output_weight.astype(jnp.float32), gate_weight.astype(jnp.float32), up_weight.astype(jnp.float32), down_weight.astype(jnp.float32))

    def forward(rows, weights):
        shaped = rows.reshape(TREES, TREE_TOKENS, MODEL_WIDTH)

        def advance(carry, item):
            return (carry, tree_layer(item, weights))
        _, results = lax.scan(jax.checkpoint(advance), jnp.float32(0.0), (shaped, parents, lengths))
        return results.reshape(TOKENS, MODEL_WIDTH)
    result, pullback = jax.vjp(forward, layer_in.astype(jnp.float32), params)
    input_grad, grads = pullback(out_grad.astype(jnp.float32))
    return (result.astype(jnp.bfloat16), input_grad.astype(jnp.bfloat16), grads[0], grads[1], grads[2], grads[3], grads[4], grads[5], grads[6], grads[7], grads[8], grads[9], grads[10], grads[11])
```

```python
from functools import partial

import jax
import jax.numpy as jnp
from jax import lax
from jax.experimental import pallas as pl
from jax.experimental.pallas import tpu as pltpu
from jax.sharding import PartitionSpec as P

HEAD_SIZE = 128
TREE_TOKENS = 4096
EPS = 1e-06
THETA = 1000000.0
f32 = jnp.float32
bf = jnp.bfloat16

LOG2E=1.4426950408889634
BQ=256
BK=512
NT=(((1,),(1,)),((),()))
NN=(((1,),(0,)),((),()))
TN=(((0,),(0,)),((),()))
def dg(a,b,d): return lax.dot_general(a,b,d,preferred_element_type=f32)

def attn_forward_body(base, flags, q_ref, k_ref, v_ref, qbit_ref, kbit_ref, o_ref, l_ref, acc, tot):
    qb = pl.program_id(0)
    bq = q_ref.shape[0]
    nk, _, bk = kbit_ref.shape
    q = jnp.concatenate([q_ref[:, :HEAD_SIZE], q_ref[:, HEAD_SIZE:]], axis=0)
    acc[...] = jnp.zeros_like(acc)
    tot[...] = jnp.zeros_like(tot)
    factor = LOG2E * HEAD_SIZE ** (-0.5)
    def step(kb, masked):
        rows = pl.ds(pl.multiple_of(kb * bk, bk), bk)
        s = dg(q, k_ref[rows, :], NT) * factor
        if masked:
            seen = (qbit_ref[...] & kbit_ref[kb]) != 0
            at = lax.broadcasted_iota(jnp.int32, (bq, bk), 1) + kb * bk
            row = lax.broadcasted_iota(jnp.int32, (bq, bk), 0) + base + qb * bq
            seen = seen & (at <= row)
            s = jnp.where(jnp.concatenate([seen, seen], axis=0), s, -1e30)
        p = jnp.exp2(s)
        part = p[:, 0:128]
        for i in range(1, bk // 128):
            part = part + p[:, i * 128:(i + 1) * 128]
        tot[...] += part
        acc[...] += dg(p.astype(bf), v_ref[rows, :], NN)
    def body(kb, _):
        flag = flags[qb, kb]
        pl.when(flag == 1)(lambda: step(kb, True))
        pl.when(flag == 2)(lambda: step(kb, False))
        return 0
    lax.fori_loop(0, nk, body, 0)
    total = jnp.sum(tot[...], axis=1, keepdims=True)
    out = acc[...] / total
    o_ref[:, :HEAD_SIZE] = out[:bq]
    o_ref[:, HEAD_SIZE:] = out[bq:]
    lse = jnp.log2(total)
    l_ref[...] = jnp.concatenate([lse[:bq], lse[bq:]], axis=1)

def attn_forward(flags, q, k, v, qbit, kbit):
    T = q.shape[0]; N = k.shape[0]
    nk = N // BK
    return pl.pallas_call(
        partial(attn_forward_body, N - T),
        grid_spec=pltpu.PrefetchScalarGridSpec(
            num_scalar_prefetch=1, grid=(T // BQ,),
            in_specs=[
                pl.BlockSpec((BQ, 256), lambda i, f: (i, 0)),
                pl.BlockSpec((N, 128), lambda i, f: (0, 0)),
                pl.BlockSpec((N, 128), lambda i, f: (0, 0)),
                pl.BlockSpec((BQ, 1), lambda i, f: (i, 0)),
                pl.BlockSpec((nk, 1, BK), lambda i, f: (0, 0, 0)),
            ],
            out_specs=[pl.BlockSpec((BQ, 256), lambda i, f: (i, 0)), pl.BlockSpec((BQ, 2), lambda i, f: (i, 0))],
            scratch_shapes=[pltpu.VMEM((2 * BQ, 128), f32), pltpu.VMEM((2 * BQ, 128), f32)],
        ),
        out_shape=[jax.ShapeDtypeStruct((T, 256), f32), jax.ShapeDtypeStruct((T, 2), f32)],
        cost_estimate=pl.CostEstimate(flops=2*2*T*N*256*3//4, bytes_accessed=8<<20, transcendentals=T*N*3//2),
        name="attn_forward",
    )(flags, q, k, v, qbit, kbit)

def attn_backward_body(base, flags, q_ref, g_ref, k_ref, v_ref, qbit_ref, kbit_ref, lse_ref, del_ref, dq_ref, dk_ref, dv_ref):
    kb = pl.program_id(0)
    bk = k_ref.shape[0]
    T = q_ref.shape[0]
    bq = BQ
    factor = LOG2E * HEAD_SIZE ** (-0.5)
    @pl.when(kb == 0)
    def _():
        dq_ref[...] = jnp.zeros_like(dq_ref)
    dk_ref[...] = jnp.zeros_like(dk_ref)
    dv_ref[...] = jnp.zeros_like(dv_ref)
    def pair(ref, rows):
        return jnp.concatenate([ref[rows, :HEAD_SIZE], ref[rows, HEAD_SIZE:]], axis=0)
    def line(ref, rows):
        return jnp.concatenate([ref[0:1, rows], ref[1:2, rows]], axis=1)
    def step(qb, masked):
        rows = pl.ds(pl.multiple_of(qb * bq, bq), bq)
        q = pair(q_ref, rows)
        g = pair(g_ref, rows)
        k = k_ref[...]
        s = dg(k, q, NT) * factor - line(lse_ref, rows)
        if masked:
            seen = (kbit_ref[...] & qbit_ref[0:1, rows]) != 0
            at = lax.broadcasted_iota(jnp.int32, (bk, bq), 0) + kb * bk
            row = lax.broadcasted_iota(jnp.int32, (bk, bq), 1) + base + qb * bq
            seen = seen & (at <= row)
            s = jnp.where(jnp.concatenate([seen, seen], axis=1), s, -1e30)
        p = jnp.exp2(s)
        dv_ref[...] += dg(p.astype(bf), g, NN)
        dp = dg(v_ref[...], g, NT)
        ds = (p * (dp - line(del_ref, rows))).astype(bf)
        dk_ref[...] += dg(ds, q, NN)
        dq = dg(ds, k, TN)
        dq_ref[rows, :HEAD_SIZE] += dq[:bq]
        dq_ref[rows, HEAD_SIZE:] += dq[bq:]
    def body(qb, _):
        flag = flags[qb, kb]
        pl.when(flag == 1)(lambda: step(qb, True))
        pl.when(flag == 2)(lambda: step(qb, False))
        return 0
    lax.fori_loop(0, T // bq, body, 0)

def attn_backward(flags, q, g, k, v, qbit, kbit, lse, delta):
    T = q.shape[0]; N = k.shape[0]
    nk = N // BK
    whole = lambda *s: pl.BlockSpec(s, lambda i, f: (0,) * len(s))
    return pl.pallas_call(
        partial(attn_backward_body, N - T),
        grid_spec=pltpu.PrefetchScalarGridSpec(
            num_scalar_prefetch=1, grid=(nk,),
            in_specs=[whole(T, 256), whole(T, 256), pl.BlockSpec((BK, 128), lambda i, f: (i, 0)), pl.BlockSpec((BK, 128), lambda i, f: (i, 0)),
                whole(1, T), pl.BlockSpec((BK, 1), lambda i, f: (i, 0)), whole(2, T), whole(2, T)],
            out_specs=[whole(T, 256), pl.BlockSpec((BK, 128), lambda i, f: (i, 0)), pl.BlockSpec((BK, 128), lambda i, f: (i, 0))],
        ),
        out_shape=[jax.ShapeDtypeStruct((T, 256), f32), jax.ShapeDtypeStruct((N, 128), f32), jax.ShapeDtypeStruct((N, 128), f32)],
        cost_estimate=pl.CostEstimate(flops=5*2*T*N*256*3//4, bytes_accessed=12<<20, transcendentals=T*N*3//2),
        name="attn_backward",
    )(flags, q, g, k, v, qbit, kbit, lse, delta)


GROUP=4
MESH=pl.DeviceIdType.MESH

def places():
    dp = lax.axis_index("dp"); c = lax.axis_index("mp")
    t = dp % GROUP
    base = dp - t
    tx = t + 1 - 2 * (t % 2)
    ty = t + 2 - 4 * (t // 2)
    td = 3 - t
    return base, t, tx, ty, td, c

def greet(devices):
    barrier = pltpu.get_barrier_semaphore()
    for device in devices:
        pl.semaphore_signal(barrier, inc=1, device_id=device, device_id_type=MESH)
    pl.semaphore_wait(barrier, len(devices))

def gather_body(x_ref, out_ref, send, recv, local):
    base, t, tx, ty, td, c = places()
    share = x_ref.shape[0]
    half = share // 2
    xdev, ydev, mate = (base + tx, c), (base + ty, c), (base + t, 1 - c)
    greet([xdev, ydev, mate])
    def spot(who, part=None):
        start = (2 * who + c) * share
        if part is None:
            return out_ref.at[pl.ds(pl.multiple_of(start, share), share)]
        return out_ref.at[pl.ds(pl.multiple_of(start + part * half, half), half)]
    def copy(kind, src, dst, device):
        return pltpu.make_async_remote_copy(src_ref=src, dst_ref=dst, send_sem=send.at[kind], recv_sem=recv.at[kind], device_id=device, device_id_type=MESH)
    own = pltpu.make_async_copy(x_ref, spot(t), local)
    own.start()
    mine = [x_ref.at[pl.ds(0, half)], x_ref.at[pl.ds(half, half)]]
    k = {}
    k[2] = copy(2, mine[0], spot(t, 0), ydev); k[2].start()
    k[1] = copy(1, mine[1], spot(t, 1), xdev); k[1].start()
    k[3] = copy(3, mine[1], spot(t, 1), ydev); k[3].start()
    k[0] = copy(0, mine[0], spot(t, 0), xdev); k[0].start()
    k[6] = copy(6, x_ref, spot(t), mate); k[6].start()
    k[2].wait_recv()
    k[4] = copy(4, spot(ty, 0), spot(ty, 0), xdev); k[4].start()
    k[9] = copy(9, spot(ty, 0), spot(ty, 0), mate); k[9].start()
    k[1].wait_recv()
    k[5] = copy(5, spot(tx, 1), spot(tx, 1), ydev); k[5].start()
    k[8] = copy(8, spot(tx, 1), spot(tx, 1), mate); k[8].start()
    k[0].wait_recv()
    k[7] = copy(7, spot(tx, 0), spot(tx, 0), mate); k[7].start()
    k[3].wait_recv()
    k[10] = copy(10, spot(ty, 1), spot(ty, 1), mate); k[10].start()
    k[4].wait_recv()
    k[11] = copy(11, spot(td, 0), spot(td, 0), mate); k[11].start()
    k[5].wait_recv()
    k[12] = copy(12, spot(td, 1), spot(td, 1), mate); k[12].start()
    for kind in range(6, 13):
        k[kind].wait_recv()
    for kind in range(13):
        k[kind].wait_send()
    own.wait()

def gather_group(x):
    share, width = x.shape
    return pl.pallas_call(
        gather_body,
        out_shape=jax.ShapeDtypeStruct((share * GROUP * 2, width), x.dtype),
        in_specs=[pl.BlockSpec(memory_space=pltpu.VMEM)],
        out_specs=pl.BlockSpec(memory_space=pl.ANY),
        scratch_shapes=[pltpu.SemaphoreType.DMA((13,)), pltpu.SemaphoreType.DMA((13,)), pltpu.SemaphoreType.DMA],
        compiler_params=pltpu.CompilerParams(collective_id=1, has_side_effects=True),
        name="gather_group",
    )(x)

def reduce_body(p_ref, out_ref, near, mates, sums, xin, yin, zin, turn, load, send, recv):
    base, t, tx, ty, td, c = places()
    share = out_ref.shape[0]
    half = share // 2
    xdev, ydev, mate = (base + tx, c), (base + ty, c), (base + t, 1 - c)
    greet([xdev, ydev, mate])
    def spot(who, core):
        return p_ref.at[pl.ds(pl.multiple_of((2 * who + core) * share, share), share)]
    def copy(kind, src, dst, device):
        return pltpu.make_async_remote_copy(src_ref=src, dst_ref=dst, send_sem=send.at[kind], recv_sem=recv.at[kind], device_id=device, device_id_type=MESH)
    def add(dst, left, right):
        step = 16
        def go(i, _):
            rows = pl.ds(pl.multiple_of(i * step, step), step)
            dst[rows, :] = (left[rows, :].astype(f32) + right[rows, :].astype(f32)).astype(dst.dtype)
            return 0
        lax.fori_loop(0, dst.shape[0] // step, go, 0)
    order = [td, tx, ty, t]
    over, loads = [], []
    for i, who in enumerate(order):
        over.append(copy(i, spot(who, 1 - c), mates.at[i], mate)); over[i].start()
        loads.append(pltpu.make_async_copy(spot(who, c), near.at[i], load.at[i])); loads[i].start()
    A, B = pl.ds(0, half), pl.ds(half, half)
    k = {}
    for i in range(4):
        loads[i].wait()
        over[i].wait_recv()
        add(sums.at[i], near.at[i], mates.at[i])
        if i == 0:
            k[4] = copy(4, sums.at[0, A], xin.at[1], xdev); k[4].start()
            k[5] = copy(5, sums.at[0, B], yin.at[1], ydev); k[5].start()
        if i == 1:
            k[6] = copy(6, sums.at[1, A], xin.at[0], xdev); k[6].start()
        if i == 2:
            k[7] = copy(7, sums.at[2, B], yin.at[0], ydev); k[7].start()
    k[4].wait_recv()
    add(turn.at[0], sums.at[2, A], xin.at[1])
    k[8] = copy(8, turn.at[0], zin.at[0], ydev); k[8].start()
    k[5].wait_recv()
    add(turn.at[1], sums.at[1, B], yin.at[1])
    k[9] = copy(9, turn.at[1], zin.at[1], xdev); k[9].start()
    k[6].wait_recv()
    add(out_ref.at[A], sums.at[3, A], xin.at[0])
    k[7].wait_recv()
    add(out_ref.at[B], sums.at[3, B], yin.at[0])
    k[8].wait_recv()
    add(out_ref.at[A], out_ref.at[A], zin.at[0])
    k[9].wait_recv()
    add(out_ref.at[B], out_ref.at[B], zin.at[1])
    for i in range(4):
        over[i].wait_send()
    for kind in range(4, 10):
        k[kind].wait_send()

def reduce_group(p):
    rows, width = p.shape
    share = rows // (2 * GROUP)
    half = share // 2
    return pl.pallas_call(
        reduce_body,
        out_shape=jax.ShapeDtypeStruct((share, width), f32),
        in_specs=[pl.BlockSpec(memory_space=pl.ANY)],
        out_specs=pl.BlockSpec(memory_space=pltpu.VMEM),
        scratch_shapes=[pltpu.VMEM((4, share, width), bf), pltpu.VMEM((4, share, width), bf), pltpu.VMEM((4, share, width), bf),
            pltpu.VMEM((2, half, width), bf), pltpu.VMEM((2, half, width), bf), pltpu.VMEM((2, half, width), bf), pltpu.VMEM((2, half, width), bf),
            pltpu.SemaphoreType.DMA((4,)), pltpu.SemaphoreType.DMA((10,)), pltpu.SemaphoreType.DMA((10,))],
        compiler_params=pltpu.CompilerParams(collective_id=2, has_side_effects=True),
        name="reduce_group",
    )(p)

def trade_body(x_ref, out_ref, send, recv, local):
    base, t, tx, ty, td, c = places()
    partners = [td, tx, ty]
    greet([(base + who, c) for who in partners])
    own = pltpu.make_async_copy(x_ref.at[t], out_ref.at[t], local)
    copies = []
    for i, who in enumerate(partners):
        copies.append(pltpu.make_async_remote_copy(src_ref=x_ref.at[who], dst_ref=out_ref.at[t], send_sem=send.at[i], recv_sem=recv.at[i], device_id=(base + who, c), device_id_type=MESH))
        copies[i].start()
    own.start()
    for one in copies:
        one.wait()
    own.wait()

def trade_group(x, key):
    return pl.pallas_call(
        trade_body,
        out_shape=jax.ShapeDtypeStruct(x.shape, x.dtype),
        in_specs=[pl.BlockSpec(memory_space=pltpu.VMEM)],
        out_specs=pl.BlockSpec(memory_space=pl.ANY),
        scratch_shapes=[pltpu.SemaphoreType.DMA((3,)), pltpu.SemaphoreType.DMA((3,)), pltpu.SemaphoreType.DMA],
        compiler_params=pltpu.CompilerParams(collective_id=key, has_side_effects=True),
        name="trade_group",
    )(x)


def row_norm(values, gain):
    scale = lax.rsqrt(jnp.mean(values * values, axis=-1, keepdims=True) + EPS)
    return values * scale * gain


def rotate(values):
    half = values.shape[-1] // 2
    return jnp.concatenate([-values[..., half:], values[..., :half]], axis=-1)


def rope_tables(positions, width):
    half = width // 2
    freqs = THETA ** (-(jnp.arange(half, dtype=f32) / half))
    angle = positions.astype(f32)[:, None] * freqs[None, :]
    angle = jnp.concatenate([angle, angle], axis=-1)
    return (jnp.cos(angle)[:, None, :], jnp.sin(angle)[:, None, :])


def prepare_heads(raw, gain, cosine_table, sine_table):
    normed = row_norm(raw, gain)
    return normed * cosine_table + rotate(normed) * sine_table


def swiglu(gate, up):
    return jax.nn.silu(gate) * up


def gating(attn, logit):
    return attn * jax.nn.sigmoid(logit)[..., None]


def ancestors(parent_row, count):
    table = jnp.eye(count, dtype=jnp.int32)
    for seg_index in range(1, count):
        joined = jnp.maximum(table[seg_index], table[parent_row[seg_index]])
        table = table.at[seg_index].set(joined)
    return table


def segment_onehot(offsets, starts, count):
    segment = jnp.sum((offsets[:, None] >= starts[None, 1:]).astype(jnp.int32), axis=1)
    return (segment[:, None] == jnp.arange(count, dtype=jnp.int32)[None, :]).astype(jnp.int32)


def inner(left, right):
    return dg(left, right, TN)


def against(left, right):
    return dg(left, right, NT)


def by_member(weight, pieces):
    rows = weight.shape[0]
    return weight.reshape(rows, pieces, -1).transpose(1, 0, 2)


def from_members(pieces):
    return pieces.transpose(1, 0, 2).reshape(pieces.shape[1], -1)


def per_device(
    layer_in,
    out_grad,
    parents,
    lengths,
    attn_gain,
    mlp_gain,
    query_norm_gain,
    key_gain,
    query_weight,
    key_matrix,
    value_matrix,
    headgate_weight,
    output_weight,
    gate_weight,
    up_weight,
    down_weight,
):
    data_count = lax.axis_size("dp")
    model_count = lax.axis_size("mp")
    share, width = layer_in.shape
    rows_here = query_weight.shape[0]
    group_tokens = share * model_count * GROUP
    seg_count = parents.shape[1]
    far = [[member + GROUP * plane for plane in range(data_count // GROUP)] for member in range(GROUP)]
    planes = TREE_TOKENS // group_tokens

    pieces_attn = jnp.concatenate(
        [
            by_member(query_weight, GROUP),
            by_member(key_matrix, GROUP),
            by_member(value_matrix, GROUP),
            jnp.pad(by_member(headgate_weight, GROUP), ((0, 0), (0, 0), (0, HEAD_SIZE - headgate_weight.shape[1] // GROUP))),
        ],
        axis=-1,
    )
    pieces_out = by_member(output_weight.T, GROUP)
    pieces_glu = jnp.concatenate([by_member(gate_weight, GROUP), by_member(up_weight, GROUP)], axis=-1)
    pieces_down = by_member(down_weight.T, GROUP)

    def far_gather(pieces, key):
        mine = trade_group(pieces, key).reshape(GROUP * rows_here, -1)
        return lax.all_gather(mine, "dp", axis=0, tiled=True, axis_index_groups=far)

    full_attn = far_gather(pieces_attn, 3)
    full_out = far_gather(pieces_out, 4)
    full_glu = far_gather(pieces_glu, 5)
    full_down = far_gather(pieces_down, 6)

    def far_scatter(grad, key):
        mine = lax.psum_scatter(grad, "dp", scatter_dimension=0, tiled=True, axis_index_groups=far)
        return trade_group(mine.reshape(GROUP, rows_here, -1), key)

    sizes = [attn_gain.shape[0], mlp_gain.shape[0], query_norm_gain.shape[0], key_gain.shape[0]]
    cuts = [0, sizes[0], sizes[0] + sizes[1], sizes[0] + sizes[1] + sizes[2], sum(sizes)]
    gains = lax.all_gather(
        jnp.concatenate([attn_gain, mlp_gain, query_norm_gain, key_gain]), ("dp", "mp"), axis=0, tiled=False
    ).astype(f32)
    gain_one, gain_two, gain_query, gain_key = [
        gains[:, cuts[i] : cuts[i + 1]].reshape(-1) for i in range(4)
    ]

    group_index = lax.axis_index("dp") // GROUP
    first = group_index * group_tokens
    tree = first // TREE_TOKENS
    begin = first - tree * TREE_TOKENS
    later = begin // group_tokens
    parent_row = lax.dynamic_index_in_dim(parents, tree, 0, keepdims=False)
    length_row = lax.dynamic_index_in_dim(lengths, tree, 0, keepdims=False)
    starts = jnp.cumsum(length_row) - length_row
    table = ancestors(parent_row, seg_count)
    depth = jnp.sum(table * length_row[None, :], axis=1) - length_row
    offsets = begin + jnp.arange(group_tokens, dtype=jnp.int32)
    onehot = segment_onehot(offsets, starts, seg_count)
    positions = jnp.sum(onehot * (depth - starts)[None, :], axis=1) + offsets
    powers = 1 << jnp.arange(seg_count, dtype=jnp.int32)
    query_bits = jnp.sum(onehot * jnp.sum(table * powers[None, :], axis=1)[None, :], axis=1)
    key_count = planes * group_tokens
    key_offsets = begin - (key_count - group_tokens) + jnp.arange(key_count, dtype=jnp.int32)
    key_hot = segment_onehot(key_offsets, starts, seg_count) * (key_offsets >= 0).astype(jnp.int32)[:, None]
    key_bits = jnp.sum(key_hot * powers[None, :], axis=1)
    query_has = jnp.max(onehot.reshape(-1, BQ, seg_count), axis=1)
    key_has = jnp.max(key_hot.reshape(-1, BK, seg_count), axis=1)
    reached = jnp.dot(jnp.dot(query_has, table), key_has.T) > 0
    missed = jnp.dot(jnp.dot(query_has, 1 - table), key_has.T) > 0
    q_first = key_count - group_tokens + BQ * jnp.arange(query_has.shape[0], dtype=jnp.int32)[:, None]
    k_first = BK * jnp.arange(key_has.shape[0], dtype=jnp.int32)[None, :]
    some = reached & (k_first <= q_first + BQ - 1)
    every = ~missed & (k_first + BK - 1 <= q_first)
    flags = jnp.where(some, jnp.where(every, 2, 1), 0).astype(jnp.int32)
    cosine_table, sine_table = rope_tables(positions, HEAD_SIZE)

    rows = layer_in.astype(f32)
    normed_one, norm_one_back = jax.vjp(row_norm, rows, gain_one)
    hidden_first = gather_group(normed_one.astype(bf))
    grad_tokens = gather_group(out_grad)
    raw = jnp.dot(hidden_first, full_attn, preferred_element_type=f32)
    q_width = query_weight.shape[1] // GROUP
    k_width = key_matrix.shape[1] // GROUP
    heads = q_width // HEAD_SIZE
    query_unnormed = raw[:, :q_width].reshape(group_tokens, heads, HEAD_SIZE)
    key_unnormed = raw[:, q_width : q_width + k_width].reshape(group_tokens, 1, HEAD_SIZE)
    value_rows = raw[:, q_width + k_width : q_width + 2 * k_width].astype(bf)
    logit = raw[:, q_width + 2 * k_width : q_width + 2 * k_width + heads]
    prepare = partial(prepare_heads, cosine_table=cosine_table, sine_table=sine_table)
    query_f, query_back = jax.vjp(prepare, query_unnormed, gain_query)
    key_f, key_back = jax.vjp(prepare, key_unnormed, gain_key)
    query_rows = query_f.astype(bf).reshape(group_tokens, q_width)
    key_rows = key_f.astype(bf).reshape(group_tokens, k_width)
    ahead = [(s, s + GROUP) for s in range(data_count) if (s // GROUP) % planes == 0]
    back = [(d, s) for s, d in ahead]
    both = lax.ppermute(jnp.concatenate([key_rows, value_rows], axis=1), "dp", ahead)
    key_all = jnp.concatenate([both[:, :k_width], key_rows], axis=0)
    value_all = jnp.concatenate([both[:, k_width:], value_rows], axis=0)
    attn, lse = attn_forward(
        flags, query_rows, key_all, value_all, query_bits[:, None], key_bits.reshape(-1, 1, BK)
    )
    attn = attn.reshape(group_tokens, heads, HEAD_SIZE)
    mixed_f, gate_back = jax.vjp(gating, attn, logit)
    mixed = mixed_f.astype(bf).reshape(group_tokens, -1)
    middle = rows + reduce_group(against(mixed, full_out).astype(bf))

    normed_two, norm_two_back = jax.vjp(row_norm, middle, gain_two)
    h_two = gather_group(normed_two.astype(bf))
    both_glu = jnp.dot(h_two, full_glu, preferred_element_type=f32)
    units = full_down.shape[1]
    gate, up = both_glu[:, :units], both_glu[:, units:]
    hidden_f, glu_back = jax.vjp(swiglu, gate, up)
    hidden = hidden_f.astype(bf)
    layer_out = (middle + reduce_group(against(hidden, full_down).astype(bf))).astype(bf)

    down_grad = far_scatter(inner(grad_tokens, hidden).astype(bf), 7)
    grad_hidden = jnp.dot(grad_tokens, full_down, preferred_element_type=f32)
    grad_gate_f, grad_up_f = glu_back(grad_hidden)
    grad_glu = jnp.concatenate([grad_gate_f.astype(bf), grad_up_f.astype(bf)], axis=1)
    glu_grad = far_scatter(inner(h_two, grad_glu).astype(bf), 8)
    grad_h_two = reduce_group(against(grad_glu, full_glu).astype(bf))
    grad_mid_norm, gain_two_grad = norm_two_back(grad_h_two)
    grad_middle = out_grad.astype(f32) + grad_mid_norm

    grad_branch = gather_group(grad_middle.astype(bf))
    output_grad = far_scatter(inner(grad_branch, mixed).astype(bf), 9)
    grad_mixed = jnp.dot(grad_branch, full_out, preferred_element_type=f32).reshape(
        group_tokens, heads, HEAD_SIZE
    )
    grad_attn_f, grad_logit_f = gate_back(grad_mixed)
    grad_attn = grad_attn_f.astype(bf)
    delta = jnp.sum(grad_attn.astype(f32) * attn, axis=-1)
    grad_query, grad_key, grad_value = attn_backward(
        flags,
        query_rows,
        grad_attn.reshape(group_tokens, q_width),
        key_all,
        value_all,
        query_bits[None, :],
        key_bits[:, None],
        lse.T,
        delta.T,
    )
    early = key_count - group_tokens
    returned = lax.ppermute(
        jnp.concatenate([grad_key[:early], grad_value[:early]], axis=1).astype(bf), "dp", back
    ).astype(f32)
    score_scale = HEAD_SIZE ** (-0.5)
    grad_key = (grad_key[early:] + returned[:, :k_width]) * score_scale
    grad_value = grad_value[early:] + returned[:, k_width:]
    grad_q_raw, query_gain_grad = query_back((grad_query * score_scale).reshape(group_tokens, heads, HEAD_SIZE))
    grad_k_raw, key_gain_grad = key_back(grad_key.reshape(group_tokens, 1, HEAD_SIZE))
    grad_raw = jnp.concatenate(
        [
            grad_q_raw.reshape(group_tokens, -1),
            grad_k_raw.reshape(group_tokens, -1),
            grad_value,
            jnp.pad(grad_logit_f, ((0, 0), (0, HEAD_SIZE - heads))),
        ],
        axis=1,
    ).astype(bf)
    attn_grad = far_scatter(inner(hidden_first, grad_raw).astype(bf), 10)
    grad_h_one = reduce_group(against(grad_raw, full_attn).astype(bf))
    grad_in_norm, gain_one_grad = norm_one_back(grad_h_one)
    input_grad = (grad_middle + grad_in_norm).astype(bf)

    gain_parts = jnp.concatenate(
        [
            piece.reshape(data_count * model_count, -1)
            for piece in (gain_one_grad, gain_two_grad, query_gain_grad, key_gain_grad)
        ],
        axis=1,
    )
    gain_sums = lax.psum_scatter(gain_parts, ("dp", "mp"), scatter_dimension=0, tiled=True)[0]
    full = lambda pieces: from_members(pieces).astype(f32)
    return (
        layer_out,
        input_grad,
        gain_sums[cuts[0] : cuts[1]],
        gain_sums[cuts[1] : cuts[2]],
        gain_sums[cuts[2] : cuts[3]],
        gain_sums[cuts[3] : cuts[4]],
        full(attn_grad[:, :, :q_width]),
        full(attn_grad[:, :, q_width : q_width + k_width]),
        full(attn_grad[:, :, q_width + k_width : q_width + 2 * k_width]),
        full(attn_grad[:, :, q_width + 2 * k_width : q_width + 2 * k_width + heads]),
        full(output_grad).T,
        full(glu_grad[:, :, :units]),
        full(glu_grad[:, :, units:]),
        full(down_grad).T,
    )


def solution(mesh):
    in_specs = (
        P(("dp", "mp"), None),
        P(("dp", "mp"), None),
        P(),
        P(),
        P(("dp", "mp")),
        P(("dp", "mp")),
        P(("dp", "mp")),
        P(("dp", "mp")),
        P("dp", "mp"),
        P("dp", "mp"),
        P("dp", "mp"),
        P("dp", "mp"),
        P("mp", "dp"),
        P("dp", "mp"),
        P("dp", "mp"),
        P("mp", "dp"),
    )
    out_specs = (
        P(("dp", "mp"), None),
        P(("dp", "mp"), None),
        P(("dp", "mp")),
        P(("dp", "mp")),
        P(("dp", "mp")),
        P(("dp", "mp")),
        P("dp", "mp"),
        P("dp", "mp"),
        P("dp", "mp"),
        P("dp", "mp"),
        P("mp", "dp"),
        P("dp", "mp"),
        P("dp", "mp"),
        P("mp", "dp"),
    )
    return jax.shard_map(
        per_device, mesh=mesh, in_specs=in_specs, out_specs=out_specs, check_vma=False
    )
```

```python
from functools import partial

import jax
import jax.numpy as jnp
from jax import lax
from jax.experimental import pallas as pl
from jax.experimental.pallas import tpu as pltpu
from jax.sharding import PartitionSpec as P

HEAD_SIZE = 128
TREE_TOKENS = 4096
EPS = 1e-06
THETA = 1000000.0
f32 = jnp.float32
bf = jnp.bfloat16

LOG2E = 1.4426950408889634
SCORE_SCALE = HEAD_SIZE ** (-0.5)
BQ = 256
BK = 512
NT = (((1,), (1,)), ((), ()))
NN = (((1,), (0,)), ((), ()))
TN = (((0,), (0,)), ((), ()))


def dg(left, right, dims):
    return lax.dot_general(left, right, dims, preferred_element_type=f32)


def halves(ref, rows):
    return jnp.concatenate([ref[rows, :HEAD_SIZE], ref[rows, HEAD_SIZE:]], axis=0)


def as_rows(column):
    return jnp.broadcast_to(column, (column.shape[0], HEAD_SIZE)).T[0:1, :]


def attend_body(causal, last, flags, q_ref, kv_ref, qbit_ref, kbit_ref, *refs):
    if last:
        acc_in, tot_in, logit_ref, attn_ref, mixed_ref, lse_ref, acc, tot = refs
    else:
        acc_out, tot_out, acc, tot = refs
    qb = pl.program_id(0)
    bq = q_ref.shape[0]
    nk, _, bk = kbit_ref.shape
    q = halves(q_ref, slice(None))
    acc[...] = jnp.zeros_like(acc)
    tot[...] = jnp.zeros_like(tot)

    def step(kb, masked):
        rows = pl.ds(pl.multiple_of(kb * bk, bk), bk)
        s = dg(q, kv_ref[rows, :HEAD_SIZE], NT) * (LOG2E * SCORE_SCALE)
        if masked:
            seen = (qbit_ref[...] & kbit_ref[kb]) != 0
            if causal:
                at = lax.broadcasted_iota(jnp.int32, (bq, bk), 1) + kb * bk
                row = lax.broadcasted_iota(jnp.int32, (bq, bk), 0) + qb * bq
                seen = seen & (at <= row)
            s = jnp.where(jnp.concatenate([seen, seen], axis=0), s, -1e30)
        p = jnp.exp2(s)
        part = p[:, 0:128]
        for i in range(1, bk // 128):
            part = part + p[:, i * 128 : (i + 1) * 128]
        tot[...] += part
        acc[...] += dg(p.astype(bf), kv_ref[rows, HEAD_SIZE:], NN)

    def body(kb, _):
        flag = flags[qb, kb]
        pl.when(flag == 1)(lambda: step(kb, True))
        pl.when(flag == 2)(lambda: step(kb, False))
        return 0

    lax.fori_loop(0, nk, body, 0)
    total = jnp.sum(tot[...], axis=1, keepdims=True)
    if not last:
        acc_out[:, :HEAD_SIZE] = acc[:bq, :]
        acc_out[:, HEAD_SIZE:] = acc[bq:, :]
        tot_out[...] = jnp.concatenate([total[:bq], total[bq:]], axis=1)
    else:
        for h in range(2):
            rows = slice(h * bq, (h + 1) * bq)
            cols = slice(h * HEAD_SIZE, (h + 1) * HEAD_SIZE)
            sums = total[rows] + tot_in[:, h : h + 1]
            out = (acc[rows, :] + acc_in[:, cols]) / sums
            attn_ref[:, cols] = out
            mixed_ref[:, cols] = (out * jax.nn.sigmoid(logit_ref[:, h : h + 1])).astype(bf)
            lse_ref[h : h + 1, :] = as_rows(jnp.log2(sums))


def attend(causal, flags, q, kv, qbit, kbit, earlier=None):
    T = q.shape[0]
    N = kv.shape[0]
    nk = N // BK
    W = 2 * HEAD_SIZE
    blk = lambda w, j=0: pl.BlockSpec((BQ, w), lambda i, f: (i, j))
    last = earlier is not None
    in_specs = [
        blk(W),
        pl.BlockSpec((N, W), lambda i, f: (0, 0)),
        blk(1),
        pl.BlockSpec((nk, 1, BK), lambda i, f: (0, 0, 0)),
    ]
    if last:
        acc, tot, raw = earlier
        extra = [acc, tot, raw]
        in_specs += [blk(W), blk(2), blk(HEAD_SIZE, raw.shape[1] // HEAD_SIZE - 1)]
        out_specs = [blk(W), blk(W), pl.BlockSpec((2, BQ), lambda i, f: (0, i))]
        out_shape = [
            jax.ShapeDtypeStruct((T, W), f32),
            jax.ShapeDtypeStruct((T, W), bf),
            jax.ShapeDtypeStruct((2, T), f32),
        ]
    else:
        extra = []
        out_specs = [blk(W), blk(2)]
        out_shape = [jax.ShapeDtypeStruct((T, W), f32), jax.ShapeDtypeStruct((T, 2), f32)]
    return pl.pallas_call(
        partial(attend_body, causal, last),
        grid_spec=pltpu.PrefetchScalarGridSpec(
            num_scalar_prefetch=1,
            grid=(T // BQ,),
            in_specs=in_specs,
            out_specs=out_specs,
            scratch_shapes=[pltpu.VMEM((2 * BQ, HEAD_SIZE), f32), pltpu.VMEM((2 * BQ, HEAD_SIZE), f32)],
        ),
        out_shape=out_shape,
        cost_estimate=pl.CostEstimate(
            flops=(2 if causal else 4) * T * N * W, bytes_accessed=8 << 20, transcendentals=T * N * (1 if causal else 2)
        ),
        name="attend_own" if causal else "attend_earlier",
    )(flags, q, kv, qbit, kbit, *extra)


def attend_back_body(causal, flags, q_ref, g_ref, kv_ref, qbit_ref, kbit_ref, lse_ref, del_ref, *refs):
    if causal:
        dq_in, dq_ref, dkv_ref, dk_acc, dv_acc = refs
    else:
        dq_ref, dkv_ref, dk_acc, dv_acc = refs
    kb = pl.program_id(0)
    bk = kv_ref.shape[0]
    T = q_ref.shape[0]
    bq = BQ

    @pl.when(kb == 0)
    def _():
        if causal:
            dq_ref[...] = dq_in[...]
        else:
            dq_ref[...] = jnp.zeros_like(dq_ref)

    dk_acc[...] = jnp.zeros_like(dk_acc)
    dv_acc[...] = jnp.zeros_like(dv_acc)

    def line(ref, rows):
        return jnp.concatenate([ref[0:1, rows], ref[1:2, rows]], axis=1)

    def step(qb, masked):
        rows = pl.ds(pl.multiple_of(qb * bq, bq), bq)
        q = halves(q_ref, rows)
        g = halves(g_ref, rows)
        k = kv_ref[:, :HEAD_SIZE]
        s = dg(k, q, NT) * (LOG2E * SCORE_SCALE) - line(lse_ref, rows)
        if masked:
            seen = (kbit_ref[...] & qbit_ref[0:1, rows]) != 0
            if causal:
                at = lax.broadcasted_iota(jnp.int32, (bk, bq), 0) + kb * bk
                row = lax.broadcasted_iota(jnp.int32, (bk, bq), 1) + qb * bq
                seen = seen & (at <= row)
            s = jnp.where(jnp.concatenate([seen, seen], axis=1), s, -1e30)
        p = jnp.exp2(s)
        dv_acc[...] += dg(p.astype(bf), g, NN)
        dp = dg(kv_ref[:, HEAD_SIZE:], g, NT)
        ds = (p * (dp - line(del_ref, rows))).astype(bf)
        dk_acc[...] += dg(ds, q, NN)
        dq = dg(ds, k, TN)
        dq_ref[rows, :HEAD_SIZE] += dq[:bq]
        dq_ref[rows, HEAD_SIZE:] += dq[bq:]

    def body(qb, _):
        flag = flags[qb, kb]
        pl.when(flag == 1)(lambda: step(qb, True))
        pl.when(flag == 2)(lambda: step(qb, False))
        return 0

    lax.fori_loop(0, T // bq, body, 0)
    dkv_ref[:, :HEAD_SIZE] = (dk_acc[...] * SCORE_SCALE).astype(dkv_ref.dtype)
    dkv_ref[:, HEAD_SIZE:] = dv_acc[...].astype(dkv_ref.dtype)


def attend_back(causal, flags, q, g, kv, qbit, kbit, lse, delta, dq=None):
    T = q.shape[0]
    N = kv.shape[0]
    W = 2 * HEAD_SIZE
    whole = lambda *s: pl.BlockSpec(s, lambda i, f: (0,) * len(s))
    along = lambda w: pl.BlockSpec((BK, w), lambda i, f: (i, 0))
    in_specs = [whole(T, W), whole(T, W), along(W), whole(1, T), along(1), whole(2, T), whole(2, T)]
    extra = []
    if causal:
        in_specs.append(whole(T, W))
        extra = [dq]
    return pl.pallas_call(
        partial(attend_back_body, causal),
        grid_spec=pltpu.PrefetchScalarGridSpec(
            num_scalar_prefetch=1,
            grid=(N // BK,),
            in_specs=in_specs,
            out_specs=[whole(T, W), along(W)],
            scratch_shapes=[pltpu.VMEM((BK, HEAD_SIZE), f32), pltpu.VMEM((BK, HEAD_SIZE), f32)],
        ),
        out_shape=[jax.ShapeDtypeStruct((T, W), f32), jax.ShapeDtypeStruct((N, W), f32 if causal else bf)],
        cost_estimate=pl.CostEstimate(
            flops=(5 if causal else 10) * T * N * W, bytes_accessed=12 << 20, transcendentals=T * N * (1 if causal else 2)
        ),
        name="attend_own_back" if causal else "attend_earlier_back",
    )(flags, q, g, kv, qbit, kbit, lse, delta, *extra)


def turn(values):
    return pltpu.roll(values, HEAD_SIZE // 2, 1)


def prepare_body(raw_ref, cos_ref, sin_ref, gain_ref, q_ref, kv_ref):
    for i in range(3):
        cols = slice(i * HEAD_SIZE, (i + 1) * HEAD_SIZE)
        u = raw_ref[:, cols]
        r = lax.rsqrt(jnp.mean(u * u, axis=-1, keepdims=True) + EPS)
        n = u * r * gain_ref[(1 if i == 2 else 0) : (2 if i == 2 else 1), :]
        out = (n * cos_ref[...] + turn(n) * sin_ref[...]).astype(bf)
        if i < 2:
            q_ref[:, cols] = out
        else:
            kv_ref[:, :HEAD_SIZE] = out
    kv_ref[:, HEAD_SIZE:] = raw_ref[:, 3 * HEAD_SIZE : 4 * HEAD_SIZE].astype(bf)


def prepare(raw, cos, sin, gains):
    T, width = raw.shape
    blk = lambda w: pl.BlockSpec((BQ, w), lambda i: (i, 0))
    return pl.pallas_call(
        prepare_body,
        grid=(T // BQ,),
        in_specs=[blk(width), blk(HEAD_SIZE), blk(HEAD_SIZE), pl.BlockSpec((2, HEAD_SIZE), lambda i: (0, 0))],
        out_specs=[blk(2 * HEAD_SIZE), blk(2 * HEAD_SIZE)],
        out_shape=[jax.ShapeDtypeStruct((T, 2 * HEAD_SIZE), bf)] * 2,
        cost_estimate=pl.CostEstimate(flops=T * 4000, bytes_accessed=T * 640 * 8, transcendentals=T),
        name="prepare_heads",
    )(raw, cos, sin, gains)


def prepare_back_body(raw_ref, cos_ref, sin_ref, gain_ref, dq_ref, dkv_ref, back_ref, dlogit_ref, out_ref, sums_ref):
    @pl.when(pl.program_id(0) == 0)
    def _():
        sums_ref[...] = jnp.zeros_like(sums_ref)

    for i in range(3):
        cols = slice(i * HEAD_SIZE, (i + 1) * HEAD_SIZE)
        if i < 2:
            w = dq_ref[:, cols] * SCORE_SCALE
        else:
            w = dkv_ref[:, :HEAD_SIZE] + back_ref[:, :HEAD_SIZE].astype(f32)
        u = raw_ref[:, cols]
        j = 1 if i == 2 else 0
        r = lax.rsqrt(jnp.mean(u * u, axis=-1, keepdims=True) + EPS)
        w = w * cos_ref[...] + turn(w * sin_ref[...])
        sums_ref[j : j + 1, :] += jnp.sum(w * u * r, axis=0, keepdims=True)
        w = w * gain_ref[j : j + 1, :]
        out_ref[:, cols] = (r * w - u * (r * r * r * jnp.mean(w * u, axis=-1, keepdims=True))).astype(bf)
    out_ref[:, 3 * HEAD_SIZE : 4 * HEAD_SIZE] = (dkv_ref[:, HEAD_SIZE:] + back_ref[:, HEAD_SIZE:].astype(f32)).astype(bf)
    out_ref[:, 4 * HEAD_SIZE :] = dlogit_ref[...]


def prepare_back(raw, cos, sin, gains, dq, dkv, back, dlogit):
    T, width = raw.shape
    W = 2 * HEAD_SIZE
    blk = lambda w: pl.BlockSpec((BQ, w), lambda i: (i, 0))
    flat = pl.BlockSpec((2, HEAD_SIZE), lambda i: (0, 0))
    return pl.pallas_call(
        prepare_back_body,
        grid=(T // BQ,),
        in_specs=[blk(width), blk(HEAD_SIZE), blk(HEAD_SIZE), flat, blk(W), blk(W), blk(W), blk(HEAD_SIZE)],
        out_specs=[blk(width), flat],
        out_shape=[jax.ShapeDtypeStruct((T, width), bf), jax.ShapeDtypeStruct((2, HEAD_SIZE), f32)],
        cost_estimate=pl.CostEstimate(flops=T * 8000, bytes_accessed=T * 640 * 10, transcendentals=T),
        name="prepare_heads_back",
    )(raw, cos, sin, gains, dq, dkv, back, dlogit)


def gate_back_body(gm_ref, attn_ref, logit_ref, ga_ref, dlogit_ref, del_ref):
    lanes = lax.broadcasted_iota(jnp.int32, dlogit_ref.shape, 1)
    grads = jnp.zeros(dlogit_ref.shape, f32)
    for h in range(2):
        cols = slice(h * HEAD_SIZE, (h + 1) * HEAD_SIZE)
        g = jax.nn.sigmoid(logit_ref[:, h : h + 1])
        gm = gm_ref[:, cols]
        at = attn_ref[:, cols]
        ga = (gm * g).astype(bf)
        ga_ref[:, cols] = ga
        slope = jnp.sum(gm * at, axis=-1, keepdims=True) * (g * (1 - g))
        grads = jnp.where(lanes == h, slope, grads)
        del_ref[h : h + 1, :] = as_rows(jnp.sum(ga.astype(f32) * at, axis=-1, keepdims=True))
    dlogit_ref[...] = grads.astype(bf)


def gate_back(grad_mixed, attn, raw):
    T, W = attn.shape
    blk = lambda w, j=0: pl.BlockSpec((BQ, w), lambda i: (i, j))
    return pl.pallas_call(
        gate_back_body,
        grid=(T // BQ,),
        in_specs=[blk(W), blk(W), blk(HEAD_SIZE, raw.shape[1] // HEAD_SIZE - 1)],
        out_specs=[blk(W), blk(HEAD_SIZE), pl.BlockSpec((2, BQ), lambda i: (0, i))],
        out_shape=[
            jax.ShapeDtypeStruct((T, W), bf),
            jax.ShapeDtypeStruct((T, HEAD_SIZE), bf),
            jax.ShapeDtypeStruct((2, T), f32),
        ],
        cost_estimate=pl.CostEstimate(flops=T * 3000, bytes_accessed=T * 640 * 8, transcendentals=T),
        name="gate_back",
    )(grad_mixed, attn, raw)


GROUP=4
MESH=pl.DeviceIdType.MESH

def places():
    dp = lax.axis_index("dp"); c = lax.axis_index("mp")
    t = dp % GROUP
    base = dp - t
    tx = t + 1 - 2 * (t % 2)
    ty = t + 2 - 4 * (t // 2)
    td = 3 - t
    return base, t, tx, ty, td, c

def greet(devices):
    barrier = pltpu.get_barrier_semaphore()
    for device in devices:
        pl.semaphore_signal(barrier, inc=1, device_id=device, device_id_type=MESH)
    pl.semaphore_wait(barrier, len(devices))

def gather_body(x_ref, out_ref, send, recv, local):
    base, t, tx, ty, td, c = places()
    share = x_ref.shape[0]
    half = share // 2
    xdev, ydev, mate = (base + tx, c), (base + ty, c), (base + t, 1 - c)
    greet([xdev, ydev, mate])
    def spot(who, part=None):
        start = (2 * who + c) * share
        if part is None:
            return out_ref.at[pl.ds(pl.multiple_of(start, share), share)]
        return out_ref.at[pl.ds(pl.multiple_of(start + part * half, half), half)]
    def copy(kind, src, dst, device):
        return pltpu.make_async_remote_copy(src_ref=src, dst_ref=dst, send_sem=send.at[kind], recv_sem=recv.at[kind], device_id=device, device_id_type=MESH)
    own = pltpu.make_async_copy(x_ref, spot(t), local)
    own.start()
    mine = [x_ref.at[pl.ds(0, half)], x_ref.at[pl.ds(half, half)]]
    k = {}
    k[2] = copy(2, mine[0], spot(t, 0), ydev); k[2].start()
    k[1] = copy(1, mine[1], spot(t, 1), xdev); k[1].start()
    k[3] = copy(3, mine[1], spot(t, 1), ydev); k[3].start()
    k[0] = copy(0, mine[0], spot(t, 0), xdev); k[0].start()
    k[6] = copy(6, x_ref, spot(t), mate); k[6].start()
    k[2].wait_recv()
    k[4] = copy(4, spot(ty, 0), spot(ty, 0), xdev); k[4].start()
    k[9] = copy(9, spot(ty, 0), spot(ty, 0), mate); k[9].start()
    k[1].wait_recv()
    k[5] = copy(5, spot(tx, 1), spot(tx, 1), ydev); k[5].start()
    k[8] = copy(8, spot(tx, 1), spot(tx, 1), mate); k[8].start()
    k[0].wait_recv()
    k[7] = copy(7, spot(tx, 0), spot(tx, 0), mate); k[7].start()
    k[3].wait_recv()
    k[10] = copy(10, spot(ty, 1), spot(ty, 1), mate); k[10].start()
    k[4].wait_recv()
    k[11] = copy(11, spot(td, 0), spot(td, 0), mate); k[11].start()
    k[5].wait_recv()
    k[12] = copy(12, spot(td, 1), spot(td, 1), mate); k[12].start()
    for kind in range(6, 13):
        k[kind].wait_recv()
    for kind in range(13):
        k[kind].wait_send()
    own.wait()

def gather_group(x):
    share, width = x.shape
    return pl.pallas_call(
        gather_body,
        out_shape=jax.ShapeDtypeStruct((share * GROUP * 2, width), x.dtype),
        in_specs=[pl.BlockSpec(memory_space=pltpu.VMEM)],
        out_specs=pl.BlockSpec(memory_space=pl.ANY),
        scratch_shapes=[pltpu.SemaphoreType.DMA((13,)), pltpu.SemaphoreType.DMA((13,)), pltpu.SemaphoreType.DMA],
        compiler_params=pltpu.CompilerParams(collective_id=1, has_side_effects=True),
        name="gather_group",
    )(x)

def reduce_body(p_ref, out_ref, near, mates, sums, xin, yin, zin, turn, load, send, recv):
    base, t, tx, ty, td, c = places()
    share = out_ref.shape[0]
    half = share // 2
    xdev, ydev, mate = (base + tx, c), (base + ty, c), (base + t, 1 - c)
    greet([xdev, ydev, mate])
    def spot(who, core):
        return p_ref.at[pl.ds(pl.multiple_of((2 * who + core) * share, share), share)]
    def copy(kind, src, dst, device):
        return pltpu.make_async_remote_copy(src_ref=src, dst_ref=dst, send_sem=send.at[kind], recv_sem=recv.at[kind], device_id=device, device_id_type=MESH)
    def add(dst, left, right):
        step = 16
        def go(i, _):
            rows = pl.ds(pl.multiple_of(i * step, step), step)
            dst[rows, :] = (left[rows, :].astype(f32) + right[rows, :].astype(f32)).astype(dst.dtype)
            return 0
        lax.fori_loop(0, dst.shape[0] // step, go, 0)
    order = [td, tx, ty, t]
    over, loads = [], []
    for i, who in enumerate(order):
        over.append(copy(i, spot(who, 1 - c), mates.at[i], mate)); over[i].start()
        loads.append(pltpu.make_async_copy(spot(who, c), near.at[i], load.at[i])); loads[i].start()
    A, B = pl.ds(0, half), pl.ds(half, half)
    k = {}
    for i in range(4):
        loads[i].wait()
        over[i].wait_recv()
        add(sums.at[i], near.at[i], mates.at[i])
        if i == 0:
            k[4] = copy(4, sums.at[0, A], xin.at[1], xdev); k[4].start()
            k[5] = copy(5, sums.at[0, B], yin.at[1], ydev); k[5].start()
        if i == 1:
            k[6] = copy(6, sums.at[1, A], xin.at[0], xdev); k[6].start()
        if i == 2:
            k[7] = copy(7, sums.at[2, B], yin.at[0], ydev); k[7].start()
    k[4].wait_recv()
    add(turn.at[0], sums.at[2, A], xin.at[1])
    k[8] = copy(8, turn.at[0], zin.at[0], ydev); k[8].start()
    k[5].wait_recv()
    add(turn.at[1], sums.at[1, B], yin.at[1])
    k[9] = copy(9, turn.at[1], zin.at[1], xdev); k[9].start()
    k[6].wait_recv()
    add(out_ref.at[A], sums.at[3, A], xin.at[0])
    k[7].wait_recv()
    add(out_ref.at[B], sums.at[3, B], yin.at[0])
    k[8].wait_recv()
    add(out_ref.at[A], out_ref.at[A], zin.at[0])
    k[9].wait_recv()
    add(out_ref.at[B], out_ref.at[B], zin.at[1])
    for i in range(4):
        over[i].wait_send()
    for kind in range(4, 10):
        k[kind].wait_send()

def reduce_group(p):
    rows, width = p.shape
    share = rows // (2 * GROUP)
    half = share // 2
    return pl.pallas_call(
        reduce_body,
        out_shape=jax.ShapeDtypeStruct((share, width), f32),
        in_specs=[pl.BlockSpec(memory_space=pl.ANY)],
        out_specs=pl.BlockSpec(memory_space=pltpu.VMEM),
        scratch_shapes=[pltpu.VMEM((4, share, width), bf), pltpu.VMEM((4, share, width), bf), pltpu.VMEM((4, share, width), bf),
            pltpu.VMEM((2, half, width), bf), pltpu.VMEM((2, half, width), bf), pltpu.VMEM((2, half, width), bf), pltpu.VMEM((2, half, width), bf),
            pltpu.SemaphoreType.DMA((4,)), pltpu.SemaphoreType.DMA((10,)), pltpu.SemaphoreType.DMA((10,))],
        compiler_params=pltpu.CompilerParams(collective_id=2, has_side_effects=True),
        name="reduce_group",
    )(p)

def trade_body(x_ref, out_ref, send, recv, local):
    base, t, tx, ty, td, c = places()
    partners = [td, tx, ty]
    greet([(base + who, c) for who in partners])
    own = pltpu.make_async_copy(x_ref.at[t], out_ref.at[t], local)
    copies = []
    for i, who in enumerate(partners):
        copies.append(pltpu.make_async_remote_copy(src_ref=x_ref.at[who], dst_ref=out_ref.at[t], send_sem=send.at[i], recv_sem=recv.at[i], device_id=(base + who, c), device_id_type=MESH))
        copies[i].start()
    own.start()
    for one in copies:
        one.wait()
    own.wait()

def trade_group(x, key):
    return pl.pallas_call(
        trade_body,
        out_shape=jax.ShapeDtypeStruct(x.shape, x.dtype),
        in_specs=[pl.BlockSpec(memory_space=pltpu.VMEM)],
        out_specs=pl.BlockSpec(memory_space=pl.ANY),
        scratch_shapes=[pltpu.SemaphoreType.DMA((3,)), pltpu.SemaphoreType.DMA((3,)), pltpu.SemaphoreType.DMA],
        compiler_params=pltpu.CompilerParams(collective_id=key, has_side_effects=True),
        name="trade_group",
    )(x)

def far_places():
    dp = lax.axis_index("dp")
    return dp // GROUP, lax.axis_size("dp") // GROUP

def gather_all_body(x_ref, out_ref, send, recv, local):
    base, t, tx, ty, td, c = places()
    r, count = far_places()
    mates = [td, tx, ty]
    others = [(r + i) % count for i in range(1, count)]
    greet([(z * GROUP + t, c) for z in others] + [(base + who, c) for who in mates] + [(base + t, 1 - c)])
    def copy(kind, src, dst, device):
        return pltpu.make_async_remote_copy(src_ref=src, dst_ref=dst, send_sem=send.at[kind], recv_sem=recv.at[kind], device_id=device, device_id_type=MESH)
    own = pltpu.make_async_copy(x_ref, out_ref.at[c, t, r], local)
    own.start()
    stage = [copy(i, x_ref, out_ref.at[c, t, r], (z * GROUP + t, c)) for i, z in enumerate(others)]
    for one in stage: one.start()
    own.wait()
    for one in stage: one.wait()
    stage = [copy(count - 1 + i, out_ref.at[c, t], out_ref.at[c, t], (base + who, c)) for i, who in enumerate(mates)]
    for one in stage: one.start()
    for one in stage: one.wait()
    last = copy(count + 2, out_ref.at[c], out_ref.at[c], (base + t, 1 - c))
    last.start()
    last.wait()

def gather_all(x):
    count = lax.axis_size("dp") // GROUP
    return pl.pallas_call(
        gather_all_body,
        out_shape=jax.ShapeDtypeStruct((2, GROUP, count) + x.shape, x.dtype),
        in_specs=[pl.BlockSpec(memory_space=pltpu.VMEM)],
        out_specs=pl.BlockSpec(memory_space=pltpu.VMEM),
        scratch_shapes=[pltpu.SemaphoreType.DMA((count + 3,)), pltpu.SemaphoreType.DMA((count + 3,)), pltpu.SemaphoreType.DMA],
        compiler_params=pltpu.CompilerParams(collective_id=11, has_side_effects=True),
        name="gather_all",
    )(x)

def reduce_all_body(x_ref, out_ref, one_in, one_sum, two_in, two_sum, far_in, send, recv):
    base, t, tx, ty, td, c = places()
    r, count = far_places()
    mates = [td, tx, ty]
    others = [(r + i) % count for i in range(1, count)]
    greet([(z * GROUP + t, c) for z in others] + [(base + who, c) for who in mates] + [(base + t, 1 - c)])
    def copy(kind, src, dst, device):
        return pltpu.make_async_remote_copy(src_ref=src, dst_ref=dst, send_sem=send.at[kind], recv_sem=recv.at[kind], device_id=device, device_id_type=MESH)
    first = copy(0, x_ref.at[1 - c], one_in, (base + t, 1 - c))
    first.start()
    first.wait()
    one_sum[...] = x_ref[c] + one_in[...]
    stage = [copy(1 + i, one_sum.at[who], two_in.at[i], (base + who, c)) for i, who in enumerate(mates)]
    for one in stage: one.start()
    for one in stage: one.wait()
    two_sum[...] = one_sum[t] + two_in[0] + two_in[1] + two_in[2]
    stage = [copy(4 + i, two_sum.at[z], far_in.at[i], (z * GROUP + t, c)) for i, z in enumerate(others)]
    for one in stage: one.start()
    for one in stage: one.wait()
    total = two_sum[r]
    for i in range(count - 1):
        total = total + far_in[i]
    out_ref[...] = total

def reduce_all(x):
    tile = x.shape[3:]
    count = lax.axis_size("dp") // GROUP
    return pl.pallas_call(
        reduce_all_body,
        out_shape=jax.ShapeDtypeStruct(tile, x.dtype),
        in_specs=[pl.BlockSpec(memory_space=pltpu.VMEM)],
        out_specs=pl.BlockSpec(memory_space=pltpu.VMEM),
        scratch_shapes=[pltpu.VMEM((GROUP, count) + tile, f32), pltpu.VMEM((GROUP, count) + tile, f32), pltpu.VMEM((3, count) + tile, f32), pltpu.VMEM((count,) + tile, f32), pltpu.VMEM((count - 1,) + tile, f32),
            pltpu.SemaphoreType.DMA((count + 3,)), pltpu.SemaphoreType.DMA((count + 3,))],
        compiler_params=pltpu.CompilerParams(collective_id=12, has_side_effects=True),
        name="reduce_all",
    )(x)


def row_norm(values, gain):
    scale = lax.rsqrt(jnp.mean(values * values, axis=-1, keepdims=True) + EPS)
    return values * scale * gain


def rope_tables(positions, width):
    half = width // 2
    freqs = THETA ** (-(jnp.arange(half, dtype=f32) / half))
    angle = positions.astype(f32)[:, None] * freqs[None, :]
    cosine, sine = jnp.cos(angle), jnp.sin(angle)
    return (jnp.concatenate([cosine, cosine], axis=-1), jnp.concatenate([-sine, sine], axis=-1))


def swiglu(gate, up):
    return jax.nn.silu(gate) * up


def ancestors(parent_row, count):
    table = jnp.eye(count, dtype=jnp.int32)
    for seg_index in range(1, count):
        joined = jnp.maximum(table[seg_index], table[parent_row[seg_index]])
        table = table.at[seg_index].set(joined)
    return table


def segment_onehot(offsets, starts, count):
    segment = jnp.sum((offsets[:, None] >= starts[None, 1:]).astype(jnp.int32), axis=1)
    return (segment[:, None] == jnp.arange(count, dtype=jnp.int32)[None, :]).astype(jnp.int32)


def inner(left, right):
    return dg(left, right, TN)


def against(left, right):
    return dg(left, right, NT)


def after(value, *others):
    return lax.optimization_barrier((value,) + others)[0]


def by_member(weight, pieces):
    rows = weight.shape[0]
    return weight.reshape(rows, pieces, -1).transpose(1, 0, 2)


def from_members(pieces):
    return pieces.transpose(1, 0, 2).reshape(pieces.shape[1], -1)


def per_device(
    layer_in,
    out_grad,
    parents,
    lengths,
    attn_gain,
    mlp_gain,
    query_norm_gain,
    key_gain,
    query_weight,
    key_matrix,
    value_matrix,
    headgate_weight,
    output_weight,
    gate_weight,
    up_weight,
    down_weight,
):
    data_count = lax.axis_size("dp")
    model_count = lax.axis_size("mp")
    share, width = layer_in.shape
    rows_here = query_weight.shape[0]
    group_tokens = share * model_count * GROUP
    seg_count = parents.shape[1]
    far = [[member + GROUP * plane for plane in range(data_count // GROUP)] for member in range(GROUP)]
    planes = TREE_TOKENS // group_tokens

    pieces_attn = jnp.concatenate(
        [
            by_member(query_weight, GROUP),
            by_member(key_matrix, GROUP),
            by_member(value_matrix, GROUP),
            jnp.pad(by_member(headgate_weight, GROUP), ((0, 0), (0, 0), (0, HEAD_SIZE - headgate_weight.shape[1] // GROUP))),
        ],
        axis=-1,
    )
    pieces_out = by_member(output_weight.T, GROUP)
    pieces_glu = jnp.concatenate([by_member(gate_weight, GROUP), by_member(up_weight, GROUP)], axis=-1)
    pieces_down = by_member(down_weight.T, GROUP)

    def far_gather(mine):
        return lax.all_gather(
            mine.reshape(GROUP * rows_here, -1), "dp", axis=0, tiled=True, axis_index_groups=far
        )

    def far_scatter(grad):
        mine = lax.psum_scatter(grad, "dp", scatter_dimension=0, tiled=True, axis_index_groups=far)
        return mine.reshape(GROUP, rows_here, -1)

    mine_attn = trade_group(pieces_attn, 3)
    full_attn = far_gather(mine_attn)

    sizes = [attn_gain.shape[0], mlp_gain.shape[0], query_norm_gain.shape[0], key_gain.shape[0]]
    cuts = [sum(sizes[:i]) for i in range(5)]
    tile = (8, 128)
    spare = tile[0] * tile[1] - cuts[4]
    gain_tile = jnp.pad(
        jnp.concatenate([attn_gain, mlp_gain, query_norm_gain, key_gain]).astype(f32), (0, spare)
    ).reshape(tile)
    all_gains = gather_all(after(gain_tile, mine_attn))
    gains = all_gains.transpose(2, 1, 0, 3, 4).reshape(data_count * model_count, -1)
    gain_one, gain_two, gain_query, gain_key = [
        gains[:, cuts[i] : cuts[i + 1]].reshape(-1) for i in range(4)
    ]
    head_gains = jnp.stack([gain_query, gain_key])
    mine_out = trade_group(after(pieces_out, all_gains), 4)
    full_out = far_gather(mine_out)

    group_index = lax.axis_index("dp") // GROUP
    first = group_index * group_tokens
    tree = first // TREE_TOKENS
    begin = first - tree * TREE_TOKENS
    later = begin // group_tokens
    parent_row = lax.dynamic_index_in_dim(parents, tree, 0, keepdims=False)
    length_row = lax.dynamic_index_in_dim(lengths, tree, 0, keepdims=False)
    starts = jnp.cumsum(length_row) - length_row
    table = ancestors(parent_row, seg_count)
    depth = jnp.sum(table * length_row[None, :], axis=1) - length_row
    offsets = begin + jnp.arange(group_tokens, dtype=jnp.int32)
    onehot = segment_onehot(offsets, starts, seg_count)
    positions = jnp.sum(onehot * (depth - starts)[None, :], axis=1) + offsets
    powers = 1 << jnp.arange(seg_count, dtype=jnp.int32)
    query_bits = jnp.sum(onehot * jnp.sum(table * powers[None, :], axis=1)[None, :], axis=1)
    key_count = planes * group_tokens
    key_offsets = begin - (key_count - group_tokens) + jnp.arange(key_count, dtype=jnp.int32)
    key_hot = segment_onehot(key_offsets, starts, seg_count) * (key_offsets >= 0).astype(jnp.int32)[:, None]
    key_bits = jnp.sum(key_hot * powers[None, :], axis=1)
    query_has = jnp.max(onehot.reshape(-1, BQ, seg_count), axis=1)
    key_has = jnp.max(key_hot.reshape(-1, BK, seg_count), axis=1)
    early = key_count - group_tokens
    reached = jnp.dot(jnp.dot(query_has, table), key_has.T) > 0
    missed = jnp.dot(jnp.dot(query_has, 1 - table), key_has.T) > 0
    q_first = early + BQ * jnp.arange(query_has.shape[0], dtype=jnp.int32)[:, None]
    k_first = BK * jnp.arange(key_has.shape[0], dtype=jnp.int32)[None, :]
    some = reached & (k_first <= q_first + BQ - 1)
    every = ~missed & (k_first + BK - 1 <= q_first)
    flags = jnp.where(some, jnp.where(every, 2, 1), 0).astype(jnp.int32)
    cosine, sine = rope_tables(positions, HEAD_SIZE)
    query_column, query_line = query_bits[:, None], query_bits[None, :]
    key_lines = key_bits.reshape(-1, 1, BK)
    key_column = key_bits[:, None]
    key_cut = early // BK

    rows = layer_in.astype(f32)
    normed_one, norm_one_back = jax.vjp(row_norm, rows, gain_one)
    hidden_first = gather_group(after(normed_one.astype(bf), mine_out))
    raw = jnp.dot(hidden_first, full_attn, preferred_element_type=f32)
    q_width = query_weight.shape[1] // GROUP
    k_width = key_matrix.shape[1] // GROUP
    heads = q_width // HEAD_SIZE
    query, pair = prepare(raw, cosine, sine, head_gains)
    ahead = [(s, s + GROUP) for s in range(data_count) if (s // GROUP) % planes == 0]
    back = [(d, s) for s, d in ahead]
    pair_early = lax.ppermute(pair, "dp", ahead)
    mine_glu = trade_group(after(pieces_glu, query), 5)
    full_glu = far_gather(mine_glu)
    own = attend(True, flags[:, key_cut:], query, pair, query_column, key_lines[key_cut:])
    mine_down = trade_group(after(pieces_down, own[0], mine_glu), 6)
    full_down = far_gather(mine_down)
    attn, mixed, lse = attend(
        False, flags[:, :key_cut], query, pair_early, query_column, key_lines[:key_cut], (own[0], own[1], raw)
    )
    branch = reduce_group(after(against(mixed, full_out).astype(bf), mine_down))
    middle = rows + branch

    normed_two, norm_two_back = jax.vjp(row_norm, middle, gain_two)
    h_two = gather_group(normed_two.astype(bf))
    grad_tokens = gather_group(after(out_grad, h_two))
    both_glu = jnp.dot(h_two, full_glu, preferred_element_type=f32)
    units = full_down.shape[1]
    gate, up = both_glu[:, :units], both_glu[:, units:]
    hidden_f, glu_back = jax.vjp(swiglu, gate, up)
    hidden = hidden_f.astype(bf)

    down_part = inner(grad_tokens, hidden).astype(bf)
    down_rows = far_scatter(down_part)
    grad_hidden = jnp.dot(after(grad_tokens, down_part), full_down, preferred_element_type=f32)
    grad_gate_f, grad_up_f = glu_back(grad_hidden)
    grad_glu = jnp.concatenate([grad_gate_f.astype(bf), grad_up_f.astype(bf)], axis=1)
    glu_part = inner(h_two, grad_glu).astype(bf)
    glu_rows = far_scatter(glu_part)
    grad_h_two = reduce_group(against(after(grad_glu, glu_part), full_glu).astype(bf))
    grad_mid_norm, gain_two_grad = norm_two_back(grad_h_two)
    grad_middle = out_grad.astype(f32) + grad_mid_norm

    grad_branch = gather_group(grad_middle.astype(bf))
    grad_mixed = jnp.dot(grad_branch, full_out, preferred_element_type=f32)
    out_part = inner(after(grad_branch, grad_mixed), mixed).astype(bf)
    out_rows = far_scatter(out_part)
    grad_attn, grad_logit, delta = gate_back(grad_mixed, attn, raw)
    query_grad, early_grad = attend_back(
        False, flags[:, :key_cut], after(query, out_part), grad_attn, pair_early, query_line, key_column[:early], lse, delta
    )
    returned = lax.ppermute(early_grad, "dp", back)
    query_grad, own_grad = attend_back(
        True, flags[:, key_cut:], query, grad_attn, pair, query_line, key_column[early:], lse, delta, query_grad
    )
    down_grad = trade_group(after(down_rows, own_grad), 7)
    last_branch = reduce_group(after(against(after(hidden, own_grad), full_down).astype(bf), down_grad))
    layer_out = (middle + last_branch).astype(bf)
    glu_grad = trade_group(after(glu_rows, last_branch), 8)
    grad_raw, head_gain_grads = prepare_back(
        raw, cosine, sine, head_gains, query_grad, own_grad, after(returned, glu_grad), grad_logit
    )
    attn_part = inner(hidden_first, grad_raw).astype(bf)
    attn_rows = far_scatter(attn_part)
    grad_h_one = reduce_group(against(after(grad_raw, attn_part), full_attn).astype(bf))
    grad_in_norm, gain_one_grad = norm_one_back(grad_h_one)
    input_grad = (grad_middle + grad_in_norm).astype(bf)

    devices = data_count * model_count
    gain_parts = jnp.concatenate(
        [
            piece.reshape(devices, -1)
            for piece in (gain_one_grad, gain_two_grad, head_gain_grads[0], head_gain_grads[1], jnp.zeros((devices, spare), f32))
        ],
        axis=1,
    )
    gain_parts = gain_parts.reshape((data_count // GROUP, GROUP, model_count) + tile).transpose(2, 1, 0, 3, 4)
    gain_sums = reduce_all(gain_parts).reshape(-1)
    out_weight_grad = trade_group(after(out_rows, gain_sums), 9)
    attn_grad = trade_group(after(attn_rows, out_weight_grad), 10)
    full = lambda pieces: from_members(pieces).astype(f32)
    return (
        layer_out,
        input_grad,
        gain_sums[cuts[0] : cuts[1]],
        gain_sums[cuts[1] : cuts[2]],
        gain_sums[cuts[2] : cuts[3]],
        gain_sums[cuts[3] : cuts[4]],
        full(attn_grad[:, :, :q_width]),
        full(attn_grad[:, :, q_width : q_width + k_width]),
        full(attn_grad[:, :, q_width + k_width : q_width + 2 * k_width]),
        full(attn_grad[:, :, q_width + 2 * k_width : q_width + 2 * k_width + heads]),
        full(out_weight_grad).T,
        full(glu_grad[:, :, :units]),
        full(glu_grad[:, :, units:]),
        full(down_grad).T,
    )


def solution(mesh):
    in_specs = (
        P(("dp", "mp"), None),
        P(("dp", "mp"), None),
        P(),
        P(),
        P(("dp", "mp")),
        P(("dp", "mp")),
        P(("dp", "mp")),
        P(("dp", "mp")),
        P("dp", "mp"),
        P("dp", "mp"),
        P("dp", "mp"),
        P("dp", "mp"),
        P("mp", "dp"),
        P("dp", "mp"),
        P("dp", "mp"),
        P("mp", "dp"),
    )
    out_specs = (
        P(("dp", "mp"), None),
        P(("dp", "mp"), None),
        P(("dp", "mp")),
        P(("dp", "mp")),
        P(("dp", "mp")),
        P(("dp", "mp")),
        P("dp", "mp"),
        P("dp", "mp"),
        P("dp", "mp"),
        P("dp", "mp"),
        P("mp", "dp"),
        P("dp", "mp"),
        P("dp", "mp"),
        P("mp", "dp"),
    )
    return jax.shard_map(
        per_device, mesh=mesh, in_specs=in_specs, out_specs=out_specs, check_vma=False
    )
```

```python
from functools import partial

import jax
import jax.numpy as jnp
from jax import lax
from jax.experimental import pallas as pl
from jax.experimental.pallas import tpu as pltpu
from jax.sharding import PartitionSpec as P

HEAD_SIZE = 128
TREE_TOKENS = 4096
EPS = 1e-06
THETA = 1000000.0
f32 = jnp.float32
bf = jnp.bfloat16

LOG2E = 1.4426950408889634
SCORE_SCALE = HEAD_SIZE ** (-0.5)
BQ = 256
BK = 512
NT = (((1,), (1,)), ((), ()))
NN = (((1,), (0,)), ((), ()))
TN = (((0,), (0,)), ((), ()))


def dg(left, right, dims):
    return lax.dot_general(left, right, dims, preferred_element_type=f32)


def halves(ref, rows):
    return jnp.concatenate([ref[rows, :HEAD_SIZE], ref[rows, HEAD_SIZE:]], axis=0)


def as_rows(column):
    return jnp.broadcast_to(column, (column.shape[0], HEAD_SIZE)).T[0:1, :]


def attend_body(causal, last, flags, q_ref, kv_ref, qbit_ref, kbit_ref, *refs):
    if last:
        acc_in, tot_in, logit_ref, attn_ref, mixed_ref, lse_ref, acc, tot = refs
    else:
        acc_out, tot_out, acc, tot = refs
    qb = pl.program_id(0)
    bq = q_ref.shape[0]
    nk, _, bk = kbit_ref.shape
    q = halves(q_ref, slice(None))
    acc[...] = jnp.zeros_like(acc)
    tot[...] = jnp.zeros_like(tot)

    def step(kb, masked):
        rows = pl.ds(pl.multiple_of(kb * bk, bk), bk)
        s = dg(q, kv_ref[rows, :HEAD_SIZE], NT) * (LOG2E * SCORE_SCALE)
        if masked:
            seen = (qbit_ref[...] & kbit_ref[kb]) != 0
            if causal:
                at = lax.broadcasted_iota(jnp.int32, (bq, bk), 1) + kb * bk
                row = lax.broadcasted_iota(jnp.int32, (bq, bk), 0) + qb * bq
                seen = seen & (at <= row)
            s = jnp.where(jnp.concatenate([seen, seen], axis=0), s, -1e30)
        p = jnp.exp2(s)
        part = p[:, 0:128]
        for i in range(1, bk // 128):
            part = part + p[:, i * 128 : (i + 1) * 128]
        tot[...] += part
        acc[...] += dg(p.astype(bf), kv_ref[rows, HEAD_SIZE:], NN)

    def body(kb, _):
        flag = flags[qb, kb]
        pl.when(flag == 1)(lambda: step(kb, True))
        pl.when(flag == 2)(lambda: step(kb, False))
        return 0

    lax.fori_loop(0, nk, body, 0)
    total = jnp.sum(tot[...], axis=1, keepdims=True)
    if not last:
        acc_out[:, :HEAD_SIZE] = acc[:bq, :]
        acc_out[:, HEAD_SIZE:] = acc[bq:, :]
        tot_out[...] = jnp.concatenate([total[:bq], total[bq:]], axis=1)
    else:
        for h in range(2):
            rows = slice(h * bq, (h + 1) * bq)
            cols = slice(h * HEAD_SIZE, (h + 1) * HEAD_SIZE)
            sums = total[rows] + tot_in[:, h : h + 1]
            out = (acc[rows, :] + acc_in[:, cols]) / sums
            attn_ref[:, cols] = out
            mixed_ref[:, cols] = (out * jax.nn.sigmoid(logit_ref[:, h : h + 1])).astype(bf)
            lse_ref[h : h + 1, :] = as_rows(jnp.log2(sums))


def attend(causal, flags, q, kv, qbit, kbit, earlier=None):
    T = q.shape[0]
    N = kv.shape[0]
    nk = N // BK
    W = 2 * HEAD_SIZE
    blk = lambda w, j=0: pl.BlockSpec((BQ, w), lambda i, f: (i, j))
    last = earlier is not None
    in_specs = [
        blk(W),
        pl.BlockSpec((N, W), lambda i, f: (0, 0)),
        blk(1),
        pl.BlockSpec((nk, 1, BK), lambda i, f: (0, 0, 0)),
    ]
    if last:
        acc, tot, raw = earlier
        extra = [acc, tot, raw]
        in_specs += [blk(W), blk(2), blk(HEAD_SIZE, raw.shape[1] // HEAD_SIZE - 1)]
        out_specs = [blk(W), blk(W), pl.BlockSpec((2, BQ), lambda i, f: (0, i))]
        out_shape = [
            jax.ShapeDtypeStruct((T, W), f32),
            jax.ShapeDtypeStruct((T, W), bf),
            jax.ShapeDtypeStruct((2, T), f32),
        ]
    else:
        extra = []
        out_specs = [blk(W), blk(2)]
        out_shape = [jax.ShapeDtypeStruct((T, W), f32), jax.ShapeDtypeStruct((T, 2), f32)]
    return pl.pallas_call(
        partial(attend_body, causal, last),
        grid_spec=pltpu.PrefetchScalarGridSpec(
            num_scalar_prefetch=1,
            grid=(T // BQ,),
            in_specs=in_specs,
            out_specs=out_specs,
            scratch_shapes=[pltpu.VMEM((2 * BQ, HEAD_SIZE), f32), pltpu.VMEM((2 * BQ, HEAD_SIZE), f32)],
        ),
        out_shape=out_shape,
        cost_estimate=pl.CostEstimate(
            flops=(2 if causal else 4) * T * N * W, bytes_accessed=8 << 20, transcendentals=T * N * (1 if causal else 2)
        ),
        name="attend_own" if causal else "attend_earlier",
    )(flags, q, kv, qbit, kbit, *extra)


def attend_back_body(causal, flags, q_ref, g_ref, kv_ref, qbit_ref, kbit_ref, lse_ref, del_ref, *refs):
    if causal:
        dq_in, dq_ref, dkv_ref, dk_acc, dv_acc = refs
    else:
        dq_ref, dkv_ref, dk_acc, dv_acc = refs
    kb = pl.program_id(0)
    bk = kv_ref.shape[0]
    T = q_ref.shape[0]
    bq = BQ

    @pl.when(kb == 0)
    def _():
        if causal:
            dq_ref[...] = dq_in[...]
        else:
            dq_ref[...] = jnp.zeros_like(dq_ref)

    dk_acc[...] = jnp.zeros_like(dk_acc)
    dv_acc[...] = jnp.zeros_like(dv_acc)

    def line(ref, rows):
        return jnp.concatenate([ref[0:1, rows], ref[1:2, rows]], axis=1)

    def step(qb, masked):
        rows = pl.ds(pl.multiple_of(qb * bq, bq), bq)
        q = halves(q_ref, rows)
        g = halves(g_ref, rows)
        k = kv_ref[:, :HEAD_SIZE]
        s = dg(k, q, NT) * (LOG2E * SCORE_SCALE) - line(lse_ref, rows)
        if masked:
            seen = (kbit_ref[...] & qbit_ref[0:1, rows]) != 0
            if causal:
                at = lax.broadcasted_iota(jnp.int32, (bk, bq), 0) + kb * bk
                row = lax.broadcasted_iota(jnp.int32, (bk, bq), 1) + qb * bq
                seen = seen & (at <= row)
            s = jnp.where(jnp.concatenate([seen, seen], axis=1), s, -1e30)
        p = jnp.exp2(s)
        dv_acc[...] += dg(p.astype(bf), g, NN)
        dp = dg(kv_ref[:, HEAD_SIZE:], g, NT)
        ds = (p * (dp - line(del_ref, rows))).astype(bf)
        dk_acc[...] += dg(ds, q, NN)
        dq = dg(ds, k, TN)
        dq_ref[rows, :HEAD_SIZE] += dq[:bq]
        dq_ref[rows, HEAD_SIZE:] += dq[bq:]

    def body(qb, _):
        flag = flags[qb, kb]
        pl.when(flag == 1)(lambda: step(qb, True))
        pl.when(flag == 2)(lambda: step(qb, False))
        return 0

    lax.fori_loop(0, T // bq, body, 0)
    dkv_ref[:, :HEAD_SIZE] = (dk_acc[...] * SCORE_SCALE).astype(dkv_ref.dtype)
    dkv_ref[:, HEAD_SIZE:] = dv_acc[...].astype(dkv_ref.dtype)


def attend_back(causal, flags, q, g, kv, qbit, kbit, lse, delta, dq=None):
    T = q.shape[0]
    N = kv.shape[0]
    W = 2 * HEAD_SIZE
    whole = lambda *s: pl.BlockSpec(s, lambda i, f: (0,) * len(s))
    along = lambda w: pl.BlockSpec((BK, w), lambda i, f: (i, 0))
    in_specs = [whole(T, W), whole(T, W), along(W), whole(1, T), along(1), whole(2, T), whole(2, T)]
    extra = []
    if causal:
        in_specs.append(whole(T, W))
        extra = [dq]
    return pl.pallas_call(
        partial(attend_back_body, causal),
        grid_spec=pltpu.PrefetchScalarGridSpec(
            num_scalar_prefetch=1,
            grid=(N // BK,),
            in_specs=in_specs,
            out_specs=[whole(T, W), along(W)],
            scratch_shapes=[pltpu.VMEM((BK, HEAD_SIZE), f32), pltpu.VMEM((BK, HEAD_SIZE), f32)],
        ),
        out_shape=[jax.ShapeDtypeStruct((T, W), f32), jax.ShapeDtypeStruct((N, W), f32 if causal else bf)],
        cost_estimate=pl.CostEstimate(
            flops=(5 if causal else 10) * T * N * W, bytes_accessed=12 << 20, transcendentals=T * N * (1 if causal else 2)
        ),
        name="attend_own_back" if causal else "attend_earlier_back",
    )(flags, q, g, kv, qbit, kbit, lse, delta, *extra)


def turn(values):
    return pltpu.roll(values, HEAD_SIZE // 2, 1)


def prepare_body(raw_ref, cos_ref, sin_ref, gain_ref, q_ref, kv_ref):
    for i in range(3):
        cols = slice(i * HEAD_SIZE, (i + 1) * HEAD_SIZE)
        u = raw_ref[:, cols]
        r = lax.rsqrt(jnp.mean(u * u, axis=-1, keepdims=True) + EPS)
        n = u * r * gain_ref[(1 if i == 2 else 0) : (2 if i == 2 else 1), :]
        out = (n * cos_ref[...] + turn(n) * sin_ref[...]).astype(bf)
        if i < 2:
            q_ref[:, cols] = out
        else:
            kv_ref[:, :HEAD_SIZE] = out
    kv_ref[:, HEAD_SIZE:] = raw_ref[:, 3 * HEAD_SIZE : 4 * HEAD_SIZE].astype(bf)


def prepare(raw, cos, sin, gains):
    T, width = raw.shape
    blk = lambda w: pl.BlockSpec((BQ, w), lambda i: (i, 0))
    return pl.pallas_call(
        prepare_body,
        grid=(T // BQ,),
        in_specs=[blk(width), blk(HEAD_SIZE), blk(HEAD_SIZE), pl.BlockSpec((2, HEAD_SIZE), lambda i: (0, 0))],
        out_specs=[blk(2 * HEAD_SIZE), blk(2 * HEAD_SIZE)],
        out_shape=[jax.ShapeDtypeStruct((T, 2 * HEAD_SIZE), bf)] * 2,
        cost_estimate=pl.CostEstimate(flops=T * 4000, bytes_accessed=T * 640 * 8, transcendentals=T),
        name="prepare_heads",
    )(raw, cos, sin, gains)


def prepare_back_body(raw_ref, cos_ref, sin_ref, gain_ref, dq_ref, dkv_ref, back_ref, dlogit_ref, out_ref, sums_ref):
    @pl.when(pl.program_id(0) == 0)
    def _():
        sums_ref[...] = jnp.zeros_like(sums_ref)

    for i in range(3):
        cols = slice(i * HEAD_SIZE, (i + 1) * HEAD_SIZE)
        if i < 2:
            w = dq_ref[:, cols] * SCORE_SCALE
        else:
            w = dkv_ref[:, :HEAD_SIZE] + back_ref[:, :HEAD_SIZE].astype(f32)
        u = raw_ref[:, cols]
        j = 1 if i == 2 else 0
        r = lax.rsqrt(jnp.mean(u * u, axis=-1, keepdims=True) + EPS)
        w = w * cos_ref[...] + turn(w * sin_ref[...])
        sums_ref[j : j + 1, :] += jnp.sum(w * u * r, axis=0, keepdims=True)
        w = w * gain_ref[j : j + 1, :]
        out_ref[:, cols] = (r * w - u * (r * r * r * jnp.mean(w * u, axis=-1, keepdims=True))).astype(bf)
    out_ref[:, 3 * HEAD_SIZE : 4 * HEAD_SIZE] = (dkv_ref[:, HEAD_SIZE:] + back_ref[:, HEAD_SIZE:].astype(f32)).astype(bf)
    out_ref[:, 4 * HEAD_SIZE :] = dlogit_ref[...]


def prepare_back(raw, cos, sin, gains, dq, dkv, back, dlogit):
    T, width = raw.shape
    W = 2 * HEAD_SIZE
    blk = lambda w: pl.BlockSpec((BQ, w), lambda i: (i, 0))
    flat = pl.BlockSpec((2, HEAD_SIZE), lambda i: (0, 0))
    return pl.pallas_call(
        prepare_back_body,
        grid=(T // BQ,),
        in_specs=[blk(width), blk(HEAD_SIZE), blk(HEAD_SIZE), flat, blk(W), blk(W), blk(W), blk(HEAD_SIZE)],
        out_specs=[blk(width), flat],
        out_shape=[jax.ShapeDtypeStruct((T, width), bf), jax.ShapeDtypeStruct((2, HEAD_SIZE), f32)],
        cost_estimate=pl.CostEstimate(flops=T * 8000, bytes_accessed=T * 640 * 10, transcendentals=T),
        name="prepare_heads_back",
    )(raw, cos, sin, gains, dq, dkv, back, dlogit)


def gate_back_body(gm_ref, attn_ref, logit_ref, ga_ref, dlogit_ref, del_ref):
    lanes = lax.broadcasted_iota(jnp.int32, dlogit_ref.shape, 1)
    grads = jnp.zeros(dlogit_ref.shape, f32)
    for h in range(2):
        cols = slice(h * HEAD_SIZE, (h + 1) * HEAD_SIZE)
        g = jax.nn.sigmoid(logit_ref[:, h : h + 1])
        gm = gm_ref[:, cols]
        at = attn_ref[:, cols]
        ga = (gm * g).astype(bf)
        ga_ref[:, cols] = ga
        slope = jnp.sum(gm * at, axis=-1, keepdims=True) * (g * (1 - g))
        grads = jnp.where(lanes == h, slope, grads)
        del_ref[h : h + 1, :] = as_rows(jnp.sum(ga.astype(f32) * at, axis=-1, keepdims=True))
    dlogit_ref[...] = grads.astype(bf)


def gate_back(grad_mixed, attn, raw):
    T, W = attn.shape
    blk = lambda w, j=0: pl.BlockSpec((BQ, w), lambda i: (i, j))
    return pl.pallas_call(
        gate_back_body,
        grid=(T // BQ,),
        in_specs=[blk(W), blk(W), blk(HEAD_SIZE, raw.shape[1] // HEAD_SIZE - 1)],
        out_specs=[blk(W), blk(HEAD_SIZE), pl.BlockSpec((2, BQ), lambda i: (0, i))],
        out_shape=[
            jax.ShapeDtypeStruct((T, W), bf),
            jax.ShapeDtypeStruct((T, HEAD_SIZE), bf),
            jax.ShapeDtypeStruct((2, T), f32),
        ],
        cost_estimate=pl.CostEstimate(flops=T * 3000, bytes_accessed=T * 640 * 8, transcendentals=T),
        name="gate_back",
    )(grad_mixed, attn, raw)


GROUP = 4
MESH = pl.DeviceIdType.MESH
QUICK = pl.CostEstimate(flops=0, bytes_accessed=1 << 16, transcendentals=0)

def places():
    dp = lax.axis_index("dp"); c = lax.axis_index("mp")
    t = dp % GROUP
    base = dp - t
    tx = t + 1 - 2 * (t % 2)
    ty = t + 2 - 4 * (t // 2)
    td = 3 - t
    return base, t, tx, ty, td, c

def greet(devices):
    barrier = pltpu.get_barrier_semaphore()
    for device in devices:
        pl.semaphore_signal(barrier, inc=1, device_id=device, device_id_type=MESH)
    pl.semaphore_wait(barrier, len(devices))

def gather_body(x_ref, out_ref, send, recv, local):
    base, t, tx, ty, td, c = places()
    share = x_ref.shape[0]
    half = share // 2
    xdev, ydev, mate = (base + tx, c), (base + ty, c), (base + t, 1 - c)
    greet([xdev, ydev, mate])
    def spot(who, part=None):
        start = (2 * who + c) * share
        if part is None:
            return out_ref.at[pl.ds(pl.multiple_of(start, share), share)]
        return out_ref.at[pl.ds(pl.multiple_of(start + part * half, half), half)]
    def copy(kind, src, dst, device):
        return pltpu.make_async_remote_copy(src_ref=src, dst_ref=dst, send_sem=send.at[kind], recv_sem=recv.at[kind], device_id=device, device_id_type=MESH)
    own = pltpu.make_async_copy(x_ref, spot(t), local)
    own.start()
    mine = [x_ref.at[pl.ds(0, half)], x_ref.at[pl.ds(half, half)]]
    k = {}
    k[2] = copy(2, mine[0], spot(t, 0), ydev); k[2].start()
    k[1] = copy(1, mine[1], spot(t, 1), xdev); k[1].start()
    k[3] = copy(3, mine[1], spot(t, 1), ydev); k[3].start()
    k[0] = copy(0, mine[0], spot(t, 0), xdev); k[0].start()
    k[6] = copy(6, x_ref, spot(t), mate); k[6].start()
    k[2].wait_recv()
    k[4] = copy(4, spot(ty, 0), spot(ty, 0), xdev); k[4].start()
    k[9] = copy(9, spot(ty, 0), spot(ty, 0), mate); k[9].start()
    k[1].wait_recv()
    k[5] = copy(5, spot(tx, 1), spot(tx, 1), ydev); k[5].start()
    k[8] = copy(8, spot(tx, 1), spot(tx, 1), mate); k[8].start()
    k[0].wait_recv()
    k[7] = copy(7, spot(tx, 0), spot(tx, 0), mate); k[7].start()
    k[3].wait_recv()
    k[10] = copy(10, spot(ty, 1), spot(ty, 1), mate); k[10].start()
    k[4].wait_recv()
    k[11] = copy(11, spot(td, 0), spot(td, 0), mate); k[11].start()
    k[5].wait_recv()
    k[12] = copy(12, spot(td, 1), spot(td, 1), mate); k[12].start()
    for kind in range(6, 13):
        k[kind].wait_recv()
    for kind in range(13):
        k[kind].wait_send()
    own.wait()

def gather_group(x):
    share, width = x.shape
    return pl.pallas_call(
        gather_body,
        out_shape=jax.ShapeDtypeStruct((share * GROUP * 2, width), x.dtype),
        in_specs=[pl.BlockSpec(memory_space=pltpu.VMEM)],
        out_specs=pl.BlockSpec(memory_space=pl.ANY),
        scratch_shapes=[pltpu.SemaphoreType.DMA((13,)), pltpu.SemaphoreType.DMA((13,)), pltpu.SemaphoreType.DMA],
        compiler_params=pltpu.CompilerParams(collective_id=1, has_side_effects=True),
        cost_estimate=QUICK,
        name="gather_group",
    )(x)

def reduce_body(left_ref, right_ref, out_ref, left, right, fars, near, mates, sums, xin, yin, zin, turned, fetch, send, recv):
    base, t, tx, ty, td, c = places()
    share = out_ref.shape[0]
    half = share // 2
    chunk = right.shape[0] // 4
    xdev, ydev, mate = (base + tx, c), (base + ty, c), (base + t, 1 - c)
    order = [td, tx, ty, t]
    lefts, rights = [], []
    for i, who in enumerate(order):
        for side, core in enumerate((1 - c, c)):
            rows = pl.ds(pl.multiple_of((2 * who + core) * share, share), share)
            n = 2 * i + side
            lefts.append(pltpu.make_async_copy(left_ref.at[rows], left.at[n], fetch.at[n]))
    for j in range(4):
        rows = pl.ds(j * chunk, chunk)
        rights.append(pltpu.make_async_copy(right_ref.at[rows], right.at[rows], fetch.at[8 + j]))
    for one in lefts[:2] + rights + lefts[2:]:
        one.start()
    greet([xdev, ydev, mate])

    def copy(kind, src, dst, device):
        return pltpu.make_async_remote_copy(
            src_ref=src, dst_ref=dst, send_sem=send.at[kind], recv_sem=recv.at[kind], device_id=device, device_id_type=MESH
        )

    def product(n, dst):
        lefts[n].wait()

        def go(j, _):
            rows = pl.ds(pl.multiple_of(j * chunk, chunk), chunk)
            dst[:, rows] = dg(left[n], right[rows, :], NT).astype(dst.dtype)
            return 0

        if n == 0:
            for j in range(4):
                rights[j].wait()
                go(j, 0)
        else:
            lax.fori_loop(0, 4, go, 0)

    def add(dst, one, two):
        step = 16

        def go(i, _):
            rows = pl.ds(pl.multiple_of(i * step, step), step)
            dst[rows, :] = (one[rows, :].astype(f32) + two[rows, :].astype(f32)).astype(dst.dtype)
            return 0

        lax.fori_loop(0, dst.shape[0] // step, go, 0)

    A, B = pl.ds(0, half), pl.ds(half, half)
    over, k = [], {}

    def join(i):
        over[i].wait_recv()
        add(sums.at[i], near.at[i], mates.at[i])
        if i == 0:
            k[4] = copy(4, sums.at[0, A], xin.at[1], xdev)
            k[5] = copy(5, sums.at[0, B], yin.at[1], ydev)
            k[4].start()
            k[5].start()
        if i == 1:
            k[6] = copy(6, sums.at[1, A], xin.at[0], xdev)
            k[6].start()
        if i == 2:
            k[7] = copy(7, sums.at[2, B], yin.at[0], ydev)
            k[7].start()

    for i in range(4):
        product(2 * i, fars.at[i])
        over.append(copy(i, fars.at[i], mates.at[i], mate))
        over[i].start()
        product(2 * i + 1, near.at[i])
        if i:
            join(i - 1)
    join(3)
    k[4].wait_recv()
    add(turned.at[0], sums.at[2, A], xin.at[1])
    k[8] = copy(8, turned.at[0], zin.at[0], ydev)
    k[8].start()
    k[5].wait_recv()
    add(turned.at[1], sums.at[1, B], yin.at[1])
    k[9] = copy(9, turned.at[1], zin.at[1], xdev)
    k[9].start()
    k[6].wait_recv()
    add(out_ref.at[A], sums.at[3, A], xin.at[0])
    k[7].wait_recv()
    add(out_ref.at[B], sums.at[3, B], yin.at[0])
    k[8].wait_recv()
    add(out_ref.at[A], out_ref.at[A], zin.at[0])
    k[9].wait_recv()
    add(out_ref.at[B], out_ref.at[B], zin.at[1])
    for i in range(4):
        over[i].wait_send()
    for kind in range(4, 10):
        k[kind].wait_send()


def product_reduce(left, right, key):
    rows, depth = left.shape
    width = right.shape[0]
    share = rows // (2 * GROUP)
    half = share // 2
    block = lambda n, r: pltpu.VMEM((n, r, width), bf)
    return pl.pallas_call(
        reduce_body,
        out_shape=jax.ShapeDtypeStruct((share, width), f32),
        in_specs=[pl.BlockSpec(memory_space=pl.ANY)] * 2,
        out_specs=pl.BlockSpec(memory_space=pltpu.VMEM),
        scratch_shapes=[
            pltpu.VMEM((2 * GROUP, share, depth), bf),
            pltpu.VMEM((width, depth), bf),
            block(4, share),
            block(4, share),
            block(4, share),
            block(4, share),
            block(2, half),
            block(2, half),
            block(2, half),
            block(2, half),
            pltpu.SemaphoreType.DMA((12,)),
            pltpu.SemaphoreType.DMA((10,)),
            pltpu.SemaphoreType.DMA((10,)),
        ],
        compiler_params=pltpu.CompilerParams(collective_id=key, has_side_effects=True, vmem_limit_bytes=56 << 20),
        cost_estimate=QUICK,
        name="product_reduce",
    )(left, right)


def gather_product_body(glu, x_ref, w_ref, full_ref, y_ref, *refs):
    if glu:
        hidden_ref, refs = refs[0], refs[1:]
        hs, refs = refs[0], refs[1:]
    buf, w, ys, fetch, put_x, put_y, send, recv = refs
    base, t, tx, ty, td, c = places()
    share = x_ref.shape[0]
    half = share // 2
    width = w.shape[1]
    xdev, ydev, mate = (base + tx, c), (base + ty, c), (base + t, 1 - c)
    weights = pltpu.make_async_copy(w_ref, w, fetch)
    weights.start()
    greet([xdev, ydev, mate])

    def unit(who, core):
        return pl.ds(pl.multiple_of((2 * who + core) * share, share), share)

    def spot(who, part):
        start = (2 * who + c) * share + part * half
        return buf.at[pl.ds(pl.multiple_of(start, half), half)]

    def copy(kind, src, dst, device):
        one = pltpu.make_async_remote_copy(
            src_ref=src, dst_ref=dst, send_sem=send.at[kind], recv_sem=recv.at[kind], device_id=device, device_id_type=MESH
        )
        one.start()
        return one

    mine = [x_ref.at[pl.ds(0, half)], x_ref.at[pl.ds(half, half)]]
    k, puts = {}, []
    k[2] = copy(2, mine[0], spot(t, 0), ydev)
    k[1] = copy(1, mine[1], spot(t, 1), xdev)
    k[3] = copy(3, mine[1], spot(t, 1), ydev)
    k[0] = copy(0, mine[0], spot(t, 0), xdev)
    k[6] = copy(6, x_ref, buf.at[unit(t, c)], mate)
    weights.wait()

    def work(n, src, who, core):
        rows = unit(who, core)
        slot = n % 2
        one = pltpu.make_async_copy(src, full_ref.at[rows], put_x.at[n])
        one.start()
        if n >= 2:
            for old in puts[n - 2][1:]:
                old.wait()
        if glu:
            chunk = 256

            def go(j, _):
                left = pl.ds(pl.multiple_of(j * chunk, chunk), chunk)
                right = pl.ds(pl.multiple_of(width // 2 + j * chunk, chunk), chunk)
                gate = dg(src[...], w[:, left], NN)
                up = dg(src[...], w[:, right], NN)
                ys[slot, :, left] = gate
                ys[slot, :, right] = up
                hs[slot, :, left] = (gate * jax.nn.sigmoid(gate) * up).astype(bf)
                return 0

            lax.fori_loop(0, width // 2 // chunk, go, 0)
        else:
            chunk = 128 if width % 256 else 256

            def go(j, _):
                cols = pl.ds(pl.multiple_of(j * chunk, chunk), chunk)
                ys[slot, :, cols] = dg(src[...], w[:, cols], NN)
                return 0

            lax.fori_loop(0, width // chunk, go, 0)
        outs = [one, pltpu.make_async_copy(ys.at[slot], y_ref.at[rows], put_y.at[n])]
        if glu:
            outs.append(pltpu.make_async_copy(hs.at[slot], hidden_ref.at[rows], put_y.at[8 + n]))
        for out in outs[1:]:
            out.start()
        puts.append(outs)

    def landed(who, core):
        return buf.at[unit(who, core)]

    work(0, x_ref, t, c)
    k[6].wait_recv()
    work(1, landed(t, 1 - c), t, 1 - c)
    k[2].wait_recv()
    k[4] = copy(4, spot(ty, 0), spot(ty, 0), xdev)
    k[9] = copy(9, spot(ty, 0), spot(ty, 0), mate)
    k[1].wait_recv()
    k[5] = copy(5, spot(tx, 1), spot(tx, 1), ydev)
    k[8] = copy(8, spot(tx, 1), spot(tx, 1), mate)
    k[0].wait_recv()
    k[7] = copy(7, spot(tx, 0), spot(tx, 0), mate)
    k[3].wait_recv()
    k[10] = copy(10, spot(ty, 1), spot(ty, 1), mate)
    work(2, landed(tx, c), tx, c)
    work(3, landed(ty, c), ty, c)
    k[7].wait_recv()
    k[8].wait_recv()
    work(4, landed(tx, 1 - c), tx, 1 - c)
    k[9].wait_recv()
    k[10].wait_recv()
    work(5, landed(ty, 1 - c), ty, 1 - c)
    k[4].wait_recv()
    k[11] = copy(11, spot(td, 0), spot(td, 0), mate)
    k[5].wait_recv()
    k[12] = copy(12, spot(td, 1), spot(td, 1), mate)
    work(6, landed(td, c), td, c)
    k[11].wait_recv()
    k[12].wait_recv()
    work(7, landed(td, 1 - c), td, 1 - c)
    for kind in range(13):
        k[kind].wait_send()
    for n, outs in enumerate(puts):
        outs[0].wait()
        if n >= 6:
            for out in outs[1:]:
                out.wait()


def gather_product(x, w, key, glu=False):
    share, depth = x.shape
    width = w.shape[1]
    rows = share * GROUP * 2
    anywhere = pl.BlockSpec(memory_space=pl.ANY)
    outs = [jax.ShapeDtypeStruct((rows, depth), bf), jax.ShapeDtypeStruct((rows, width), f32)]
    extra = []
    if glu:
        outs.append(jax.ShapeDtypeStruct((rows, width // 2), bf))
        extra = [pltpu.VMEM((2, share, width // 2), bf)]
    return pl.pallas_call(
        partial(gather_product_body, glu),
        out_shape=outs,
        in_specs=[pl.BlockSpec(memory_space=pltpu.VMEM), anywhere],
        out_specs=[anywhere] * len(outs),
        scratch_shapes=extra
        + [
            pltpu.VMEM((rows, depth), bf),
            pltpu.VMEM((depth, width), bf),
            pltpu.VMEM((2, share, width), f32),
            pltpu.SemaphoreType.DMA,
            pltpu.SemaphoreType.DMA((8,)),
            pltpu.SemaphoreType.DMA((16,)),
            pltpu.SemaphoreType.DMA((13,)),
            pltpu.SemaphoreType.DMA((13,)),
        ],
        compiler_params=pltpu.CompilerParams(collective_id=key, has_side_effects=True, vmem_limit_bytes=48 << 20),
        cost_estimate=QUICK,
        name="gather_product",
    )(x, w)


def trade_body(widths, kv, out_side, *refs):
    count = len(widths)
    base, t, tx, ty, td, c = places()
    partners = [td, tx, ty]
    friends = [(base + who, c) for who in partners]
    if kv:
        ins, refs = refs[: count + 1], refs[count + 1 :]
        outs, refs = refs[:2], refs[2:]
        send, recv, local = refs
        plane = lax.axis_index("dp") // GROUP
        late = plane % kv
        friends.append((lax.axis_index("dp") + (GROUP - 2 * GROUP * late), c))
    elif out_side:
        ins, outs, (send, recv, local) = refs[:1], refs[1 : 1 + count], refs[1 + count :]
    else:
        ins, outs, (send, recv, local) = refs[:count], refs[count : count + 1], refs[count + 1 :]
    greet(friends)
    starts = [sum(widths[:i]) for i in range(count)]

    def column(who, width):
        return pl.ds(pl.multiple_of(who * width, width), width)

    def source(i, who):
        if out_side:
            return ins[0].at[who, :, pl.ds(starts[i], widths[i])]
        return ins[i].at[:, column(who, widths[i])]

    def target(i):
        if out_side:
            return outs[i].at[:, column(t, widths[i])]
        return outs[0].at[t, :, pl.ds(starts[i], widths[i])]

    copies = []
    for j, who in enumerate(partners):
        for i in range(count):
            kind = j * count + i
            one = pltpu.make_async_remote_copy(
                src_ref=source(i, who),
                dst_ref=target(i),
                send_sem=send.at[kind],
                recv_sem=recv.at[kind],
                device_id=(base + who, c),
                device_id_type=MESH,
            )
            one.start()
            copies.append(one)
    if kv:
        pair = pltpu.make_async_remote_copy(
            src_ref=ins[count],
            dst_ref=outs[1],
            send_sem=send.at[3 * count],
            recv_sem=recv.at[3 * count],
            device_id=friends[-1],
            device_id_type=MESH,
        )
        keep = pltpu.make_async_copy(ins[count], outs[1], local.at[count])

        @pl.when(late == 0)
        def _():
            pair.start()
            keep.start()

    owns = [pltpu.make_async_copy(source(i, t), target(i), local.at[i]) for i in range(count)]
    for own in owns:
        own.start()
    for one in copies:
        one.wait()
    for own in owns:
        own.wait()
    if kv:

        @pl.when(late == 0)
        def _():
            pair.wait_send()
            keep.wait()

        @pl.when(late == 1)
        def _():
            pair.wait_recv()


def trade_call(ins, outs, widths, key, kv, out_side):
    vmem = pl.BlockSpec(memory_space=pltpu.VMEM)
    anywhere = pl.BlockSpec(memory_space=pl.ANY)
    kinds = 3 * len(widths) + 1
    return pl.pallas_call(
        partial(trade_body, widths, kv, out_side),
        out_shape=outs,
        in_specs=[vmem] * len(ins),
        out_specs=[anywhere] * len(outs),
        scratch_shapes=[
            pltpu.SemaphoreType.DMA((kinds,)),
            pltpu.SemaphoreType.DMA((kinds,)),
            pltpu.SemaphoreType.DMA((len(widths) + 1,)),
        ],
        compiler_params=pltpu.CompilerParams(collective_id=key, has_side_effects=True),
        cost_estimate=QUICK,
        name="trade_group",
    )(*ins)


def trade_group(weights, key, pair=None, planes=2):
    rows = weights[0].shape[0]
    widths = tuple(w.shape[1] // GROUP for w in weights)
    outs = [jax.ShapeDtypeStruct((GROUP, rows, sum(widths)), bf)]
    if pair is None:
        return trade_call(weights, outs, widths, key, 0, False)[0]
    outs.append(jax.ShapeDtypeStruct(pair.shape, bf))
    return trade_call(list(weights) + [pair], outs, widths, key, planes, False)


def trade_back(grad, widths, key):
    rows = grad.shape[1]
    outs = [jax.ShapeDtypeStruct((rows, GROUP * w), bf) for w in widths]
    return trade_call([grad], outs, tuple(widths), key, 0, True)


def far_places():
    dp = lax.axis_index("dp")
    return dp // GROUP, lax.axis_size("dp") // GROUP

def gather_all_body(x_ref, out_ref, send, recv, local):
    base, t, tx, ty, td, c = places()
    r, count = far_places()
    mates = [td, tx, ty]
    others = [(r + i) % count for i in range(1, count)]
    greet([(z * GROUP + t, c) for z in others] + [(base + who, c) for who in mates] + [(base + t, 1 - c)])
    def copy(kind, src, dst, device):
        return pltpu.make_async_remote_copy(src_ref=src, dst_ref=dst, send_sem=send.at[kind], recv_sem=recv.at[kind], device_id=device, device_id_type=MESH)
    own = pltpu.make_async_copy(x_ref, out_ref.at[c, t, r], local)
    own.start()
    stage = [copy(i, x_ref, out_ref.at[c, t, r], (z * GROUP + t, c)) for i, z in enumerate(others)]
    for one in stage: one.start()
    own.wait()
    for one in stage: one.wait()
    stage = [copy(count - 1 + i, out_ref.at[c, t], out_ref.at[c, t], (base + who, c)) for i, who in enumerate(mates)]
    for one in stage: one.start()
    for one in stage: one.wait()
    last = copy(count + 2, out_ref.at[c], out_ref.at[c], (base + t, 1 - c))
    last.start()
    last.wait()

def gather_all(x):
    count = lax.axis_size("dp") // GROUP
    return pl.pallas_call(
        gather_all_body,
        out_shape=jax.ShapeDtypeStruct((2, GROUP, count) + x.shape, x.dtype),
        in_specs=[pl.BlockSpec(memory_space=pltpu.VMEM)],
        out_specs=pl.BlockSpec(memory_space=pltpu.VMEM),
        scratch_shapes=[pltpu.SemaphoreType.DMA((count + 3,)), pltpu.SemaphoreType.DMA((count + 3,)), pltpu.SemaphoreType.DMA],
        compiler_params=pltpu.CompilerParams(collective_id=11, has_side_effects=True),
        cost_estimate=QUICK,
        name="gather_all",
    )(x)

def reduce_all_body(x_ref, out_ref, one_in, one_sum, two_in, two_sum, far_in, send, recv):
    base, t, tx, ty, td, c = places()
    r, count = far_places()
    mates = [td, tx, ty]
    others = [(r + i) % count for i in range(1, count)]
    greet([(z * GROUP + t, c) for z in others] + [(base + who, c) for who in mates] + [(base + t, 1 - c)])
    def copy(kind, src, dst, device):
        return pltpu.make_async_remote_copy(src_ref=src, dst_ref=dst, send_sem=send.at[kind], recv_sem=recv.at[kind], device_id=device, device_id_type=MESH)
    first = copy(0, x_ref.at[1 - c], one_in, (base + t, 1 - c))
    first.start()
    first.wait()
    one_sum[...] = x_ref[c] + one_in[...]
    stage = [copy(1 + i, one_sum.at[who], two_in.at[i], (base + who, c)) for i, who in enumerate(mates)]
    for one in stage: one.start()
    for one in stage: one.wait()
    two_sum[...] = one_sum[t] + two_in[0] + two_in[1] + two_in[2]
    stage = [copy(4 + i, two_sum.at[z], far_in.at[i], (z * GROUP + t, c)) for i, z in enumerate(others)]
    for one in stage: one.start()
    for one in stage: one.wait()
    total = two_sum[r]
    for i in range(count - 1):
        total = total + far_in[i]
    out_ref[...] = total

def reduce_all(x):
    tile = x.shape[3:]
    count = lax.axis_size("dp") // GROUP
    return pl.pallas_call(
        reduce_all_body,
        out_shape=jax.ShapeDtypeStruct(tile, x.dtype),
        in_specs=[pl.BlockSpec(memory_space=pltpu.VMEM)],
        out_specs=pl.BlockSpec(memory_space=pltpu.VMEM),
        scratch_shapes=[pltpu.VMEM((GROUP, count) + tile, f32), pltpu.VMEM((GROUP, count) + tile, f32), pltpu.VMEM((3, count) + tile, f32), pltpu.VMEM((count,) + tile, f32), pltpu.VMEM((count - 1,) + tile, f32),
            pltpu.SemaphoreType.DMA((count + 3,)), pltpu.SemaphoreType.DMA((count + 3,))],
        compiler_params=pltpu.CompilerParams(collective_id=12, has_side_effects=True),
        cost_estimate=QUICK,
        name="reduce_all",
    )(x)


def row_norm(values, gain):
    scale = lax.rsqrt(jnp.mean(values * values, axis=-1, keepdims=True) + EPS)
    return values * scale * gain


def rope_tables(positions, width):
    half = width // 2
    lanes = jnp.arange(width, dtype=jnp.int32)
    freqs = THETA ** (-((lanes % half).astype(f32) / half))
    angle = positions.astype(f32) * freqs[None, :]
    return jnp.cos(angle), jnp.sin(angle) * jnp.where(lanes < half, -1.0, 1.0)[None, :]


def tables_body(group_tokens, early, seg_count, parents, lengths, pos_ref, qcol_ref, qline_ref, kline_ref, kcol_ref, flags, key_any):
    step = pl.program_id(0)
    first = lax.axis_index("dp") // GROUP * group_tokens
    tree = first // TREE_TOKENS
    begin = first - tree * TREE_TOKENS
    size = [lengths[tree, seg] for seg in range(seg_count)]
    starts, bits, depth = [jnp.int32(0)], [jnp.int32(1)], [jnp.int32(0)]
    for seg in range(1, seg_count):
        starts.append(starts[-1] + size[seg - 1])
        parent = parents[tree, seg]
        above, deep = bits[0], depth[0] + size[0]
        for p in range(1, seg):
            above = jnp.where(parent == p, bits[p], above)
            deep = jnp.where(parent == p, depth[p] + size[p], deep)
        bits.append(above | (1 << seg))
        depth.append(deep)
    powers = [jnp.int32(1 << seg) for seg in range(seg_count)]

    def by_segment(offsets, values):
        out = jnp.zeros_like(offsets) + values[0]
        for start, value in zip(starts[1:], values[1:]):
            out = jnp.where(offsets >= start, value, out)
        return out

    q_first = begin + step * BQ
    k_first = begin - early + step * BK
    column = lax.broadcasted_iota(jnp.int32, (BQ, 1), 0) + q_first
    pos_ref[...] = by_segment(column, [d - s for d, s in zip(depth, starts)]) + column
    qcol_ref[...] = by_segment(column, bits)
    qline_ref[...] = by_segment(lax.broadcasted_iota(jnp.int32, (1, BQ), 1) + q_first, bits)
    column = lax.broadcasted_iota(jnp.int32, (BK, 1), 0) + k_first
    kcol_ref[...] = jnp.where(column >= 0, by_segment(column, powers), 0)
    line = lax.broadcasted_iota(jnp.int32, (1, BK), 1) + k_first
    kline_ref[0] = jnp.where(line >= 0, by_segment(line, powers), 0)

    def touches(begins, seg, span):
        return (starts[seg] <= begins + span - 1) & (starts[seg] + size[seg] > begins)

    @pl.when(step == 0)
    def _():
        for k in range(key_any.shape[0]):
            seen = jnp.int32(0)
            for seg in range(seg_count):
                seen = jnp.where(touches(begin - early + k * BK, seg, BK), seen | powers[seg], seen)
            key_any[k] = seen

    query_any, query_all = jnp.int32(0), jnp.int32(-1)
    for seg in range(seg_count):
        inside = touches(q_first, seg, BQ)
        query_any = jnp.where(inside, query_any | bits[seg], query_any)
        query_all = jnp.where(inside, query_all & bits[seg], query_all)
    for k in range(key_any.shape[0]):
        keys_at = begin - early + k * BK
        some = ((query_any & key_any[k]) != 0) & (keys_at <= q_first + BQ - 1)
        every = ((key_any[k] & ~query_all) == 0) & (keys_at + BK - 1 <= q_first)
        flags[step, k] = jnp.where(some, jnp.where(every, 2, 1), 0)


def tables(parents, lengths, group_tokens, planes):
    seg_count = parents.shape[1]
    early = (planes - 1) * group_tokens
    steps = group_tokens // BQ
    blocks = planes * group_tokens // BK
    i32 = lambda *shape: jax.ShapeDtypeStruct(shape, jnp.int32)
    smem = pl.BlockSpec(memory_space=pltpu.SMEM)
    return pl.pallas_call(
        partial(tables_body, group_tokens, early, seg_count),
        grid=(steps,),
        in_specs=[smem, smem],
        out_specs=[
            pl.BlockSpec((BQ, 1), lambda i: (i, 0)),
            pl.BlockSpec((BQ, 1), lambda i: (i, 0)),
            pl.BlockSpec((1, BQ), lambda i: (0, i)),
            pl.BlockSpec((1, 1, BK), lambda i: (i, 0, 0)),
            pl.BlockSpec((BK, 1), lambda i: (i, 0)),
            smem,
        ],
        out_shape=[
            i32(group_tokens, 1),
            i32(group_tokens, 1),
            i32(1, group_tokens),
            i32(blocks, 1, BK),
            i32(blocks * BK, 1),
            i32(steps, blocks),
        ],
        scratch_shapes=[pltpu.SMEM((blocks,), jnp.int32)],
        cost_estimate=QUICK,
        name="tables",
    )(parents, lengths)


def inner(left, right):
    return dg(left, right, TN)


def after(value, *others):
    return lax.optimization_barrier((value,) + others)[0]


def per_device(
    layer_in,
    out_grad,
    parents,
    lengths,
    attn_gain,
    mlp_gain,
    query_norm_gain,
    key_gain,
    query_weight,
    key_matrix,
    value_matrix,
    headgate_weight,
    output_weight,
    gate_weight,
    up_weight,
    down_weight,
):
    data_count = lax.axis_size("dp")
    model_count = lax.axis_size("mp")
    share, width = layer_in.shape
    rows_here = query_weight.shape[0]
    group_tokens = share * model_count * GROUP
    seg_count = parents.shape[1]
    far = [[member + GROUP * plane for plane in range(data_count // GROUP)] for member in range(GROUP)]
    planes = TREE_TOKENS // group_tokens

    gates = headgate_weight.shape[1] // GROUP
    pieces_gates = jnp.pad(
        headgate_weight.reshape(rows_here, GROUP, gates), ((0, 0), (0, 0), (0, HEAD_SIZE - gates))
    ).reshape(rows_here, GROUP * HEAD_SIZE)

    def far_gather(mine):
        return lax.all_gather(
            mine.reshape(GROUP * rows_here, -1), "dp", axis=0, tiled=True, axis_index_groups=far
        )

    def far_scatter(grad):
        mine = lax.psum_scatter(grad, "dp", scatter_dimension=0, tiled=True, axis_index_groups=far)
        return mine.reshape(GROUP, rows_here, -1)

    mine_attn = trade_group([query_weight, key_matrix, value_matrix, pieces_gates], 3)
    full_attn = far_gather(mine_attn)

    sizes = [attn_gain.shape[0], mlp_gain.shape[0], query_norm_gain.shape[0], key_gain.shape[0]]
    cuts = [sum(sizes[:i]) for i in range(5)]
    tile = (8, 128)
    spare = tile[0] * tile[1] - cuts[4]
    gain_tile = jnp.pad(
        jnp.concatenate([attn_gain, mlp_gain, query_norm_gain, key_gain]).astype(f32), (0, spare)
    ).reshape(tile)
    all_gains = gather_all(after(gain_tile, mine_attn))
    gains = all_gains.transpose(2, 1, 0, 3, 4).reshape(data_count * model_count, -1)
    gain_one, gain_two, gain_query, gain_key = [
        gains[:, cuts[i] : cuts[i + 1]].reshape(-1) for i in range(4)
    ]
    head_gains = jnp.stack([gain_query, gain_key])
    mine_out = trade_group([after(output_weight.T, all_gains)], 4)
    full_out = far_gather(mine_out)

    positions, query_column, query_line, key_lines, key_column, flags = tables(parents, lengths, group_tokens, planes)
    cosine, sine = rope_tables(positions, HEAD_SIZE)
    early = (planes - 1) * group_tokens
    key_cut = early // BK

    rows = layer_in.astype(f32)
    normed_one, norm_one_back = jax.vjp(row_norm, rows, gain_one)
    hidden_first = gather_group(after(normed_one.astype(bf), mine_out))
    raw = jnp.dot(hidden_first, full_attn, preferred_element_type=f32)
    q_width = query_weight.shape[1] // GROUP
    k_width = key_matrix.shape[1] // GROUP
    heads = q_width // HEAD_SIZE
    query, pair = prepare(raw, cosine, sine, head_gains)
    ahead = [(s, s + GROUP) for s in range(data_count) if (s // GROUP) % planes == 0]
    back = [(d, s) for s, d in ahead]
    mine_glu, pair_early = trade_group([gate_weight, up_weight], 5, pair, planes)
    full_glu = far_gather(mine_glu)
    query = after(query, mine_glu)
    own = attend(True, flags[:, key_cut:], query, pair, query_column, key_lines[key_cut:])
    mine_down = trade_group([after(down_weight.T, own[0])], 6)
    full_down = far_gather(mine_down)
    grad_tokens = gather_group(after(out_grad, mine_down))
    attn, mixed, lse = attend(
        False, flags[:, :key_cut], after(query, grad_tokens), pair_early, query_column, key_lines[:key_cut], (own[0], own[1], raw)
    )
    branch = product_reduce(mixed, full_out, 2)
    middle = rows + branch

    normed_two, norm_two_back = jax.vjp(row_norm, middle, gain_two)
    h_two, both_glu, hidden = gather_product(normed_two.astype(bf), full_glu, 14, True)
    units = full_down.shape[1]
    gate, up = both_glu[:, :units], both_glu[:, units:]

    down_part = inner(grad_tokens, hidden).astype(bf)
    down_rows = far_scatter(down_part)
    grad_hidden = jnp.dot(after(grad_tokens, down_part), full_down, preferred_element_type=f32)
    open_gate = jax.nn.sigmoid(gate)
    grad_gate = grad_hidden * up * open_gate * (1 + gate * (1 - open_gate))
    grad_up = grad_hidden * gate * open_gate
    grad_glu = jnp.concatenate([grad_gate.astype(bf), grad_up.astype(bf)], axis=1)
    glu_part = inner(h_two, grad_glu).astype(bf)
    glu_rows = far_scatter(glu_part)
    grad_h_two = product_reduce(after(grad_glu, glu_part), full_glu, 15)
    grad_mid_norm, gain_two_grad = norm_two_back(grad_h_two)
    grad_middle = out_grad.astype(f32) + grad_mid_norm

    grad_branch, grad_mixed = gather_product(grad_middle.astype(bf), full_out, 16)
    out_part = inner(after(grad_branch, grad_mixed), mixed).astype(bf)
    out_rows = far_scatter(out_part)
    grad_attn, grad_logit, delta = gate_back(grad_mixed, attn, raw)
    query_grad, early_grad = attend_back(
        False, flags[:, :key_cut], after(query, out_part), grad_attn, pair_early, query_line, key_column[:early], lse, delta
    )
    returned = lax.ppermute(early_grad, "dp", back)
    query_grad, own_grad = attend_back(
        True, flags[:, key_cut:], query, grad_attn, pair, query_line, key_column[early:], lse, delta, query_grad
    )
    (down_grad,) = trade_back(after(down_rows, own_grad), [units], 7)
    gate_grad, up_grad = trade_back(after(glu_rows, down_grad), [units, units], 8)
    grad_raw, head_gain_grads = prepare_back(
        raw, cosine, sine, head_gains, query_grad, own_grad, after(returned, gate_grad), grad_logit
    )
    attn_part = inner(hidden_first, grad_raw).astype(bf)
    attn_rows = far_scatter(attn_part)
    grad_h_one = product_reduce(after(grad_raw, attn_part), full_attn, 17)
    grad_in_norm, gain_one_grad = norm_one_back(grad_h_one)
    input_grad = (grad_middle + grad_in_norm).astype(bf)
    last_branch = product_reduce(after(hidden, grad_h_one), full_down, 18)
    layer_out = (middle + last_branch).astype(bf)

    devices = data_count * model_count
    gain_parts = jnp.concatenate(
        [
            piece.reshape(devices, -1)
            for piece in (gain_one_grad, gain_two_grad, head_gain_grads[0], head_gain_grads[1], jnp.zeros((devices, spare), f32))
        ],
        axis=1,
    )
    gain_parts = gain_parts.reshape((data_count // GROUP, GROUP, model_count) + tile).transpose(2, 1, 0, 3, 4)
    (out_weight_grad,) = trade_back(after(out_rows, last_branch), [q_width], 9)
    gain_sums = reduce_all(after(gain_parts, out_weight_grad)).reshape(-1)
    q_grad, k_grad, v_grad, gates_grad = trade_back(
        after(attn_rows, gain_sums), [q_width, k_width, k_width, HEAD_SIZE], 10
    )
    gates_grad = gates_grad.reshape(rows_here, GROUP, HEAD_SIZE)[:, :, :heads].reshape(rows_here, -1)
    return (
        layer_out,
        input_grad,
        gain_sums[cuts[0] : cuts[1]],
        gain_sums[cuts[1] : cuts[2]],
        gain_sums[cuts[2] : cuts[3]],
        gain_sums[cuts[3] : cuts[4]],
        q_grad.astype(f32),
        k_grad.astype(f32),
        v_grad.astype(f32),
        gates_grad.astype(f32),
        out_weight_grad.astype(f32).T,
        gate_grad.astype(f32),
        up_grad.astype(f32),
        down_grad.astype(f32).T,
    )


def solution(mesh):
    in_specs = (
        P(("dp", "mp"), None),
        P(("dp", "mp"), None),
        P(),
        P(),
        P(("dp", "mp")),
        P(("dp", "mp")),
        P(("dp", "mp")),
        P(("dp", "mp")),
        P("dp", "mp"),
        P("dp", "mp"),
        P("dp", "mp"),
        P("dp", "mp"),
        P("mp", "dp"),
        P("dp", "mp"),
        P("dp", "mp"),
        P("mp", "dp"),
    )
    out_specs = (
        P(("dp", "mp"), None),
        P(("dp", "mp"), None),
        P(("dp", "mp")),
        P(("dp", "mp")),
        P(("dp", "mp")),
        P(("dp", "mp")),
        P("dp", "mp"),
        P("dp", "mp"),
        P("dp", "mp"),
        P("dp", "mp"),
        P("mp", "dp"),
        P("dp", "mp"),
        P("dp", "mp"),
        P("mp", "dp"),
    )
    return jax.shard_map(
        per_device, mesh=mesh, in_specs=in_specs, out_specs=out_specs, check_vma=False
    )
```

```python
from functools import partial

import jax
import jax.numpy as jnp
from jax import lax
from jax.experimental import pallas as pl
from jax.experimental.pallas import tpu as pltpu
from jax.sharding import PartitionSpec as P

HEAD_SIZE = 128
TREE_TOKENS = 4096
EPS = 1e-06
THETA = 1000000.0
f32 = jnp.float32
bf = jnp.bfloat16

LOG2E = 1.4426950408889634
SCORE_SCALE = HEAD_SIZE ** (-0.5)
BQ = 256
BK = 512
NT = (((1,), (1,)), ((), ()))
NN = (((1,), (0,)), ((), ()))
TN = (((0,), (0,)), ((), ()))


def dg(left, right, dims):
    return lax.dot_general(left, right, dims, preferred_element_type=f32)


def halves(ref, rows):
    return jnp.concatenate([ref[rows, :HEAD_SIZE], ref[rows, HEAD_SIZE:]], axis=0)


def as_rows(column):
    return jnp.broadcast_to(column, (column.shape[0], HEAD_SIZE)).T[0:1, :]


def attend_body(causal, last, flags, q_ref, kv_ref, qbit_ref, kbit_ref, *refs):
    if last:
        acc_in, tot_in, logit_ref, attn_ref, mixed_ref, lse_ref, acc, tot = refs
    else:
        acc_out, tot_out, acc, tot = refs
    qb = pl.program_id(0)
    bq = q_ref.shape[0]
    nk, _, bk = kbit_ref.shape
    q = halves(q_ref, slice(None))
    acc[...] = jnp.zeros_like(acc)
    tot[...] = jnp.zeros_like(tot)

    def step(kb, masked):
        rows = pl.ds(pl.multiple_of(kb * bk, bk), bk)
        s = dg(q, kv_ref[rows, :HEAD_SIZE], NT) * (LOG2E * SCORE_SCALE)
        if masked:
            seen = (qbit_ref[...] & kbit_ref[kb]) != 0
            if causal:
                at = lax.broadcasted_iota(jnp.int32, (bq, bk), 1) + kb * bk
                row = lax.broadcasted_iota(jnp.int32, (bq, bk), 0) + qb * bq
                seen = seen & (at <= row)
            s = jnp.where(jnp.concatenate([seen, seen], axis=0), s, -1e30)
        p = jnp.exp2(s)
        part = p[:, 0:128]
        for i in range(1, bk // 128):
            part = part + p[:, i * 128 : (i + 1) * 128]
        tot[...] += part
        acc[...] += dg(p.astype(bf), kv_ref[rows, HEAD_SIZE:], NN)

    def body(kb, _):
        flag = flags[qb, kb]
        pl.when(flag == 1)(lambda: step(kb, True))
        pl.when(flag == 2)(lambda: step(kb, False))
        return 0

    lax.fori_loop(0, nk, body, 0)
    total = jnp.sum(tot[...], axis=1, keepdims=True)
    if not last:
        acc_out[:, :HEAD_SIZE] = acc[:bq, :]
        acc_out[:, HEAD_SIZE:] = acc[bq:, :]
        tot_out[...] = jnp.concatenate([total[:bq], total[bq:]], axis=1)
    else:
        for h in range(2):
            rows = slice(h * bq, (h + 1) * bq)
            cols = slice(h * HEAD_SIZE, (h + 1) * HEAD_SIZE)
            sums = total[rows] + tot_in[:, h : h + 1]
            out = (acc[rows, :] + acc_in[:, cols]) / sums
            attn_ref[:, cols] = out
            mixed_ref[:, cols] = (out * jax.nn.sigmoid(logit_ref[:, h : h + 1])).astype(bf)
            lse_ref[h : h + 1, :] = as_rows(jnp.log2(sums))


def attend(causal, flags, q, kv, qbit, kbit, earlier=None):
    T = q.shape[0]
    N = kv.shape[0]
    nk = N // BK
    W = 2 * HEAD_SIZE
    blk = lambda w, j=0: pl.BlockSpec((BQ, w), lambda i, f: (i, j))
    last = earlier is not None
    in_specs = [
        blk(W),
        pl.BlockSpec((N, W), lambda i, f: (0, 0)),
        blk(1),
        pl.BlockSpec((nk, 1, BK), lambda i, f: (0, 0, 0)),
    ]
    if last:
        acc, tot, raw = earlier
        extra = [acc, tot, raw]
        in_specs += [blk(W), blk(2), blk(HEAD_SIZE, raw.shape[1] // HEAD_SIZE - 1)]
        out_specs = [blk(W), blk(W), pl.BlockSpec((2, BQ), lambda i, f: (0, i))]
        out_shape = [
            jax.ShapeDtypeStruct((T, W), f32),
            jax.ShapeDtypeStruct((T, W), bf),
            jax.ShapeDtypeStruct((2, T), f32),
        ]
    else:
        extra = []
        out_specs = [blk(W), blk(2)]
        out_shape = [jax.ShapeDtypeStruct((T, W), f32), jax.ShapeDtypeStruct((T, 2), f32)]
    return pl.pallas_call(
        partial(attend_body, causal, last),
        grid_spec=pltpu.PrefetchScalarGridSpec(
            num_scalar_prefetch=1,
            grid=(T // BQ,),
            in_specs=in_specs,
            out_specs=out_specs,
            scratch_shapes=[pltpu.VMEM((2 * BQ, HEAD_SIZE), f32), pltpu.VMEM((2 * BQ, HEAD_SIZE), f32)],
        ),
        out_shape=out_shape,
        cost_estimate=pl.CostEstimate(
            flops=(2 if causal else 4) * T * N * W, bytes_accessed=8 << 20, transcendentals=T * N * (1 if causal else 2)
        ),
        name="attend_own" if causal else "attend_earlier",
    )(flags, q, kv, qbit, kbit, *extra)


def attend_back_body(causal, flags, q_ref, g_ref, kv_ref, qbit_ref, kbit_ref, lse_ref, del_ref, *refs):
    if causal:
        dq_in, dq_ref, dkv_ref, dk_acc, dv_acc = refs
    else:
        dq_ref, dkv_ref, dk_acc, dv_acc = refs
    kb = pl.program_id(0)
    bk = kv_ref.shape[0]
    T = q_ref.shape[0]
    bq = BQ

    @pl.when(kb == 0)
    def _():
        if causal:
            dq_ref[...] = dq_in[...]
        else:
            dq_ref[...] = jnp.zeros_like(dq_ref)

    dk_acc[...] = jnp.zeros_like(dk_acc)
    dv_acc[...] = jnp.zeros_like(dv_acc)

    def line(ref, rows):
        return jnp.concatenate([ref[0:1, rows], ref[1:2, rows]], axis=1)

    def step(qb, masked):
        rows = pl.ds(pl.multiple_of(qb * bq, bq), bq)
        q = halves(q_ref, rows)
        g = halves(g_ref, rows)
        k = kv_ref[:, :HEAD_SIZE]
        s = dg(k, q, NT) * (LOG2E * SCORE_SCALE) - line(lse_ref, rows)
        if masked:
            seen = (kbit_ref[...] & qbit_ref[0:1, rows]) != 0
            if causal:
                at = lax.broadcasted_iota(jnp.int32, (bk, bq), 0) + kb * bk
                row = lax.broadcasted_iota(jnp.int32, (bk, bq), 1) + qb * bq
                seen = seen & (at <= row)
            s = jnp.where(jnp.concatenate([seen, seen], axis=1), s, -1e30)
        p = jnp.exp2(s)
        dv_acc[...] += dg(p.astype(bf), g, NN)
        dp = dg(kv_ref[:, HEAD_SIZE:], g, NT)
        ds = (p * (dp - line(del_ref, rows))).astype(bf)
        dk_acc[...] += dg(ds, q, NN)
        dq = dg(ds, k, TN)
        dq_ref[rows, :HEAD_SIZE] += dq[:bq]
        dq_ref[rows, HEAD_SIZE:] += dq[bq:]

    def body(qb, _):
        flag = flags[qb, kb]
        pl.when(flag == 1)(lambda: step(qb, True))
        pl.when(flag == 2)(lambda: step(qb, False))
        return 0

    lax.fori_loop(0, T // bq, body, 0)
    dkv_ref[:, :HEAD_SIZE] = (dk_acc[...] * SCORE_SCALE).astype(dkv_ref.dtype)
    dkv_ref[:, HEAD_SIZE:] = dv_acc[...].astype(dkv_ref.dtype)


def attend_back(causal, flags, q, g, kv, qbit, kbit, lse, delta, dq=None):
    T = q.shape[0]
    N = kv.shape[0]
    W = 2 * HEAD_SIZE
    whole = lambda *s: pl.BlockSpec(s, lambda i, f: (0,) * len(s))
    along = lambda w: pl.BlockSpec((BK, w), lambda i, f: (i, 0))
    in_specs = [whole(T, W), whole(T, W), along(W), whole(1, T), along(1), whole(2, T), whole(2, T)]
    extra = []
    if causal:
        in_specs.append(whole(T, W))
        extra = [dq]
    return pl.pallas_call(
        partial(attend_back_body, causal),
        grid_spec=pltpu.PrefetchScalarGridSpec(
            num_scalar_prefetch=1,
            grid=(N // BK,),
            in_specs=in_specs,
            out_specs=[whole(T, W), along(W)],
            scratch_shapes=[pltpu.VMEM((BK, HEAD_SIZE), f32), pltpu.VMEM((BK, HEAD_SIZE), f32)],
        ),
        out_shape=[jax.ShapeDtypeStruct((T, W), f32), jax.ShapeDtypeStruct((N, W), f32 if causal else bf)],
        cost_estimate=pl.CostEstimate(
            flops=(5 if causal else 10) * T * N * W, bytes_accessed=12 << 20, transcendentals=T * N * (1 if causal else 2)
        ),
        name="attend_own_back" if causal else "attend_earlier_back",
    )(flags, q, g, kv, qbit, kbit, lse, delta, *extra)


def turn(values):
    return pltpu.roll(values, HEAD_SIZE // 2, 1)


def prepare_body(raw_ref, cos_ref, sin_ref, gain_ref, q_ref, kv_ref):
    for i in range(3):
        cols = slice(i * HEAD_SIZE, (i + 1) * HEAD_SIZE)
        u = raw_ref[:, cols]
        r = lax.rsqrt(jnp.mean(u * u, axis=-1, keepdims=True) + EPS)
        n = u * r * gain_ref[(1 if i == 2 else 0) : (2 if i == 2 else 1), :]
        out = (n * cos_ref[...] + turn(n) * sin_ref[...]).astype(bf)
        if i < 2:
            q_ref[:, cols] = out
        else:
            kv_ref[:, :HEAD_SIZE] = out
    kv_ref[:, HEAD_SIZE:] = raw_ref[:, 3 * HEAD_SIZE : 4 * HEAD_SIZE].astype(bf)


def prepare(raw, cos, sin, gains):
    T, width = raw.shape
    blk = lambda w: pl.BlockSpec((BQ, w), lambda i: (i, 0))
    return pl.pallas_call(
        prepare_body,
        grid=(T // BQ,),
        in_specs=[blk(width), blk(HEAD_SIZE), blk(HEAD_SIZE), pl.BlockSpec((2, HEAD_SIZE), lambda i: (0, 0))],
        out_specs=[blk(2 * HEAD_SIZE), blk(2 * HEAD_SIZE)],
        out_shape=[jax.ShapeDtypeStruct((T, 2 * HEAD_SIZE), bf)] * 2,
        cost_estimate=pl.CostEstimate(flops=T * 4000, bytes_accessed=T * 640 * 8, transcendentals=T),
        name="prepare_heads",
    )(raw, cos, sin, gains)


def prepare_back_body(raw_ref, cos_ref, sin_ref, gain_ref, dq_ref, dkv_ref, back_ref, dlogit_ref, out_ref, sums_ref):
    @pl.when(pl.program_id(0) == 0)
    def _():
        sums_ref[...] = jnp.zeros_like(sums_ref)

    sent = lax.axis_index("dp") // GROUP % 2 == 0
    back = jnp.where(sent, back_ref[...].astype(f32), 0.0)
    for i in range(3):
        cols = slice(i * HEAD_SIZE, (i + 1) * HEAD_SIZE)
        if i < 2:
            w = dq_ref[:, cols] * SCORE_SCALE
        else:
            w = dkv_ref[:, :HEAD_SIZE] + back[:, :HEAD_SIZE]
        u = raw_ref[:, cols]
        j = 1 if i == 2 else 0
        r = lax.rsqrt(jnp.mean(u * u, axis=-1, keepdims=True) + EPS)
        w = w * cos_ref[...] + turn(w * sin_ref[...])
        sums_ref[j : j + 1, :] += jnp.sum(w * u * r, axis=0, keepdims=True)
        w = w * gain_ref[j : j + 1, :]
        out_ref[:, cols] = (r * w - u * (r * r * r * jnp.mean(w * u, axis=-1, keepdims=True))).astype(bf)
    out_ref[:, 3 * HEAD_SIZE : 4 * HEAD_SIZE] = (dkv_ref[:, HEAD_SIZE:] + back[:, HEAD_SIZE:]).astype(bf)
    out_ref[:, 4 * HEAD_SIZE :] = dlogit_ref[...]


def prepare_back(raw, cos, sin, gains, dq, dkv, back, dlogit):
    T, width = raw.shape
    W = 2 * HEAD_SIZE
    blk = lambda w: pl.BlockSpec((BQ, w), lambda i: (i, 0))
    flat = pl.BlockSpec((2, HEAD_SIZE), lambda i: (0, 0))
    return pl.pallas_call(
        prepare_back_body,
        grid=(T // BQ,),
        in_specs=[blk(width), blk(HEAD_SIZE), blk(HEAD_SIZE), flat, blk(W), blk(W), blk(W), blk(HEAD_SIZE)],
        out_specs=[blk(width), flat],
        out_shape=[jax.ShapeDtypeStruct((T, width), bf), jax.ShapeDtypeStruct((2, HEAD_SIZE), f32)],
        cost_estimate=pl.CostEstimate(flops=T * 8000, bytes_accessed=T * 640 * 10, transcendentals=T),
        name="prepare_heads_back",
    )(raw, cos, sin, gains, dq, dkv, back, dlogit)


def gate_back_rows(grad_mixed, attn_ref, logit_ref, ga_ref, dlogit_ref, del_ref):
    lanes = lax.broadcasted_iota(jnp.int32, dlogit_ref.shape, 1)
    grads = jnp.zeros(dlogit_ref.shape, f32)
    for h in range(2):
        cols = slice(h * HEAD_SIZE, (h + 1) * HEAD_SIZE)
        g = jax.nn.sigmoid(logit_ref[:, h : h + 1])
        gm = grad_mixed[:, cols]
        at = attn_ref[:, cols]
        ga = (gm * g).astype(bf)
        ga_ref[:, cols] = ga
        slope = jnp.sum(gm * at, axis=-1, keepdims=True) * (g * (1 - g))
        grads = jnp.where(lanes == h, slope, grads)
        del_ref[h : h + 1, :] = as_rows(jnp.sum(ga.astype(f32) * at, axis=-1, keepdims=True))
    dlogit_ref[...] = grads.astype(bf)


def hidden_back_body(dout_ref, down_ref, both_ref, out_ref):
    units = down_ref.shape[1]
    chunk = 256
    for j in range(units // chunk):
        left = slice(j * chunk, (j + 1) * chunk)
        right = slice(units + j * chunk, units + (j + 1) * chunk)
        grad = dg(dout_ref[...], down_ref[:, left], NN)
        gate = both_ref[:, left]
        s = jax.nn.sigmoid(gate)
        out_ref[:, left] = (grad * both_ref[:, right] * s * (1 + gate * (1 - s))).astype(bf)
        out_ref[:, right] = (grad * (gate * s)).astype(bf)


def hidden_back(dout, down, both):
    T, width = dout.shape
    units = down.shape[1]
    blk = lambda w: pl.BlockSpec((2 * BQ, w), lambda i: (i, 0))
    return pl.pallas_call(
        hidden_back_body,
        grid=(T // (2 * BQ),),
        in_specs=[blk(width), pl.BlockSpec((width, units), lambda i: (0, 0)), blk(2 * units)],
        out_specs=blk(2 * units),
        out_shape=jax.ShapeDtypeStruct((T, 2 * units), bf),
        cost_estimate=pl.CostEstimate(flops=2 * T * width * units, bytes_accessed=T * units * 30, transcendentals=T * units),
        name="hidden_back",
    )(dout, down, both)


GROUP = 4
MESH = pl.DeviceIdType.MESH
QUICK = pl.CostEstimate(flops=0, bytes_accessed=1 << 16, transcendentals=0)

def places():
    dp = lax.axis_index("dp"); c = lax.axis_index("mp")
    t = dp % GROUP
    base = dp - t
    tx = t + 1 - 2 * (t % 2)
    ty = t + 2 - 4 * (t // 2)
    td = 3 - t
    return base, t, tx, ty, td, c

def greet(devices):
    barrier = pltpu.get_barrier_semaphore()
    for device in devices:
        pl.semaphore_signal(barrier, inc=1, device_id=device, device_id_type=MESH)
    pl.semaphore_wait(barrier, len(devices))

def gather_body(x_ref, out_ref, send, recv, local):
    base, t, tx, ty, td, c = places()
    share = x_ref.shape[0]
    half = share // 2
    xdev, ydev, mate = (base + tx, c), (base + ty, c), (base + t, 1 - c)
    greet([xdev, ydev, mate])
    def spot(who, part=None):
        start = (2 * who + c) * share
        if part is None:
            return out_ref.at[pl.ds(pl.multiple_of(start, share), share)]
        return out_ref.at[pl.ds(pl.multiple_of(start + part * half, half), half)]
    def copy(kind, src, dst, device):
        return pltpu.make_async_remote_copy(src_ref=src, dst_ref=dst, send_sem=send.at[kind], recv_sem=recv.at[kind], device_id=device, device_id_type=MESH)
    own = pltpu.make_async_copy(x_ref, spot(t), local)
    own.start()
    mine = [x_ref.at[pl.ds(0, half)], x_ref.at[pl.ds(half, half)]]
    k = {}
    k[2] = copy(2, mine[0], spot(t, 0), ydev); k[2].start()
    k[1] = copy(1, mine[1], spot(t, 1), xdev); k[1].start()
    k[3] = copy(3, mine[1], spot(t, 1), ydev); k[3].start()
    k[0] = copy(0, mine[0], spot(t, 0), xdev); k[0].start()
    k[6] = copy(6, x_ref, spot(t), mate); k[6].start()
    k[2].wait_recv()
    k[4] = copy(4, spot(ty, 0), spot(ty, 0), xdev); k[4].start()
    k[9] = copy(9, spot(ty, 0), spot(ty, 0), mate); k[9].start()
    k[1].wait_recv()
    k[5] = copy(5, spot(tx, 1), spot(tx, 1), ydev); k[5].start()
    k[8] = copy(8, spot(tx, 1), spot(tx, 1), mate); k[8].start()
    k[0].wait_recv()
    k[7] = copy(7, spot(tx, 0), spot(tx, 0), mate); k[7].start()
    k[3].wait_recv()
    k[10] = copy(10, spot(ty, 1), spot(ty, 1), mate); k[10].start()
    k[4].wait_recv()
    k[11] = copy(11, spot(td, 0), spot(td, 0), mate); k[11].start()
    k[5].wait_recv()
    k[12] = copy(12, spot(td, 1), spot(td, 1), mate); k[12].start()
    for kind in range(6, 13):
        k[kind].wait_recv()
    for kind in range(13):
        k[kind].wait_send()
    own.wait()

def gather_group(x):
    share, width = x.shape
    return pl.pallas_call(
        gather_body,
        out_shape=jax.ShapeDtypeStruct((share * GROUP * 2, width), x.dtype),
        in_specs=[pl.BlockSpec(memory_space=pltpu.VMEM)],
        out_specs=pl.BlockSpec(memory_space=pl.ANY),
        scratch_shapes=[pltpu.SemaphoreType.DMA((13,)), pltpu.SemaphoreType.DMA((13,)), pltpu.SemaphoreType.DMA],
        compiler_params=pltpu.CompilerParams(collective_id=1, has_side_effects=True),
        cost_estimate=QUICK,
        name="gather_group",
    )(x)

def reduce_body(side, back, left_ref, right_ref, *refs):
    if side:
        tall_ref, out_ref, grad_ref, tall, grad, refs = *refs[:5], refs[5:]
    elif back:
        pair_ref, out_ref, pair_out, refs = *refs[:3], refs[3:]
    else:
        out_ref, refs = refs[0], refs[1:]
    left, right, fars, near, mates, sums, xin, yin, zin, turned, fetch, send, recv = refs
    base, t, tx, ty, td, c = places()
    share = out_ref.shape[0]
    half = share // 2
    chunk = right.shape[0] // 4
    xdev, ydev, mate = (base + tx, c), (base + ty, c), (base + t, 1 - c)
    order = [td, tx, ty, t]
    lefts, rights, talls = [], [], []
    for i, who in enumerate(order):
        for j, core in enumerate((1 - c, c)):
            rows = pl.ds(pl.multiple_of((2 * who + core) * share, share), share)
            n = 2 * i + j
            place = pl.ds(n * share, share)
            lefts.append(pltpu.make_async_copy(left_ref.at[rows], left.at[place], fetch.at[n]))
            if side:
                talls.append(pltpu.make_async_copy(tall_ref.at[rows], tall.at[place], fetch.at[12 + n]))
    for j in range(4):
        rows = pl.ds(j * chunk, chunk)
        rights.append(pltpu.make_async_copy(right_ref.at[rows], right.at[rows], fetch.at[8 + j]))
    for one in lefts[:2] + rights + lefts[2:] + talls:
        one.start()
    friends = [xdev, ydev, mate]
    if back:
        late = lax.axis_index("dp") // GROUP % 2
        friends.append((lax.axis_index("dp") + (GROUP - 2 * GROUP * late), c))
    greet(friends)
    if back:
        pair = pltpu.make_async_remote_copy(
            src_ref=pair_ref,
            dst_ref=pair_out,
            send_sem=send.at[10],
            recv_sem=recv.at[10],
            device_id=friends[-1],
            device_id_type=MESH,
        )
        keep = pltpu.make_async_copy(pair_ref, pair_out, fetch.at[12])

        @pl.when(late == 1)
        def _():
            pair.start()
            keep.start()

    def copy(kind, src, dst, device):
        return pltpu.make_async_remote_copy(
            src_ref=src, dst_ref=dst, send_sem=send.at[kind], recv_sem=recv.at[kind], device_id=device, device_id_type=MESH
        )

    def product(n, dst):
        lefts[n].wait()

        def go(j, _):
            rows = pl.ds(pl.multiple_of(j * chunk, chunk), chunk)
            dst[:, rows] = dg(left[n * share : (n + 1) * share, :], right[rows, :], NT).astype(dst.dtype)
            return 0

        if n == 0:
            for j in range(4):
                rights[j].wait()
                go(j, 0)
        else:
            lax.fori_loop(0, 4, go, 0)

    def add(dst, one, two):
        step = 16

        def go(i, _):
            rows = pl.ds(pl.multiple_of(i * step, step), step)
            dst[rows, :] = (one[rows, :].astype(f32) + two[rows, :].astype(f32)).astype(dst.dtype)
            return 0

        lax.fori_loop(0, dst.shape[0] // step, go, 0)

    A, B = pl.ds(0, half), pl.ds(half, half)
    over, k = [], {}

    def join(i):
        over[i].wait_recv()
        add(sums.at[i], near.at[i], mates.at[i])
        if i == 0:
            k[4] = copy(4, sums.at[0, A], xin.at[1], xdev)
            k[5] = copy(5, sums.at[0, B], yin.at[1], ydev)
            k[4].start()
            k[5].start()
        if i == 1:
            k[6] = copy(6, sums.at[1, A], xin.at[0], xdev)
            k[6].start()
        if i == 2:
            k[7] = copy(7, sums.at[2, B], yin.at[0], ydev)
            k[7].start()

    for i in range(4):
        product(2 * i, fars.at[i])
        over.append(copy(i, fars.at[i], mates.at[i], mate))
        over[i].start()
        product(2 * i + 1, near.at[i])
        if i:
            join(i - 1)
    join(3)
    k[4].wait_recv()
    add(turned.at[0], sums.at[2, A], xin.at[1])
    k[8] = copy(8, turned.at[0], zin.at[0], ydev)
    k[8].start()
    k[5].wait_recv()
    add(turned.at[1], sums.at[1, B], yin.at[1])
    k[9] = copy(9, turned.at[1], zin.at[1], xdev)
    k[9].start()
    if side:
        for one in talls:
            one.wait()

        def inner_product(j, _):
            cols = pl.ds(pl.multiple_of(j * 256, 256), 256)
            grad[cols, :] = dg(tall[:, cols], left[...], TN).astype(bf)
            return 0

        lax.fori_loop(0, tall.shape[1] // 256, inner_product, 0)
        put = pltpu.make_async_copy(grad, grad_ref, fetch.at[20])
        put.start()
    k[6].wait_recv()
    add(out_ref.at[A], sums.at[3, A], xin.at[0])
    k[7].wait_recv()
    add(out_ref.at[B], sums.at[3, B], yin.at[0])
    k[8].wait_recv()
    add(out_ref.at[A], out_ref.at[A], zin.at[0])
    k[9].wait_recv()
    add(out_ref.at[B], out_ref.at[B], zin.at[1])
    for i in range(4):
        over[i].wait_send()
    for kind in range(4, 10):
        k[kind].wait_send()
    if side:
        put.wait()
    if back:

        @pl.when(late == 1)
        def _():
            pair.wait_send()
            keep.wait()

        @pl.when(late == 0)
        def _():
            pair.wait_recv()


def product_reduce(left, right, key, tall=None, pair=None):
    rows, depth = left.shape
    side = tall is not None
    back = pair is not None
    width = right.shape[0]
    share = rows // (2 * GROUP)
    half = share // 2
    block = lambda n, r: pltpu.VMEM((n, r, width), bf)
    anywhere = pl.BlockSpec(memory_space=pl.ANY)
    outs, out_specs = [jax.ShapeDtypeStruct((share, width), f32)], [pl.BlockSpec(memory_space=pltpu.VMEM)]
    ins, extra = [left, right], []
    if side:
        ins.append(tall)
        outs.append(jax.ShapeDtypeStruct((tall.shape[1], depth), bf))
        out_specs.append(anywhere)
        extra = [pltpu.VMEM(tall.shape, bf), pltpu.VMEM((tall.shape[1], depth), bf)]
    in_specs = [anywhere] * len(ins)
    if back:
        ins.append(pair)
        in_specs.append(pl.BlockSpec(memory_space=pltpu.VMEM))
        outs.append(jax.ShapeDtypeStruct(pair.shape, bf))
        out_specs.append(anywhere)
    result = pl.pallas_call(
        partial(reduce_body, side, back),
        out_shape=outs,
        in_specs=in_specs,
        out_specs=out_specs,
        scratch_shapes=extra
        + [
            pltpu.VMEM((rows, depth), bf),
            pltpu.VMEM((width, depth), bf),
            block(4, share),
            block(4, share),
            block(4, share),
            block(4, share),
            block(2, half),
            block(2, half),
            block(2, half),
            block(2, half),
            pltpu.SemaphoreType.DMA((21,)),
            pltpu.SemaphoreType.DMA((11,)),
            pltpu.SemaphoreType.DMA((11,)),
        ],
        compiler_params=pltpu.CompilerParams(collective_id=key, has_side_effects=True, vmem_limit_bytes=60 << 20),
        cost_estimate=QUICK,
        name="product_reduce",
    )(*ins)
    return result if side or back else result[0]


def gather_product_body(glu, x_ref, w_ref, *refs):
    if glu:
        full_ref, y_ref, hidden_ref, hs, ys, refs = *refs[:5], refs[5:]
    else:
        attn_ref, raw_ref, full_ref, ga_ref, dlogit_ref, del_ref, attn, logit, gs, ds, es, refs = *refs[:11], refs[11:]
    buf, w, fetch, put_x, put_y, send, recv = refs
    base, t, tx, ty, td, c = places()
    share = x_ref.shape[0]
    half = share // 2
    width = w.shape[1]
    xdev, ydev, mate = (base + tx, c), (base + ty, c), (base + t, 1 - c)
    weights = [pltpu.make_async_copy(w_ref, w, fetch.at[0])]
    if not glu:
        edge = raw_ref.shape[1] - HEAD_SIZE
        weights.append(pltpu.make_async_copy(attn_ref, attn, fetch.at[1]))
        weights.append(pltpu.make_async_copy(raw_ref.at[:, pl.ds(edge, HEAD_SIZE)], logit, fetch.at[2]))
    for one in weights:
        one.start()
    greet([xdev, ydev, mate])

    def unit(who, core):
        return pl.ds(pl.multiple_of((2 * who + core) * share, share), share)

    def spot(who, part):
        start = (2 * who + c) * share + part * half
        return buf.at[pl.ds(pl.multiple_of(start, half), half)]

    def copy(kind, src, dst, device):
        one = pltpu.make_async_remote_copy(
            src_ref=src, dst_ref=dst, send_sem=send.at[kind], recv_sem=recv.at[kind], device_id=device, device_id_type=MESH
        )
        one.start()
        return one

    mine = [x_ref.at[pl.ds(0, half)], x_ref.at[pl.ds(half, half)]]
    k, puts = {}, []
    k[2] = copy(2, mine[0], spot(t, 0), ydev)
    k[1] = copy(1, mine[1], spot(t, 1), xdev)
    k[3] = copy(3, mine[1], spot(t, 1), ydev)
    k[0] = copy(0, mine[0], spot(t, 0), xdev)
    k[6] = copy(6, x_ref, buf.at[unit(t, c)], mate)
    for one in weights:
        one.wait()

    def work(n, src, who, core):
        rows = unit(who, core)
        slot = n % 2
        one = pltpu.make_async_copy(src, full_ref.at[rows], put_x.at[n])
        one.start()
        if n >= 2:
            for old in puts[n - 2][1:]:
                old.wait()
        if glu:
            chunk = 256

            def go(j, _):
                left = pl.ds(pl.multiple_of(j * chunk, chunk), chunk)
                right = pl.ds(pl.multiple_of(width // 2 + j * chunk, chunk), chunk)
                gate = dg(src[...], w[:, left], NN)
                up = dg(src[...], w[:, right], NN)
                ys[slot, :, left] = gate
                ys[slot, :, right] = up
                hs[slot, :, left] = (gate * jax.nn.sigmoid(gate) * up).astype(bf)
                return 0

            lax.fori_loop(0, width // 2 // chunk, go, 0)
            outs = [
                one,
                pltpu.make_async_copy(ys.at[slot], y_ref.at[rows], put_y.at[n]),
                pltpu.make_async_copy(hs.at[slot], hidden_ref.at[rows], put_y.at[8 + n]),
            ]
        else:
            gm = dg(src[...], w[...], NN)
            gate_back_rows(gm, attn.at[rows], logit.at[rows], gs.at[slot], ds.at[slot], es.at[slot])
            outs = [
                one,
                pltpu.make_async_copy(gs.at[slot], ga_ref.at[rows], put_y.at[n]),
                pltpu.make_async_copy(ds.at[slot], dlogit_ref.at[rows], put_y.at[8 + n]),
                pltpu.make_async_copy(es.at[slot], del_ref.at[:, rows], put_y.at[16 + n]),
            ]
        for out in outs[1:]:
            out.start()
        puts.append(outs)

    def landed(who, core):
        return buf.at[unit(who, core)]

    work(0, x_ref, t, c)
    k[6].wait_recv()
    work(1, landed(t, 1 - c), t, 1 - c)
    k[2].wait_recv()
    k[4] = copy(4, spot(ty, 0), spot(ty, 0), xdev)
    k[9] = copy(9, spot(ty, 0), spot(ty, 0), mate)
    k[1].wait_recv()
    k[5] = copy(5, spot(tx, 1), spot(tx, 1), ydev)
    k[8] = copy(8, spot(tx, 1), spot(tx, 1), mate)
    k[0].wait_recv()
    k[7] = copy(7, spot(tx, 0), spot(tx, 0), mate)
    k[3].wait_recv()
    k[10] = copy(10, spot(ty, 1), spot(ty, 1), mate)
    work(2, landed(tx, c), tx, c)
    work(3, landed(ty, c), ty, c)
    k[7].wait_recv()
    k[8].wait_recv()
    work(4, landed(tx, 1 - c), tx, 1 - c)
    k[9].wait_recv()
    k[10].wait_recv()
    work(5, landed(ty, 1 - c), ty, 1 - c)
    k[4].wait_recv()
    k[11] = copy(11, spot(td, 0), spot(td, 0), mate)
    k[5].wait_recv()
    k[12] = copy(12, spot(td, 1), spot(td, 1), mate)
    work(6, landed(td, c), td, c)
    k[11].wait_recv()
    k[12].wait_recv()
    work(7, landed(td, 1 - c), td, 1 - c)
    for kind in range(13):
        k[kind].wait_send()
    for n, outs in enumerate(puts):
        outs[0].wait()
        if n >= 6:
            for out in outs[1:]:
                out.wait()


def gather_product(x, w, key, gated=None):
    share, depth = x.shape
    width = w.shape[1]
    rows = share * GROUP * 2
    anywhere = pl.BlockSpec(memory_space=pl.ANY)
    shape = jax.ShapeDtypeStruct
    if gated is None:
        gated = []
        outs = [shape((rows, width), f32), shape((rows, width // 2), bf)]
        extra = [pltpu.VMEM((2, share, width // 2), bf), pltpu.VMEM((2, share, width), f32)]
    else:
        outs = [shape((rows, width), bf), shape((rows, HEAD_SIZE), bf), shape((2, rows), f32)]
        extra = [
            pltpu.VMEM((rows, width), f32),
            pltpu.VMEM((rows, HEAD_SIZE), f32),
            pltpu.VMEM((2, share, width), bf),
            pltpu.VMEM((2, share, HEAD_SIZE), bf),
            pltpu.VMEM((2, 2, share), f32),
        ]
    outs = [shape((rows, depth), bf)] + outs
    return pl.pallas_call(
        partial(gather_product_body, not gated),
        out_shape=outs,
        in_specs=[pl.BlockSpec(memory_space=pltpu.VMEM)] + [anywhere] * (1 + len(gated)),
        out_specs=[anywhere] * len(outs),
        scratch_shapes=extra
        + [
            pltpu.VMEM((rows, depth), bf),
            pltpu.VMEM((depth, width), bf),
            pltpu.SemaphoreType.DMA((3,)),
            pltpu.SemaphoreType.DMA((8,)),
            pltpu.SemaphoreType.DMA((24,)),
            pltpu.SemaphoreType.DMA((13,)),
            pltpu.SemaphoreType.DMA((13,)),
        ],
        compiler_params=pltpu.CompilerParams(collective_id=key, has_side_effects=True, vmem_limit_bytes=48 << 20),
        cost_estimate=QUICK,
        name="gather_product",
    )(x, w, *gated)


def far_places():
    dp = lax.axis_index("dp")
    return dp // GROUP, lax.axis_size("dp") // GROUP


def far_friends():
    base, t, tx, ty, td, c = places()
    r, count = far_places()
    return [((r + i) % count * GROUP + t, c) for i in range(1, count)] + [(base + t, 1 - c)]


def small_copy(send, recv):
    def copy(kind, src, dst, device):
        one = pltpu.make_async_remote_copy(
            src_ref=src, dst_ref=dst, send_sem=send.at[kind], recv_sem=recv.at[kind], device_id=device, device_id_type=MESH
        )
        one.start()
        return one

    return copy


def spread(x_ref, out_ref, send, recv, local):
    base, t, tx, ty, td, c = places()
    r, count = far_places()
    copy = small_copy(send, recv)
    own = pltpu.make_async_copy(x_ref, out_ref.at[c, t, r], local)
    own.start()
    others = [(r + i) % count for i in range(1, count)]
    stage = [copy(i, x_ref, out_ref.at[c, t, r], (z * GROUP + t, c)) for i, z in enumerate(others)]
    own.wait()
    for one in stage:
        one.wait()
    stage = [copy(count - 1 + i, out_ref.at[c, t], out_ref.at[c, t], (base + who, c)) for i, who in enumerate([td, tx, ty])]
    yield
    for one in stage:
        one.wait()
    copy(count + 2, out_ref.at[c], out_ref.at[c], (base + t, 1 - c)).wait()
    yield


def collect(x_ref, out_ref, one_in, one_sum, two_in, two_sum, far_in, send, recv):
    base, t, tx, ty, td, c = places()
    r, count = far_places()
    copy = small_copy(send, recv)
    copy(0, x_ref.at[1 - c], one_in, (base + t, 1 - c)).wait()
    one_sum[...] = x_ref[c] + one_in[...]
    stage = [copy(1 + i, one_sum.at[who], two_in.at[i], (base + who, c)) for i, who in enumerate([td, tx, ty])]
    yield
    for one in stage:
        one.wait()
    two_sum[...] = one_sum[t] + two_in[0] + two_in[1] + two_in[2]
    others = [(r + i) % count for i in range(1, count)]
    stage = [copy(4 + i, two_sum.at[z], far_in.at[i], (z * GROUP + t, c)) for i, z in enumerate(others)]
    for one in stage:
        one.wait()
    total = two_sum[r]
    for i in range(count - 1):
        total = total + far_in[i]
    out_ref[...] = total
    yield


def small_scratch(tile, inward):
    count = lax.axis_size("dp") // GROUP
    sems = [pltpu.SemaphoreType.DMA((count + 3,)), pltpu.SemaphoreType.DMA((count + 3,))]
    if inward:
        return sems + [pltpu.SemaphoreType.DMA]
    shapes = [(GROUP, count), (GROUP, count), (3, count), (count,), (count - 1,)]
    return [pltpu.VMEM(shape + tile, f32) for shape in shapes] + sems


def trade_body(inward, widths, sender, side, small, *refs):
    base, t, tx, ty, td, c = places()
    partners = [td, tx, ty]
    friends = [(base + who, c) for who in partners]
    flat = [(i, sum(ws[:j]), w) for i, ws in enumerate(widths) for j, w in enumerate(ws)]
    count = len(flat)
    packed, loose = len(widths), count
    ins, refs = refs[: loose if inward else packed], refs[loose if inward else packed :]
    if sender is not None:
        pair_ref, refs = refs[0], refs[1:]
    if side:
        tall_ref, wide_ref, refs = *refs[:2], refs[2:]
    if small:
        small_ref, refs = refs[0], refs[1:]
    outs, refs = refs[: packed if inward else loose], refs[packed if inward else loose :]
    if sender is not None:
        pair_out, refs = refs[0], refs[1:]
    if side:
        grad_ref, refs = refs[0], refs[1:]
    if small:
        small_out, refs = refs[0], refs[1:]
    if side:
        tall, wide, grad, fetch, refs = *refs[:4], refs[4:]
    send, recv, local, *rest = refs
    if small:
        friends += far_friends()
    if sender is not None:
        late = lax.axis_index("dp") // GROUP % 2
        friends.append((lax.axis_index("dp") + (GROUP - 2 * GROUP * late), c))
    greet(friends)

    def block(ref, i, who):
        array, start, width = flat[i]
        return ref[array].at[who, :, pl.ds(start, width)]

    def column(ref, i, who):
        width = flat[i][2]
        return ref[i].at[:, pl.ds(pl.multiple_of(who * width, width), width)]

    if small:
        steps = (spread if inward else collect)(small_ref, small_out, *rest)
        next(steps)
    source, target = (column, block) if inward else (block, column)
    copies = []
    for j, who in enumerate(partners):
        for i in range(count):
            kind = j * count + i
            one = pltpu.make_async_remote_copy(
                src_ref=source(ins, i, who),
                dst_ref=target(outs, i, t),
                send_sem=send.at[kind],
                recv_sem=recv.at[kind],
                device_id=(base + who, c),
                device_id_type=MESH,
            )
            one.start()
            copies.append(one)
    if sender is not None:
        pair = pltpu.make_async_remote_copy(
            src_ref=pair_ref,
            dst_ref=pair_out,
            send_sem=send.at[3 * count],
            recv_sem=recv.at[3 * count],
            device_id=friends[-1],
            device_id_type=MESH,
        )
        keep = pltpu.make_async_copy(pair_ref, pair_out, local.at[count])

        @pl.when(late == sender)
        def _():
            pair.start()
            keep.start()

    owns = [pltpu.make_async_copy(source(ins, i, t), target(outs, i, t), local.at[i]) for i in range(count)]
    for own in owns:
        own.start()
    if side:
        loads = [pltpu.make_async_copy(tall_ref, tall, fetch.at[0]), pltpu.make_async_copy(wide_ref, wide, fetch.at[1])]
        for one in loads:
            one.start()
        for one in loads:
            one.wait()

        def inner_product(j, _):
            cols = pl.ds(pl.multiple_of(j * 256, 256), 256)
            grad[cols, :] = dg(tall[:, cols], wide[...], TN).astype(bf)
            return 0

        lax.fori_loop(0, tall.shape[1] // 256, inner_product, 0)
        put = pltpu.make_async_copy(grad, grad_ref, fetch.at[2])
        put.start()
    if small:
        next(steps)
    for one in copies:
        one.wait()
    for own in owns:
        own.wait()
    if side:
        put.wait()
    if sender is not None:

        @pl.when(late == sender)
        def _():
            pair.wait_send()
            keep.wait()

        @pl.when(late == 1 - sender)
        def _():
            pair.wait_recv()


def trade_call(inward, ins, outs, widths, key, pair=None, sender=None, side=(), small=None):
    vmem = pl.BlockSpec(memory_space=pltpu.VMEM)
    anywhere = pl.BlockSpec(memory_space=pl.ANY)
    count = sum(len(ws) for ws in widths)
    scratch = []
    if sender is not None:
        ins = list(ins) + [pair]
        outs = outs + [jax.ShapeDtypeStruct(pair.shape, bf)]
    if side:
        tall, wide = side
        grad = (tall.shape[1], wide.shape[1])
        outs = outs + [jax.ShapeDtypeStruct(grad, bf)]
        scratch = [pltpu.VMEM(tall.shape, bf), pltpu.VMEM(wide.shape, bf), pltpu.VMEM(grad, bf), pltpu.SemaphoreType.DMA((3,))]
    smalls = [] if small is None else [small]
    out_specs = [anywhere] * len(outs) + [vmem] * len(smalls)
    rest = []
    if smalls:
        tile = small.shape[-2:]
        result = (2, GROUP, lax.axis_size("dp") // GROUP) + tile if inward else tile
        outs = outs + [jax.ShapeDtypeStruct(result, f32)]
        rest = small_scratch(tile, inward)
    return pl.pallas_call(
        partial(trade_body, inward, widths, sender, bool(side), bool(smalls)),
        out_shape=outs,
        in_specs=[vmem] * len(ins) + [anywhere] * len(side) + [vmem] * len(smalls),
        out_specs=out_specs,
        scratch_shapes=scratch
        + [
            pltpu.SemaphoreType.DMA((3 * count + 1,)),
            pltpu.SemaphoreType.DMA((3 * count + 1,)),
            pltpu.SemaphoreType.DMA((count + 1,)),
        ]
        + rest,
        compiler_params=pltpu.CompilerParams(collective_id=key, has_side_effects=True),
        cost_estimate=QUICK,
        name="trade_group",
    )(*ins, *side, *smalls)


def trade_group(weights, key, pair=None, small=None):
    rows = weights[0].shape[0]
    widths = (tuple(w.shape[1] // GROUP for w in weights),)
    outs = [jax.ShapeDtypeStruct((GROUP, rows, sum(widths[0])), bf)]
    if pair is None:
        result = trade_call(True, weights, outs, widths, key, small=small)
        return result[0] if small is None else result
    return trade_call(True, weights, outs, widths, key, pair, 0)


def trade_back(grads, widths, key, pair=None, side=(), small=None):
    rows = grads[0].shape[1]
    outs = [jax.ShapeDtypeStruct((rows, GROUP * w), bf) for ws in widths for w in ws]
    return trade_call(False, grads, outs, widths, key, pair, None if pair is None else 1, side, small)


def row_norm(values, gain):
    scale = lax.rsqrt(jnp.mean(values * values, axis=-1, keepdims=True) + EPS)
    return values * scale * gain


def rope_tables(positions, width):
    half = width // 2
    lanes = jnp.arange(width, dtype=jnp.int32)
    freqs = THETA ** (-((lanes % half).astype(f32) / half))
    angle = positions.astype(f32) * freqs[None, :]
    return jnp.cos(angle), jnp.sin(angle) * jnp.where(lanes < half, -1.0, 1.0)[None, :]


def tables_body(group_tokens, early, seg_count, parents, lengths, pos_ref, qcol_ref, qline_ref, kline_ref, kcol_ref, flags, key_any):
    step = pl.program_id(0)
    first = lax.axis_index("dp") // GROUP * group_tokens
    tree = first // TREE_TOKENS
    begin = first - tree * TREE_TOKENS
    size = [lengths[tree, seg] for seg in range(seg_count)]
    starts, bits, depth = [jnp.int32(0)], [jnp.int32(1)], [jnp.int32(0)]
    for seg in range(1, seg_count):
        starts.append(starts[-1] + size[seg - 1])
        parent = parents[tree, seg]
        above, deep = bits[0], depth[0] + size[0]
        for p in range(1, seg):
            above = jnp.where(parent == p, bits[p], above)
            deep = jnp.where(parent == p, depth[p] + size[p], deep)
        bits.append(above | (1 << seg))
        depth.append(deep)
    powers = [jnp.int32(1 << seg) for seg in range(seg_count)]

    def by_segment(offsets, values):
        out = jnp.zeros_like(offsets) + values[0]
        for start, value in zip(starts[1:], values[1:]):
            out = jnp.where(offsets >= start, value, out)
        return out

    q_first = begin + step * BQ
    k_first = begin - early + step * BK
    column = lax.broadcasted_iota(jnp.int32, (BQ, 1), 0) + q_first
    pos_ref[...] = by_segment(column, [d - s for d, s in zip(depth, starts)]) + column
    qcol_ref[...] = by_segment(column, bits)
    qline_ref[...] = by_segment(lax.broadcasted_iota(jnp.int32, (1, BQ), 1) + q_first, bits)
    column = lax.broadcasted_iota(jnp.int32, (BK, 1), 0) + k_first
    kcol_ref[...] = jnp.where(column >= 0, by_segment(column, powers), 0)
    line = lax.broadcasted_iota(jnp.int32, (1, BK), 1) + k_first
    kline_ref[0] = jnp.where(line >= 0, by_segment(line, powers), 0)

    def touches(begins, seg, span):
        return (starts[seg] <= begins + span - 1) & (starts[seg] + size[seg] > begins)

    @pl.when(step == 0)
    def _():
        for k in range(key_any.shape[0]):
            seen = jnp.int32(0)
            for seg in range(seg_count):
                seen = jnp.where(touches(begin - early + k * BK, seg, BK), seen | powers[seg], seen)
            key_any[k] = seen

    query_any, query_all = jnp.int32(0), jnp.int32(-1)
    for seg in range(seg_count):
        inside = touches(q_first, seg, BQ)
        query_any = jnp.where(inside, query_any | bits[seg], query_any)
        query_all = jnp.where(inside, query_all & bits[seg], query_all)
    for k in range(key_any.shape[0]):
        keys_at = begin - early + k * BK
        some = ((query_any & key_any[k]) != 0) & (keys_at <= q_first + BQ - 1)
        every = ((key_any[k] & ~query_all) == 0) & (keys_at + BK - 1 <= q_first)
        flags[step, k] = jnp.where(some, jnp.where(every, 2, 1), 0)


def tables(parents, lengths, group_tokens, planes):
    seg_count = parents.shape[1]
    early = (planes - 1) * group_tokens
    steps = group_tokens // BQ
    blocks = planes * group_tokens // BK
    i32 = lambda *shape: jax.ShapeDtypeStruct(shape, jnp.int32)
    smem = pl.BlockSpec(memory_space=pltpu.SMEM)
    return pl.pallas_call(
        partial(tables_body, group_tokens, early, seg_count),
        grid=(steps,),
        in_specs=[smem, smem],
        out_specs=[
            pl.BlockSpec((BQ, 1), lambda i: (i, 0)),
            pl.BlockSpec((BQ, 1), lambda i: (i, 0)),
            pl.BlockSpec((1, BQ), lambda i: (0, i)),
            pl.BlockSpec((1, 1, BK), lambda i: (i, 0, 0)),
            pl.BlockSpec((BK, 1), lambda i: (i, 0)),
            smem,
        ],
        out_shape=[
            i32(group_tokens, 1),
            i32(group_tokens, 1),
            i32(1, group_tokens),
            i32(blocks, 1, BK),
            i32(blocks * BK, 1),
            i32(steps, blocks),
        ],
        scratch_shapes=[pltpu.SMEM((blocks,), jnp.int32)],
        cost_estimate=QUICK,
        name="tables",
    )(parents, lengths)


def inner(left, right):
    return dg(left, right, TN)


def after(value, *others):
    return lax.optimization_barrier((value,) + others)[0]


def per_device(
    layer_in,
    out_grad,
    parents,
    lengths,
    attn_gain,
    mlp_gain,
    query_norm_gain,
    key_gain,
    query_weight,
    key_matrix,
    value_matrix,
    headgate_weight,
    output_weight,
    gate_weight,
    up_weight,
    down_weight,
):
    data_count = lax.axis_size("dp")
    model_count = lax.axis_size("mp")
    share, width = layer_in.shape
    rows_here = query_weight.shape[0]
    group_tokens = share * model_count * GROUP
    seg_count = parents.shape[1]
    far = [[member + GROUP * plane for plane in range(data_count // GROUP)] for member in range(GROUP)]
    planes = TREE_TOKENS // group_tokens

    gates = headgate_weight.shape[1] // GROUP
    pieces_gates = jnp.pad(
        headgate_weight.reshape(rows_here, GROUP, gates), ((0, 0), (0, 0), (0, HEAD_SIZE - gates))
    ).reshape(rows_here, GROUP * HEAD_SIZE)

    def far_gather(mine):
        return lax.all_gather(
            mine.reshape(GROUP * rows_here, -1), "dp", axis=0, tiled=True, axis_index_groups=far
        )

    def far_scatter(grad):
        mine = lax.psum_scatter(grad, "dp", scatter_dimension=0, tiled=True, axis_index_groups=far)
        return mine.reshape(GROUP, rows_here, -1)

    sizes = [attn_gain.shape[0], mlp_gain.shape[0], query_norm_gain.shape[0], key_gain.shape[0]]
    cuts = [sum(sizes[:i]) for i in range(5)]
    tile = (8, 128)
    spare = tile[0] * tile[1] - cuts[4]
    gain_tile = jnp.pad(
        jnp.concatenate([attn_gain, mlp_gain, query_norm_gain, key_gain]).astype(f32), (0, spare)
    ).reshape(tile)
    mine_attn, all_gains = trade_group([query_weight, key_matrix, value_matrix, pieces_gates], 3, small=gain_tile)
    full_attn = far_gather(mine_attn)
    gains = all_gains.transpose(2, 1, 0, 3, 4).reshape(data_count * model_count, -1)
    gain_one, gain_two, gain_query, gain_key = [
        gains[:, cuts[i] : cuts[i + 1]].reshape(-1) for i in range(4)
    ]
    head_gains = jnp.stack([gain_query, gain_key])
    mine_out = trade_group([after(output_weight.T, all_gains)], 4)
    full_out = far_gather(mine_out)

    positions, query_column, query_line, key_lines, key_column, flags = tables(parents, lengths, group_tokens, planes)
    cosine, sine = rope_tables(positions, HEAD_SIZE)
    early = (planes - 1) * group_tokens
    key_cut = early // BK

    rows = layer_in.astype(f32)
    normed_one, norm_one_back = jax.vjp(row_norm, rows, gain_one)
    hidden_first = gather_group(after(normed_one.astype(bf), mine_out))
    raw = jnp.dot(hidden_first, full_attn, preferred_element_type=f32)
    q_width = query_weight.shape[1] // GROUP
    k_width = key_matrix.shape[1] // GROUP
    heads = q_width // HEAD_SIZE
    query, pair = prepare(raw, cosine, sine, head_gains)
    mine_glu, pair_early = trade_group([gate_weight, up_weight], 5, pair)
    full_glu = far_gather(mine_glu)
    query = after(query, mine_glu)
    own = attend(True, flags[:, key_cut:], query, pair, query_column, key_lines[key_cut:])
    mine_down = trade_group([after(down_weight.T, own[0])], 6)
    full_down = far_gather(mine_down)
    grad_tokens = gather_group(after(out_grad, mine_down))
    attn, mixed, lse = attend(
        False, flags[:, :key_cut], after(query, grad_tokens), pair_early, query_column, key_lines[:key_cut], (own[0], own[1], raw)
    )
    branch = product_reduce(mixed, full_out, 2)
    middle = rows + branch

    normed_two, norm_two_back = jax.vjp(row_norm, middle, gain_two)
    h_two, both_glu, hidden = gather_product(normed_two.astype(bf), full_glu, 14)
    units = full_down.shape[1]

    grad_glu = hidden_back(grad_tokens, full_down, both_glu)
    down_part = inner(after(grad_tokens, grad_glu), hidden).astype(bf)
    down_rows = far_scatter(down_part)
    grad_h_two, glu_part = product_reduce(after(grad_glu, down_part), full_glu, 15, h_two)
    glu_rows = far_scatter(glu_part)
    grad_mid_norm, gain_two_grad = norm_two_back(grad_h_two)
    grad_middle = out_grad.astype(f32) + grad_mid_norm

    grad_branch, grad_attn, grad_logit, delta = gather_product(grad_middle.astype(bf), full_out, 16, [attn, raw])
    query_grad, early_grad = attend_back(
        False, flags[:, :key_cut], query, grad_attn, pair_early, query_line, key_column[:early], lse, delta
    )
    query_grad, own_grad = attend_back(
        True, flags[:, key_cut:], query, grad_attn, pair, query_line, key_column[early:], lse, delta, query_grad
    )
    down_grad, out_part = trade_back([after(down_rows, own_grad)], ((units,),), 7, side=(grad_branch, mixed))
    out_rows = far_scatter(out_part)
    last_branch, returned = product_reduce(after(hidden, out_part), full_down, 18, pair=early_grad)
    layer_out = (middle + last_branch).astype(bf)
    grad_raw, head_gain_grads = prepare_back(raw, cosine, sine, head_gains, query_grad, own_grad, returned, grad_logit)
    grad_h_one, attn_part = product_reduce(grad_raw, full_attn, 17, hidden_first)
    attn_rows = far_scatter(attn_part)
    grad_in_norm, gain_one_grad = norm_one_back(grad_h_one)
    input_grad = (grad_middle + grad_in_norm).astype(bf)

    devices = data_count * model_count
    gain_parts = jnp.concatenate(
        [
            piece.reshape(devices, -1)
            for piece in (gain_one_grad, gain_two_grad, head_gain_grads[0], head_gain_grads[1], jnp.zeros((devices, spare), f32))
        ],
        axis=1,
    )
    gain_parts = gain_parts.reshape((data_count // GROUP, GROUP, model_count) + tile).transpose(2, 1, 0, 3, 4)
    gate_grad, up_grad, out_weight_grad, gain_sums = trade_back(
        [after(glu_rows, grad_h_one), out_rows], ((units, units), (q_width,)), 8, small=gain_parts
    )
    gain_sums = gain_sums.reshape(-1)
    q_grad, k_grad, v_grad, gates_grad = trade_back(
        [after(attn_rows, gain_sums)], ((q_width, k_width, k_width, HEAD_SIZE),), 10
    )
    gates_grad = gates_grad.reshape(rows_here, GROUP, HEAD_SIZE)[:, :, :heads].reshape(rows_here, -1)
    return (
        layer_out,
        input_grad,
        gain_sums[cuts[0] : cuts[1]],
        gain_sums[cuts[1] : cuts[2]],
        gain_sums[cuts[2] : cuts[3]],
        gain_sums[cuts[3] : cuts[4]],
        q_grad.astype(f32),
        k_grad.astype(f32),
        v_grad.astype(f32),
        gates_grad.astype(f32),
        out_weight_grad.astype(f32).T,
        gate_grad.astype(f32),
        up_grad.astype(f32),
        down_grad.astype(f32).T,
    )


def solution(mesh):
    in_specs = (
        P(("dp", "mp"), None),
        P(("dp", "mp"), None),
        P(),
        P(),
        P(("dp", "mp")),
        P(("dp", "mp")),
        P(("dp", "mp")),
        P(("dp", "mp")),
        P("dp", "mp"),
        P("dp", "mp"),
        P("dp", "mp"),
        P("dp", "mp"),
        P("mp", "dp"),
        P("dp", "mp"),
        P("dp", "mp"),
        P("mp", "dp"),
    )
    out_specs = (
        P(("dp", "mp"), None),
        P(("dp", "mp"), None),
        P(("dp", "mp")),
        P(("dp", "mp")),
        P(("dp", "mp")),
        P(("dp", "mp")),
        P("dp", "mp"),
        P("dp", "mp"),
        P("dp", "mp"),
        P("dp", "mp"),
        P("mp", "dp"),
        P("dp", "mp"),
        P("dp", "mp"),
        P("mp", "dp"),
    )
    return jax.shard_map(
        per_device, mesh=mesh, in_specs=in_specs, out_specs=out_specs, check_vma=False
    )
```

```python
from functools import partial

import jax
import jax.numpy as jnp
from jax import lax
from jax.experimental import pallas as pl
from jax.experimental.pallas import tpu as pltpu
from jax.sharding import PartitionSpec as P

HEAD_SIZE = 128
TREE_TOKENS = 4096
EPS = 1e-06
THETA = 1000000.0
f32 = jnp.float32
bf = jnp.bfloat16

LOG2E = 1.4426950408889634
SCORE_SCALE = HEAD_SIZE ** (-0.5)
BQ = 256
BK = 512
NT = (((1,), (1,)), ((), ()))
NN = (((1,), (0,)), ((), ()))
TN = (((0,), (0,)), ((), ()))


def dg(left, right, dims):
    return lax.dot_general(left, right, dims, preferred_element_type=f32)


def halves(ref, rows):
    return jnp.concatenate([ref[rows, :HEAD_SIZE], ref[rows, HEAD_SIZE:]], axis=0)


def as_rows(column):
    return jnp.broadcast_to(column, (column.shape[0], HEAD_SIZE)).T[0:1, :]


def attend_body(causal, last, flags, q_ref, kv_ref, qbit_ref, kbit_ref, *refs):
    if last:
        acc_in, tot_in, logit_ref, attn_ref, mixed_ref, lse_ref, acc, tot = refs
    else:
        acc_out, tot_out, acc, tot = refs
    qb = pl.program_id(0)
    bq = q_ref.shape[0]
    nk, _, bk = kbit_ref.shape
    q = halves(q_ref, slice(None))
    acc[...] = jnp.zeros_like(acc)
    tot[...] = jnp.zeros_like(tot)

    def step(kb, masked):
        rows = pl.ds(pl.multiple_of(kb * bk, bk), bk)
        s = dg(q, kv_ref[rows, :HEAD_SIZE], NT) * (LOG2E * SCORE_SCALE)
        if masked:
            seen = (qbit_ref[...] & kbit_ref[kb]) != 0
            if causal:
                at = lax.broadcasted_iota(jnp.int32, (bq, bk), 1) + kb * bk
                row = lax.broadcasted_iota(jnp.int32, (bq, bk), 0) + qb * bq
                seen = seen & (at <= row)
            s = jnp.where(jnp.concatenate([seen, seen], axis=0), s, -1e30)
        p = jnp.exp2(s)
        part = p[:, 0:128]
        for i in range(1, bk // 128):
            part = part + p[:, i * 128 : (i + 1) * 128]
        tot[...] += part
        acc[...] += dg(p.astype(bf), kv_ref[rows, HEAD_SIZE:], NN)

    def body(kb, _):
        flag = flags[qb, kb]
        pl.when(flag == 1)(lambda: step(kb, True))
        pl.when(flag == 2)(lambda: step(kb, False))
        return 0

    lax.fori_loop(0, nk, body, 0)
    total = jnp.sum(tot[...], axis=1, keepdims=True)
    if not last:
        acc_out[:, :HEAD_SIZE] = acc[:bq, :]
        acc_out[:, HEAD_SIZE:] = acc[bq:, :]
        tot_out[...] = jnp.concatenate([total[:bq], total[bq:]], axis=1)
    else:
        for h in range(2):
            rows = slice(h * bq, (h + 1) * bq)
            cols = slice(h * HEAD_SIZE, (h + 1) * HEAD_SIZE)
            sums = total[rows] + tot_in[:, h : h + 1]
            out = (acc[rows, :] + acc_in[:, cols]) / sums
            attn_ref[:, cols] = out
            mixed_ref[:, cols] = (out * jax.nn.sigmoid(logit_ref[:, h : h + 1])).astype(bf)
            lse_ref[h : h + 1, :] = as_rows(jnp.log2(sums))


def attend(causal, flags, q, kv, qbit, kbit, earlier=None):
    T = q.shape[0]
    N = kv.shape[0]
    nk = N // BK
    W = 2 * HEAD_SIZE
    blk = lambda w, j=0: pl.BlockSpec((BQ, w), lambda i, f: (i, j))
    last = earlier is not None
    in_specs = [
        blk(W),
        pl.BlockSpec((N, W), lambda i, f: (0, 0)),
        blk(1),
        pl.BlockSpec((nk, 1, BK), lambda i, f: (0, 0, 0)),
    ]
    if last:
        acc, tot, raw = earlier
        extra = [acc, tot, raw]
        in_specs += [blk(W), blk(2), blk(HEAD_SIZE, raw.shape[1] // HEAD_SIZE - 1)]
        out_specs = [blk(W), blk(W), pl.BlockSpec((2, BQ), lambda i, f: (0, i))]
        out_shape = [
            jax.ShapeDtypeStruct((T, W), f32),
            jax.ShapeDtypeStruct((T, W), bf),
            jax.ShapeDtypeStruct((2, T), f32),
        ]
    else:
        extra = []
        out_specs = [blk(W), blk(2)]
        out_shape = [jax.ShapeDtypeStruct((T, W), f32), jax.ShapeDtypeStruct((T, 2), f32)]
    return pl.pallas_call(
        partial(attend_body, causal, last),
        grid_spec=pltpu.PrefetchScalarGridSpec(
            num_scalar_prefetch=1,
            grid=(T // BQ,),
            in_specs=in_specs,
            out_specs=out_specs,
            scratch_shapes=[pltpu.VMEM((2 * BQ, HEAD_SIZE), f32), pltpu.VMEM((2 * BQ, HEAD_SIZE), f32)],
        ),
        out_shape=out_shape,
        cost_estimate=pl.CostEstimate(
            flops=(2 if causal else 4) * T * N * W, bytes_accessed=8 << 20, transcendentals=T * N * (1 if causal else 2)
        ),
        name="attend_own" if causal else "attend_earlier",
    )(flags, q, kv, qbit, kbit, *extra)


def attend_back_body(causal, flags, q_ref, g_ref, kv_ref, qbit_ref, kbit_ref, lse_ref, del_ref, *refs):
    if causal:
        dq_in, dq_ref, dkv_ref, dk_acc, dv_acc = refs
    else:
        dq_ref, dkv_ref, dk_acc, dv_acc = refs
    kb = pl.program_id(0)
    bk = kv_ref.shape[0]
    T = q_ref.shape[0]
    bq = BQ

    @pl.when(kb == 0)
    def _():
        if causal:
            dq_ref[...] = dq_in[...]
        else:
            dq_ref[...] = jnp.zeros_like(dq_ref)

    dk_acc[...] = jnp.zeros_like(dk_acc)
    dv_acc[...] = jnp.zeros_like(dv_acc)

    def line(ref, rows):
        return jnp.concatenate([ref[0:1, rows], ref[1:2, rows]], axis=1)

    def step(qb, masked):
        rows = pl.ds(pl.multiple_of(qb * bq, bq), bq)
        q = halves(q_ref, rows)
        g = halves(g_ref, rows)
        k = kv_ref[:, :HEAD_SIZE]
        s = dg(k, q, NT) * (LOG2E * SCORE_SCALE) - line(lse_ref, rows)
        if masked:
            seen = (kbit_ref[...] & qbit_ref[0:1, rows]) != 0
            if causal:
                at = lax.broadcasted_iota(jnp.int32, (bk, bq), 0) + kb * bk
                row = lax.broadcasted_iota(jnp.int32, (bk, bq), 1) + qb * bq
                seen = seen & (at <= row)
            s = jnp.where(jnp.concatenate([seen, seen], axis=1), s, -1e30)
        p = jnp.exp2(s)
        dv_acc[...] += dg(p.astype(bf), g, NN)
        dp = dg(kv_ref[:, HEAD_SIZE:], g, NT)
        ds = (p * (dp - line(del_ref, rows))).astype(bf)
        dk_acc[...] += dg(ds, q, NN)
        dq = dg(ds, k, TN)
        dq_ref[rows, :HEAD_SIZE] += dq[:bq]
        dq_ref[rows, HEAD_SIZE:] += dq[bq:]

    def body(qb, _):
        flag = flags[qb, kb]
        pl.when(flag == 1)(lambda: step(qb, True))
        pl.when(flag == 2)(lambda: step(qb, False))
        return 0

    lax.fori_loop(0, T // bq, body, 0)
    dkv_ref[:, :HEAD_SIZE] = (dk_acc[...] * SCORE_SCALE).astype(dkv_ref.dtype)
    dkv_ref[:, HEAD_SIZE:] = dv_acc[...].astype(dkv_ref.dtype)


def attend_back(causal, flags, q, g, kv, qbit, kbit, lse, delta, dq=None):
    T = q.shape[0]
    N = kv.shape[0]
    W = 2 * HEAD_SIZE
    whole = lambda *s: pl.BlockSpec(s, lambda i, f: (0,) * len(s))
    along = lambda w: pl.BlockSpec((BK, w), lambda i, f: (i, 0))
    in_specs = [whole(T, W), whole(T, W), along(W), whole(1, T), along(1), whole(2, T), whole(2, T)]
    extra = []
    if causal:
        in_specs.append(whole(T, W))
        extra = [dq]
    return pl.pallas_call(
        partial(attend_back_body, causal),
        grid_spec=pltpu.PrefetchScalarGridSpec(
            num_scalar_prefetch=1,
            grid=(N // BK,),
            in_specs=in_specs,
            out_specs=[whole(T, W), along(W)],
            scratch_shapes=[pltpu.VMEM((BK, HEAD_SIZE), f32), pltpu.VMEM((BK, HEAD_SIZE), f32)],
        ),
        out_shape=[jax.ShapeDtypeStruct((T, W), f32), jax.ShapeDtypeStruct((N, W), f32 if causal else bf)],
        cost_estimate=pl.CostEstimate(
            flops=(5 if causal else 10) * T * N * W, bytes_accessed=12 << 20, transcendentals=T * N * (1 if causal else 2)
        ),
        name="attend_own_back" if causal else "attend_earlier_back",
    )(flags, q, g, kv, qbit, kbit, lse, delta, *extra)


def turn(values):
    return pltpu.roll(values, HEAD_SIZE // 2, 1)


def prepare_body(x_ref, w_ref, cos_ref, sin_ref, gain_ref, raw_ref, q_ref, kv_ref):
    raw_ref[...] = dg(x_ref[...], w_ref[...], NN)
    for i in range(3):
        cols = slice(i * HEAD_SIZE, (i + 1) * HEAD_SIZE)
        u = raw_ref[:, cols]
        r = lax.rsqrt(jnp.mean(u * u, axis=-1, keepdims=True) + EPS)
        n = u * r * gain_ref[(1 if i == 2 else 0) : (2 if i == 2 else 1), :]
        out = (n * cos_ref[...] + turn(n) * sin_ref[...]).astype(bf)
        if i < 2:
            q_ref[:, cols] = out
        else:
            kv_ref[:, :HEAD_SIZE] = out
    kv_ref[:, HEAD_SIZE:] = raw_ref[:, 3 * HEAD_SIZE : 4 * HEAD_SIZE].astype(bf)


def prepare(x, w, cos, sin, gains):
    T, depth = x.shape
    width = w.shape[1]
    blk = lambda w: pl.BlockSpec((BQ, w), lambda i: (i, 0))
    whole = lambda *s: pl.BlockSpec(s, lambda i: (0, 0))
    pair = jax.ShapeDtypeStruct((T, 2 * HEAD_SIZE), bf)
    return pl.pallas_call(
        prepare_body,
        grid=(T // BQ,),
        in_specs=[blk(depth), whole(depth, width), blk(HEAD_SIZE), blk(HEAD_SIZE), whole(2, HEAD_SIZE)],
        out_specs=[blk(width), blk(2 * HEAD_SIZE), blk(2 * HEAD_SIZE)],
        out_shape=[jax.ShapeDtypeStruct((T, width), f32), pair, pair],
        cost_estimate=pl.CostEstimate(flops=2 * T * depth * width, bytes_accessed=T * 640 * 12, transcendentals=T),
        name="prepare_heads",
    )(x, w, cos, sin, gains)


def prepare_back_body(raw_ref, cos_ref, sin_ref, gain_ref, dq_ref, dkv_ref, back_ref, dlogit_ref, out_ref, sums_ref):
    @pl.when(pl.program_id(0) == 0)
    def _():
        sums_ref[...] = jnp.zeros_like(sums_ref)

    sent = lax.axis_index("dp") // GROUP % 2 == 0
    back = jnp.where(sent, back_ref[...].astype(f32), 0.0)
    for i in range(3):
        cols = slice(i * HEAD_SIZE, (i + 1) * HEAD_SIZE)
        if i < 2:
            w = dq_ref[:, cols] * SCORE_SCALE
        else:
            w = dkv_ref[:, :HEAD_SIZE] + back[:, :HEAD_SIZE]
        u = raw_ref[:, cols]
        j = 1 if i == 2 else 0
        r = lax.rsqrt(jnp.mean(u * u, axis=-1, keepdims=True) + EPS)
        w = w * cos_ref[...] + turn(w * sin_ref[...])
        sums_ref[j : j + 1, :] += jnp.sum(w * u * r, axis=0, keepdims=True)
        w = w * gain_ref[j : j + 1, :]
        out_ref[:, cols] = (r * w - u * (r * r * r * jnp.mean(w * u, axis=-1, keepdims=True))).astype(bf)
    out_ref[:, 3 * HEAD_SIZE : 4 * HEAD_SIZE] = (dkv_ref[:, HEAD_SIZE:] + back[:, HEAD_SIZE:]).astype(bf)
    out_ref[:, 4 * HEAD_SIZE :] = dlogit_ref[...]


def prepare_back(raw, cos, sin, gains, dq, dkv, back, dlogit):
    T, width = raw.shape
    W = 2 * HEAD_SIZE
    blk = lambda w: pl.BlockSpec((BQ, w), lambda i: (i, 0))
    flat = pl.BlockSpec((2, HEAD_SIZE), lambda i: (0, 0))
    return pl.pallas_call(
        prepare_back_body,
        grid=(T // BQ,),
        in_specs=[blk(width), blk(HEAD_SIZE), blk(HEAD_SIZE), flat, blk(W), blk(W), blk(W), blk(HEAD_SIZE)],
        out_specs=[blk(width), flat],
        out_shape=[jax.ShapeDtypeStruct((T, width), bf), jax.ShapeDtypeStruct((2, HEAD_SIZE), f32)],
        cost_estimate=pl.CostEstimate(flops=T * 8000, bytes_accessed=T * 640 * 10, transcendentals=T),
        name="prepare_heads_back",
    )(raw, cos, sin, gains, dq, dkv, back, dlogit)


def gate_back_rows(grad_mixed, attn_ref, logit_ref, ga_ref, dlogit_ref, del_ref):
    lanes = lax.broadcasted_iota(jnp.int32, dlogit_ref.shape, 1)
    grads = jnp.zeros(dlogit_ref.shape, f32)
    for h in range(2):
        cols = slice(h * HEAD_SIZE, (h + 1) * HEAD_SIZE)
        g = jax.nn.sigmoid(logit_ref[:, h : h + 1])
        gm = grad_mixed[:, cols]
        at = attn_ref[:, cols]
        ga = (gm * g).astype(bf)
        ga_ref[:, cols] = ga
        slope = jnp.sum(gm * at, axis=-1, keepdims=True) * (g * (1 - g))
        grads = jnp.where(lanes == h, slope, grads)
        del_ref[h : h + 1, :] = as_rows(jnp.sum(ga.astype(f32) * at, axis=-1, keepdims=True))
    dlogit_ref[...] = grads.astype(bf)


def hidden_back_body(dout_ref, down_ref, both_ref, out_ref):
    units = down_ref.shape[1]
    chunk = 256
    for j in range(units // chunk):
        left = slice(j * chunk, (j + 1) * chunk)
        right = slice(units + j * chunk, units + (j + 1) * chunk)
        grad = dg(dout_ref[...], down_ref[:, left], NN)
        gate = both_ref[:, left]
        s = jax.nn.sigmoid(gate)
        out_ref[:, left] = (grad * both_ref[:, right] * s * (1 + gate * (1 - s))).astype(bf)
        out_ref[:, right] = (grad * (gate * s)).astype(bf)


def hidden_back(dout, down, both):
    T, width = dout.shape
    units = down.shape[1]
    blk = lambda w: pl.BlockSpec((2 * BQ, w), lambda i: (i, 0))
    return pl.pallas_call(
        hidden_back_body,
        grid=(T // (2 * BQ),),
        in_specs=[blk(width), pl.BlockSpec((width, units), lambda i: (0, 0)), blk(2 * units)],
        out_specs=blk(2 * units),
        out_shape=jax.ShapeDtypeStruct((T, 2 * units), bf),
        cost_estimate=pl.CostEstimate(flops=2 * T * width * units, bytes_accessed=T * units * 30, transcendentals=T * units),
        name="hidden_back",
    )(dout, down, both)


GROUP = 4
MESH = pl.DeviceIdType.MESH
QUICK = pl.CostEstimate(flops=0, bytes_accessed=1 << 16, transcendentals=0)

def places():
    dp = lax.axis_index("dp"); c = lax.axis_index("mp")
    t = dp % GROUP
    base = dp - t
    tx = t + 1 - 2 * (t % 2)
    ty = t + 2 - 4 * (t // 2)
    td = 3 - t
    return base, t, tx, ty, td, c

def greet(devices):
    barrier = pltpu.get_barrier_semaphore()
    for device in devices:
        pl.semaphore_signal(barrier, inc=1, device_id=device, device_id_type=MESH)
    pl.semaphore_wait(barrier, len(devices))

def gather_steps(x_ref, out_ref, send, recv, local):
    base, t, tx, ty, td, c = places()
    share = x_ref.shape[0]
    half = share // 2
    xdev, ydev, mate = (base + tx, c), (base + ty, c), (base + t, 1 - c)
    greet([xdev, ydev, mate])

    def spot(who, part=None):
        start = (2 * who + c) * share
        if part is None:
            return out_ref.at[pl.ds(pl.multiple_of(start, share), share)]
        return out_ref.at[pl.ds(pl.multiple_of(start + part * half, half), half)]

    def copy(kind, src, dst, device):
        one = pltpu.make_async_remote_copy(
            src_ref=src, dst_ref=dst, send_sem=send.at[kind], recv_sem=recv.at[kind], device_id=device, device_id_type=MESH
        )
        one.start()
        return one

    own = pltpu.make_async_copy(x_ref, spot(t), local)
    own.start()
    mine = [x_ref.at[pl.ds(0, half)], x_ref.at[pl.ds(half, half)]]
    k = {}
    k[2] = copy(2, mine[0], spot(t, 0), ydev)
    k[1] = copy(1, mine[1], spot(t, 1), xdev)
    k[3] = copy(3, mine[1], spot(t, 1), ydev)
    k[0] = copy(0, mine[0], spot(t, 0), xdev)
    k[6] = copy(6, x_ref, spot(t), mate)
    yield
    k[2].wait_recv()
    k[4] = copy(4, spot(ty, 0), spot(ty, 0), xdev)
    k[9] = copy(9, spot(ty, 0), spot(ty, 0), mate)
    k[1].wait_recv()
    k[5] = copy(5, spot(tx, 1), spot(tx, 1), ydev)
    k[8] = copy(8, spot(tx, 1), spot(tx, 1), mate)
    yield
    k[0].wait_recv()
    k[7] = copy(7, spot(tx, 0), spot(tx, 0), mate)
    k[3].wait_recv()
    k[10] = copy(10, spot(ty, 1), spot(ty, 1), mate)
    k[4].wait_recv()
    k[11] = copy(11, spot(td, 0), spot(td, 0), mate)
    k[5].wait_recv()
    k[12] = copy(12, spot(td, 1), spot(td, 1), mate)
    for kind in range(6, 13):
        k[kind].wait_recv()
    for kind in range(13):
        k[kind].wait_send()
    own.wait()
    yield


def gather_body(x_ref, out_ref, send, recv, local):
    for _ in gather_steps(x_ref, out_ref, send, recv, local):
        pass


def gather_sems():
    return [pltpu.SemaphoreType.DMA((13,)), pltpu.SemaphoreType.DMA((13,)), pltpu.SemaphoreType.DMA]


def gather_group(x):
    share, width = x.shape
    return pl.pallas_call(
        gather_body,
        out_shape=jax.ShapeDtypeStruct((share * GROUP * 2, width), x.dtype),
        in_specs=[pl.BlockSpec(memory_space=pltpu.VMEM)],
        out_specs=pl.BlockSpec(memory_space=pl.ANY),
        scratch_shapes=gather_sems(),
        compiler_params=pltpu.CompilerParams(collective_id=1, has_side_effects=True),
        cost_estimate=QUICK,
        name="gather_group",
    )(x)


def gather_attend_body(
    x_ref, q_ref, kv_ref, qbit_ref, kbit_ref, acc_in, tot_in, raw_ref, out_ref, attn_ref, mixed_ref, lse_ref,
    acc, tot, logit, fetch, send, recv, local
):
    edge = raw_ref.shape[1] - HEAD_SIZE
    logits = pltpu.make_async_copy(raw_ref.at[:, pl.ds(edge, HEAD_SIZE)], logit, fetch)
    logits.start()
    steps = gather_steps(x_ref, out_ref, send, recv, local)
    next(steps)
    logits.wait()
    nk, _, bk = kbit_ref.shape

    def block(qb, _):
        here = pl.ds(pl.multiple_of(qb * BQ, BQ), BQ)
        q = halves(q_ref, here)
        acc[...] = jnp.zeros_like(acc)
        tot[...] = jnp.zeros_like(tot)

        def step(kb, _):
            rows = pl.ds(pl.multiple_of(kb * bk, bk), bk)
            s = dg(q, kv_ref[rows, :HEAD_SIZE], NT) * (LOG2E * SCORE_SCALE)
            seen = (qbit_ref[here, :] & kbit_ref[kb]) != 0
            p = jnp.exp2(jnp.where(jnp.concatenate([seen, seen], axis=0), s, -1e30))
            part = p[:, 0:128]
            for i in range(1, bk // 128):
                part = part + p[:, i * 128 : (i + 1) * 128]
            tot[...] += part
            acc[...] += dg(p.astype(bf), kv_ref[rows, HEAD_SIZE:], NN)
            return 0

        lax.fori_loop(0, nk, step, 0)
        total = jnp.sum(tot[...], axis=1, keepdims=True)
        for h in range(2):
            rows = slice(h * BQ, (h + 1) * BQ)
            cols = slice(h * HEAD_SIZE, (h + 1) * HEAD_SIZE)
            sums = total[rows] + tot_in[here, h : h + 1]
            out = (acc[rows, :] + acc_in[here, cols]) / sums
            attn_ref[here, cols] = out
            mixed_ref[here, cols] = (out * jax.nn.sigmoid(logit[here, h : h + 1])).astype(bf)
            lse_ref[h : h + 1, here] = as_rows(jnp.log2(sums))
        return 0

    blocks = q_ref.shape[0] // BQ
    lax.fori_loop(0, 3 * blocks // 8, block, 0)
    next(steps)
    lax.fori_loop(3 * blocks // 8, blocks, block, 0)
    next(steps)


def gather_attend(x, q, kv, qbit, kbit, acc, tot, raw, key):
    share, width = x.shape
    T, W = q.shape
    vmem = pl.BlockSpec(memory_space=pltpu.VMEM)
    anywhere = pl.BlockSpec(memory_space=pl.ANY)
    shape = jax.ShapeDtypeStruct
    return pl.pallas_call(
        gather_attend_body,
        out_shape=[shape((share * GROUP * 2, width), bf), shape((T, W), f32), shape((T, W), bf), shape((2, T), f32)],
        in_specs=[vmem] * 7 + [anywhere],
        out_specs=[anywhere] + [vmem] * 3,
        scratch_shapes=[
            pltpu.VMEM((2 * BQ, HEAD_SIZE), f32),
            pltpu.VMEM((2 * BQ, HEAD_SIZE), f32),
            pltpu.VMEM((T, HEAD_SIZE), f32),
            pltpu.SemaphoreType.DMA,
        ]
        + gather_sems(),
        compiler_params=pltpu.CompilerParams(collective_id=key, has_side_effects=True, vmem_limit_bytes=40 << 20),
        cost_estimate=QUICK,
        name="gather_attend",
    )(x, q, kv, qbit, kbit, acc, tot, raw)


def reduce_body(side, back, left_ref, right_ref, *refs):
    if side:
        tall_ref, out_ref, grad_ref, tall, grad, refs = *refs[:5], refs[5:]
    elif back:
        pair_ref, out_ref, pair_out, refs = *refs[:3], refs[3:]
    else:
        out_ref, refs = refs[0], refs[1:]
    left, right, fars, near, mates, sums, xin, yin, zin, turned, fetch, send, recv = refs
    base, t, tx, ty, td, c = places()
    share = out_ref.shape[0]
    half = share // 2
    chunk = right.shape[0] // 4
    xdev, ydev, mate = (base + tx, c), (base + ty, c), (base + t, 1 - c)
    order = [td, tx, ty, t]
    lefts, rights, talls = [], [], []
    for i, who in enumerate(order):
        for j, core in enumerate((1 - c, c)):
            rows = pl.ds(pl.multiple_of((2 * who + core) * share, share), share)
            n = 2 * i + j
            place = pl.ds(n * share, share)
            lefts.append(pltpu.make_async_copy(left_ref.at[rows], left.at[place], fetch.at[n]))
            if side:
                talls.append(pltpu.make_async_copy(tall_ref.at[rows], tall.at[place], fetch.at[12 + n]))
    for j in range(4):
        rows = pl.ds(j * chunk, chunk)
        rights.append(pltpu.make_async_copy(right_ref.at[rows], right.at[rows], fetch.at[8 + j]))
    for one in lefts[:2] + rights + lefts[2:] + talls:
        one.start()
    friends = [xdev, ydev, mate]
    if back:
        late = lax.axis_index("dp") // GROUP % 2
        friends.append((lax.axis_index("dp") + (GROUP - 2 * GROUP * late), c))
    greet(friends)
    if back:
        pair = pltpu.make_async_remote_copy(
            src_ref=pair_ref,
            dst_ref=pair_out,
            send_sem=send.at[10],
            recv_sem=recv.at[10],
            device_id=friends[-1],
            device_id_type=MESH,
        )
        keep = pltpu.make_async_copy(pair_ref, pair_out, fetch.at[12])

        @pl.when(late == 1)
        def _():
            pair.start()
            keep.start()

    def copy(kind, src, dst, device):
        return pltpu.make_async_remote_copy(
            src_ref=src, dst_ref=dst, send_sem=send.at[kind], recv_sem=recv.at[kind], device_id=device, device_id_type=MESH
        )

    def product(n, dst):
        lefts[n].wait()

        def go(j, _):
            rows = pl.ds(pl.multiple_of(j * chunk, chunk), chunk)
            dst[:, rows] = dg(left[n * share : (n + 1) * share, :], right[rows, :], NT).astype(dst.dtype)
            return 0

        if n == 0:
            for j in range(4):
                rights[j].wait()
                go(j, 0)
        else:
            lax.fori_loop(0, 4, go, 0)

    def add(dst, one, two):
        step = 16

        def go(i, _):
            rows = pl.ds(pl.multiple_of(i * step, step), step)
            dst[rows, :] = (one[rows, :].astype(f32) + two[rows, :].astype(f32)).astype(dst.dtype)
            return 0

        lax.fori_loop(0, dst.shape[0] // step, go, 0)

    A, B = pl.ds(0, half), pl.ds(half, half)
    over, k = [], {}

    def join(i):
        over[i].wait_recv()
        add(sums.at[i], near.at[i], mates.at[i])
        if i == 0:
            k[4] = copy(4, sums.at[0, A], xin.at[1], xdev)
            k[5] = copy(5, sums.at[0, B], yin.at[1], ydev)
            k[4].start()
            k[5].start()
        if i == 1:
            k[6] = copy(6, sums.at[1, A], xin.at[0], xdev)
            k[6].start()
        if i == 2:
            k[7] = copy(7, sums.at[2, B], yin.at[0], ydev)
            k[7].start()

    for i in range(4):
        product(2 * i, fars.at[i])
        over.append(copy(i, fars.at[i], mates.at[i], mate))
        over[i].start()
        product(2 * i + 1, near.at[i])
        if i:
            join(i - 1)
    join(3)
    k[4].wait_recv()
    add(turned.at[0], sums.at[2, A], xin.at[1])
    k[8] = copy(8, turned.at[0], zin.at[0], ydev)
    k[8].start()
    k[5].wait_recv()
    add(turned.at[1], sums.at[1, B], yin.at[1])
    k[9] = copy(9, turned.at[1], zin.at[1], xdev)
    k[9].start()
    if side:
        for one in talls:
            one.wait()

        def inner_product(j, _):
            cols = pl.ds(pl.multiple_of(j * 256, 256), 256)
            grad[cols, :] = dg(tall[:, cols], left[...], TN).astype(bf)
            return 0

        lax.fori_loop(0, tall.shape[1] // 256, inner_product, 0)
        put = pltpu.make_async_copy(grad, grad_ref, fetch.at[20])
        put.start()
    k[6].wait_recv()
    add(out_ref.at[A], sums.at[3, A], xin.at[0])
    k[7].wait_recv()
    add(out_ref.at[B], sums.at[3, B], yin.at[0])
    k[8].wait_recv()
    add(out_ref.at[A], out_ref.at[A], zin.at[0])
    k[9].wait_recv()
    add(out_ref.at[B], out_ref.at[B], zin.at[1])
    for i in range(4):
        over[i].wait_send()
    for kind in range(4, 10):
        k[kind].wait_send()
    if side:
        put.wait()
    if back:

        @pl.when(late == 1)
        def _():
            pair.wait_send()
            keep.wait()

        @pl.when(late == 0)
        def _():
            pair.wait_recv()


def product_reduce(left, right, key, tall=None, pair=None):
    rows, depth = left.shape
    side = tall is not None
    back = pair is not None
    width = right.shape[0]
    share = rows // (2 * GROUP)
    half = share // 2
    block = lambda n, r: pltpu.VMEM((n, r, width), bf)
    anywhere = pl.BlockSpec(memory_space=pl.ANY)
    outs, out_specs = [jax.ShapeDtypeStruct((share, width), f32)], [pl.BlockSpec(memory_space=pltpu.VMEM)]
    ins, extra = [left, right], []
    if side:
        ins.append(tall)
        outs.append(jax.ShapeDtypeStruct((tall.shape[1], depth), bf))
        out_specs.append(anywhere)
        extra = [pltpu.VMEM(tall.shape, bf), pltpu.VMEM((tall.shape[1], depth), bf)]
    in_specs = [anywhere] * len(ins)
    if back:
        ins.append(pair)
        in_specs.append(pl.BlockSpec(memory_space=pltpu.VMEM))
        outs.append(jax.ShapeDtypeStruct(pair.shape, bf))
        out_specs.append(anywhere)
    result = pl.pallas_call(
        partial(reduce_body, side, back),
        out_shape=outs,
        in_specs=in_specs,
        out_specs=out_specs,
        scratch_shapes=extra
        + [
            pltpu.VMEM((rows, depth), bf),
            pltpu.VMEM((width, depth), bf),
            block(4, share),
            block(4, share),
            block(4, share),
            block(4, share),
            block(2, half),
            block(2, half),
            block(2, half),
            block(2, half),
            pltpu.SemaphoreType.DMA((21,)),
            pltpu.SemaphoreType.DMA((11,)),
            pltpu.SemaphoreType.DMA((11,)),
        ],
        compiler_params=pltpu.CompilerParams(collective_id=key, has_side_effects=True, vmem_limit_bytes=60 << 20),
        cost_estimate=QUICK,
        name="product_reduce",
    )(*ins)
    return result if side or back else result[0]


def gather_product_body(glu, x_ref, w_ref, *refs):
    if glu:
        full_ref, y_ref, hidden_ref, hs, ys, refs = *refs[:5], refs[5:]
    else:
        attn_ref, raw_ref, full_ref, ga_ref, dlogit_ref, del_ref, attn, logit, gs, ds, es, refs = *refs[:11], refs[11:]
    buf, w, fetch, put_x, put_y, send, recv = refs
    base, t, tx, ty, td, c = places()
    share = x_ref.shape[0]
    half = share // 2
    width = w.shape[1]
    xdev, ydev, mate = (base + tx, c), (base + ty, c), (base + t, 1 - c)
    weights = [pltpu.make_async_copy(w_ref, w, fetch.at[0])]
    if not glu:
        edge = raw_ref.shape[1] - HEAD_SIZE
        weights.append(pltpu.make_async_copy(attn_ref, attn, fetch.at[1]))
        weights.append(pltpu.make_async_copy(raw_ref.at[:, pl.ds(edge, HEAD_SIZE)], logit, fetch.at[2]))
    for one in weights:
        one.start()
    greet([xdev, ydev, mate])

    def unit(who, core):
        return pl.ds(pl.multiple_of((2 * who + core) * share, share), share)

    def spot(who, part):
        start = (2 * who + c) * share + part * half
        return buf.at[pl.ds(pl.multiple_of(start, half), half)]

    def copy(kind, src, dst, device):
        one = pltpu.make_async_remote_copy(
            src_ref=src, dst_ref=dst, send_sem=send.at[kind], recv_sem=recv.at[kind], device_id=device, device_id_type=MESH
        )
        one.start()
        return one

    mine = [x_ref.at[pl.ds(0, half)], x_ref.at[pl.ds(half, half)]]
    k, puts = {}, []
    k[2] = copy(2, mine[0], spot(t, 0), ydev)
    k[1] = copy(1, mine[1], spot(t, 1), xdev)
    k[3] = copy(3, mine[1], spot(t, 1), ydev)
    k[0] = copy(0, mine[0], spot(t, 0), xdev)
    k[6] = copy(6, x_ref, buf.at[unit(t, c)], mate)
    for one in weights:
        one.wait()

    def work(n, src, who, core):
        rows = unit(who, core)
        slot = n % 2
        one = pltpu.make_async_copy(src, full_ref.at[rows], put_x.at[n])
        one.start()
        if n >= 2:
            for old in puts[n - 2][1:]:
                old.wait()
        if glu:
            chunk = 256

            def go(j, _):
                left = pl.ds(pl.multiple_of(j * chunk, chunk), chunk)
                right = pl.ds(pl.multiple_of(width // 2 + j * chunk, chunk), chunk)
                gate = dg(src[...], w[:, left], NN)
                up = dg(src[...], w[:, right], NN)
                ys[slot, :, left] = gate
                ys[slot, :, right] = up
                hs[slot, :, left] = (gate * jax.nn.sigmoid(gate) * up).astype(bf)
                return 0

            lax.fori_loop(0, width // 2 // chunk, go, 0)
            outs = [
                one,
                pltpu.make_async_copy(ys.at[slot], y_ref.at[rows], put_y.at[n]),
                pltpu.make_async_copy(hs.at[slot], hidden_ref.at[rows], put_y.at[8 + n]),
            ]
        else:
            gm = dg(src[...], w[...], NN)
            gate_back_rows(gm, attn.at[rows], logit.at[rows], gs.at[slot], ds.at[slot], es.at[slot])
            outs = [
                one,
                pltpu.make_async_copy(gs.at[slot], ga_ref.at[rows], put_y.at[n]),
                pltpu.make_async_copy(ds.at[slot], dlogit_ref.at[rows], put_y.at[8 + n]),
                pltpu.make_async_copy(es.at[slot], del_ref.at[:, rows], put_y.at[16 + n]),
            ]
        for out in outs[1:]:
            out.start()
        puts.append(outs)

    def landed(who, core):
        return buf.at[unit(who, core)]

    work(0, x_ref, t, c)
    k[6].wait_recv()
    work(1, landed(t, 1 - c), t, 1 - c)
    k[2].wait_recv()
    k[4] = copy(4, spot(ty, 0), spot(ty, 0), xdev)
    k[9] = copy(9, spot(ty, 0), spot(ty, 0), mate)
    k[1].wait_recv()
    k[5] = copy(5, spot(tx, 1), spot(tx, 1), ydev)
    k[8] = copy(8, spot(tx, 1), spot(tx, 1), mate)
    k[0].wait_recv()
    k[7] = copy(7, spot(tx, 0), spot(tx, 0), mate)
    k[3].wait_recv()
    k[10] = copy(10, spot(ty, 1), spot(ty, 1), mate)
    work(2, landed(tx, c), tx, c)
    work(3, landed(ty, c), ty, c)
    k[7].wait_recv()
    k[8].wait_recv()
    work(4, landed(tx, 1 - c), tx, 1 - c)
    k[9].wait_recv()
    k[10].wait_recv()
    work(5, landed(ty, 1 - c), ty, 1 - c)
    k[4].wait_recv()
    k[11] = copy(11, spot(td, 0), spot(td, 0), mate)
    k[5].wait_recv()
    k[12] = copy(12, spot(td, 1), spot(td, 1), mate)
    work(6, landed(td, c), td, c)
    k[11].wait_recv()
    k[12].wait_recv()
    work(7, landed(td, 1 - c), td, 1 - c)
    for kind in range(13):
        k[kind].wait_send()
    for n, outs in enumerate(puts):
        outs[0].wait()
        if n >= 6:
            for out in outs[1:]:
                out.wait()


def gather_product(x, w, key, gated=None):
    share, depth = x.shape
    width = w.shape[1]
    rows = share * GROUP * 2
    anywhere = pl.BlockSpec(memory_space=pl.ANY)
    shape = jax.ShapeDtypeStruct
    if gated is None:
        gated = []
        outs = [shape((rows, width), f32), shape((rows, width // 2), bf)]
        extra = [pltpu.VMEM((2, share, width // 2), bf), pltpu.VMEM((2, share, width), f32)]
    else:
        outs = [shape((rows, width), bf), shape((rows, HEAD_SIZE), bf), shape((2, rows), f32)]
        extra = [
            pltpu.VMEM((rows, width), f32),
            pltpu.VMEM((rows, HEAD_SIZE), f32),
            pltpu.VMEM((2, share, width), bf),
            pltpu.VMEM((2, share, HEAD_SIZE), bf),
            pltpu.VMEM((2, 2, share), f32),
        ]
    outs = [shape((rows, depth), bf)] + outs
    return pl.pallas_call(
        partial(gather_product_body, not gated),
        out_shape=outs,
        in_specs=[pl.BlockSpec(memory_space=pltpu.VMEM)] + [anywhere] * (1 + len(gated)),
        out_specs=[anywhere] * len(outs),
        scratch_shapes=extra
        + [
            pltpu.VMEM((rows, depth), bf),
            pltpu.VMEM((depth, width), bf),
            pltpu.SemaphoreType.DMA((3,)),
            pltpu.SemaphoreType.DMA((8,)),
            pltpu.SemaphoreType.DMA((24,)),
            pltpu.SemaphoreType.DMA((13,)),
            pltpu.SemaphoreType.DMA((13,)),
        ],
        compiler_params=pltpu.CompilerParams(collective_id=key, has_side_effects=True, vmem_limit_bytes=48 << 20),
        cost_estimate=QUICK,
        name="gather_product",
    )(x, w, *gated)


def far_places():
    dp = lax.axis_index("dp")
    return dp // GROUP, lax.axis_size("dp") // GROUP


def far_friends():
    base, t, tx, ty, td, c = places()
    r, count = far_places()
    return [((r + i) % count * GROUP + t, c) for i in range(1, count)] + [(base + t, 1 - c)]


def small_copy(send, recv):
    def copy(kind, src, dst, device):
        one = pltpu.make_async_remote_copy(
            src_ref=src, dst_ref=dst, send_sem=send.at[kind], recv_sem=recv.at[kind], device_id=device, device_id_type=MESH
        )
        one.start()
        return one

    return copy


def spread(x_ref, out_ref, send, recv, local):
    base, t, tx, ty, td, c = places()
    r, count = far_places()
    copy = small_copy(send, recv)
    own = pltpu.make_async_copy(x_ref, out_ref.at[c, t, r], local)
    own.start()
    others = [(r + i) % count for i in range(1, count)]
    stage = [copy(i, x_ref, out_ref.at[c, t, r], (z * GROUP + t, c)) for i, z in enumerate(others)]
    own.wait()
    for one in stage:
        one.wait()
    stage = [copy(count - 1 + i, out_ref.at[c, t], out_ref.at[c, t], (base + who, c)) for i, who in enumerate([td, tx, ty])]
    yield
    for one in stage:
        one.wait()
    copy(count + 2, out_ref.at[c], out_ref.at[c], (base + t, 1 - c)).wait()
    yield


def collect(x_ref, out_ref, one_in, one_sum, two_in, two_sum, far_in, send, recv):
    base, t, tx, ty, td, c = places()
    r, count = far_places()
    copy = small_copy(send, recv)
    copy(0, x_ref.at[1 - c], one_in, (base + t, 1 - c)).wait()
    one_sum[...] = x_ref[c] + one_in[...]
    stage = [copy(1 + i, one_sum.at[who], two_in.at[i], (base + who, c)) for i, who in enumerate([td, tx, ty])]
    yield
    for one in stage:
        one.wait()
    two_sum[...] = one_sum[t] + two_in[0] + two_in[1] + two_in[2]
    others = [(r + i) % count for i in range(1, count)]
    stage = [copy(4 + i, two_sum.at[z], far_in.at[i], (z * GROUP + t, c)) for i, z in enumerate(others)]
    for one in stage:
        one.wait()
    total = two_sum[r]
    for i in range(count - 1):
        total = total + far_in[i]
    out_ref[...] = total
    yield


def small_scratch(tile, inward):
    count = lax.axis_size("dp") // GROUP
    sems = [pltpu.SemaphoreType.DMA((count + 3,)), pltpu.SemaphoreType.DMA((count + 3,))]
    if inward:
        return sems + [pltpu.SemaphoreType.DMA]
    shapes = [(GROUP, count), (GROUP, count), (3, count), (count,), (count - 1,)]
    return [pltpu.VMEM(shape + tile, f32) for shape in shapes] + sems


def trade_body(inward, widths, sender, side, small, *refs):
    base, t, tx, ty, td, c = places()
    partners = [td, tx, ty]
    friends = [(base + who, c) for who in partners]
    flat = [(i, sum(ws[:j]), w) for i, ws in enumerate(widths) for j, w in enumerate(ws)]
    count = len(flat)
    packed, loose = len(widths), count
    ins, refs = refs[: loose if inward else packed], refs[loose if inward else packed :]
    if sender is not None:
        pair_ref, refs = refs[0], refs[1:]
    if side:
        tall_ref, wide_ref, refs = *refs[:2], refs[2:]
    if small:
        small_ref, refs = refs[0], refs[1:]
    outs, refs = refs[: packed if inward else loose], refs[packed if inward else loose :]
    if sender is not None:
        pair_out, refs = refs[0], refs[1:]
    if side:
        grad_ref, refs = refs[0], refs[1:]
    if small:
        small_out, refs = refs[0], refs[1:]
    if side:
        tall, wide, grad, fetch, refs = *refs[:4], refs[4:]
    send, recv, local, *rest = refs
    if small:
        friends += far_friends()
    if sender is not None:
        late = lax.axis_index("dp") // GROUP % 2
        friends.append((lax.axis_index("dp") + (GROUP - 2 * GROUP * late), c))
    greet(friends)

    def block(ref, i, who):
        array, start, width = flat[i]
        return ref[array].at[who, :, pl.ds(start, width)]

    def column(ref, i, who):
        width = flat[i][2]
        return ref[i].at[:, pl.ds(pl.multiple_of(who * width, width), width)]

    if small:
        steps = (spread if inward else collect)(small_ref, small_out, *rest)
        next(steps)
    source, target = (column, block) if inward else (block, column)
    copies = []
    for j, who in enumerate(partners):
        for i in range(count):
            kind = j * count + i
            one = pltpu.make_async_remote_copy(
                src_ref=source(ins, i, who),
                dst_ref=target(outs, i, t),
                send_sem=send.at[kind],
                recv_sem=recv.at[kind],
                device_id=(base + who, c),
                device_id_type=MESH,
            )
            one.start()
            copies.append(one)
    if sender is not None:
        pair = pltpu.make_async_remote_copy(
            src_ref=pair_ref,
            dst_ref=pair_out,
            send_sem=send.at[3 * count],
            recv_sem=recv.at[3 * count],
            device_id=friends[-1],
            device_id_type=MESH,
        )
        keep = pltpu.make_async_copy(pair_ref, pair_out, local.at[count])

        @pl.when(late == sender)
        def _():
            pair.start()
            keep.start()

    owns = [pltpu.make_async_copy(source(ins, i, t), target(outs, i, t), local.at[i]) for i in range(count)]
    for own in owns:
        own.start()
    if side:
        loads = [pltpu.make_async_copy(tall_ref, tall, fetch.at[0]), pltpu.make_async_copy(wide_ref, wide, fetch.at[1])]
        for one in loads:
            one.start()
        for one in loads:
            one.wait()

        def inner_product(j, _):
            cols = pl.ds(pl.multiple_of(j * 256, 256), 256)
            grad[cols, :] = dg(tall[:, cols], wide[...], TN).astype(bf)
            return 0

        lax.fori_loop(0, tall.shape[1] // 256, inner_product, 0)
        put = pltpu.make_async_copy(grad, grad_ref, fetch.at[2])
        put.start()
    if small:
        next(steps)
    for one in copies:
        one.wait()
    for own in owns:
        own.wait()
    if side:
        put.wait()
    if sender is not None:

        @pl.when(late == sender)
        def _():
            pair.wait_send()
            keep.wait()

        @pl.when(late == 1 - sender)
        def _():
            pair.wait_recv()


def trade_call(inward, ins, outs, widths, key, pair=None, sender=None, side=(), small=None):
    vmem = pl.BlockSpec(memory_space=pltpu.VMEM)
    anywhere = pl.BlockSpec(memory_space=pl.ANY)
    count = sum(len(ws) for ws in widths)
    scratch = []
    if sender is not None:
        ins = list(ins) + [pair]
        outs = outs + [jax.ShapeDtypeStruct(pair.shape, bf)]
    if side:
        tall, wide = side
        grad = (tall.shape[1], wide.shape[1])
        outs = outs + [jax.ShapeDtypeStruct(grad, bf)]
        scratch = [pltpu.VMEM(tall.shape, bf), pltpu.VMEM(wide.shape, bf), pltpu.VMEM(grad, bf), pltpu.SemaphoreType.DMA((3,))]
    smalls = [] if small is None else [small]
    out_specs = [anywhere] * len(outs) + [vmem] * len(smalls)
    rest = []
    if smalls:
        tile = small.shape[-2:]
        result = (2, GROUP, lax.axis_size("dp") // GROUP) + tile if inward else tile
        outs = outs + [jax.ShapeDtypeStruct(result, f32)]
        rest = small_scratch(tile, inward)
    return pl.pallas_call(
        partial(trade_body, inward, widths, sender, bool(side), bool(smalls)),
        out_shape=outs,
        in_specs=[vmem] * len(ins) + [anywhere] * len(side) + [vmem] * len(smalls),
        out_specs=out_specs,
        scratch_shapes=scratch
        + [
            pltpu.SemaphoreType.DMA((3 * count + 1,)),
            pltpu.SemaphoreType.DMA((3 * count + 1,)),
            pltpu.SemaphoreType.DMA((count + 1,)),
        ]
        + rest,
        compiler_params=pltpu.CompilerParams(collective_id=key, has_side_effects=True),
        cost_estimate=QUICK,
        name="trade_group",
    )(*ins, *side, *smalls)


def trade_group(weights, key, pair=None, small=None):
    rows = weights[0].shape[0]
    widths = (tuple(w.shape[1] // GROUP for w in weights),)
    outs = [jax.ShapeDtypeStruct((GROUP, rows, sum(widths[0])), bf)]
    if pair is None:
        result = trade_call(True, weights, outs, widths, key, small=small)
        return result[0] if small is None else result
    return trade_call(True, weights, outs, widths, key, pair, 0)


def trade_back(grads, widths, key, pair=None, side=(), small=None):
    rows = grads[0].shape[1]
    outs = [jax.ShapeDtypeStruct((rows, GROUP * w), bf) for ws in widths for w in ws]
    return trade_call(False, grads, outs, widths, key, pair, None if pair is None else 1, side, small)


def row_norm(values, gain):
    scale = lax.rsqrt(jnp.mean(values * values, axis=-1, keepdims=True) + EPS)
    return values * scale * gain


def rope_tables(positions, width):
    half = width // 2
    lanes = jnp.arange(width, dtype=jnp.int32)
    freqs = THETA ** (-((lanes % half).astype(f32) / half))
    angle = positions.astype(f32) * freqs[None, :]
    return jnp.cos(angle), jnp.sin(angle) * jnp.where(lanes < half, -1.0, 1.0)[None, :]


def tables_body(group_tokens, early, seg_count, parents, lengths, pos_ref, qcol_ref, qline_ref, kline_ref, kcol_ref, flags, key_any):
    step = pl.program_id(0)
    first = lax.axis_index("dp") // GROUP * group_tokens
    tree = first // TREE_TOKENS
    begin = first - tree * TREE_TOKENS
    size = [lengths[tree, seg] for seg in range(seg_count)]
    starts, bits, depth = [jnp.int32(0)], [jnp.int32(1)], [jnp.int32(0)]
    for seg in range(1, seg_count):
        starts.append(starts[-1] + size[seg - 1])
        parent = parents[tree, seg]
        above, deep = bits[0], depth[0] + size[0]
        for p in range(1, seg):
            above = jnp.where(parent == p, bits[p], above)
            deep = jnp.where(parent == p, depth[p] + size[p], deep)
        bits.append(above | (1 << seg))
        depth.append(deep)
    powers = [jnp.int32(1 << seg) for seg in range(seg_count)]

    def by_segment(offsets, values):
        out = jnp.zeros_like(offsets) + values[0]
        for start, value in zip(starts[1:], values[1:]):
            out = jnp.where(offsets >= start, value, out)
        return out

    q_first = begin + step * BQ
    k_first = begin - early + step * BK
    column = lax.broadcasted_iota(jnp.int32, (BQ, 1), 0) + q_first
    pos_ref[...] = by_segment(column, [d - s for d, s in zip(depth, starts)]) + column
    qcol_ref[...] = by_segment(column, bits)
    qline_ref[...] = by_segment(lax.broadcasted_iota(jnp.int32, (1, BQ), 1) + q_first, bits)
    column = lax.broadcasted_iota(jnp.int32, (BK, 1), 0) + k_first
    kcol_ref[...] = jnp.where(column >= 0, by_segment(column, powers), 0)
    line = lax.broadcasted_iota(jnp.int32, (1, BK), 1) + k_first
    kline_ref[0] = jnp.where(line >= 0, by_segment(line, powers), 0)

    def touches(begins, seg, span):
        return (starts[seg] <= begins + span - 1) & (starts[seg] + size[seg] > begins)

    @pl.when(step == 0)
    def _():
        for k in range(key_any.shape[0]):
            seen = jnp.int32(0)
            for seg in range(seg_count):
                seen = jnp.where(touches(begin - early + k * BK, seg, BK), seen | powers[seg], seen)
            key_any[k] = seen

    query_any, query_all = jnp.int32(0), jnp.int32(-1)
    for seg in range(seg_count):
        inside = touches(q_first, seg, BQ)
        query_any = jnp.where(inside, query_any | bits[seg], query_any)
        query_all = jnp.where(inside, query_all & bits[seg], query_all)
    for k in range(key_any.shape[0]):
        keys_at = begin - early + k * BK
        some = ((query_any & key_any[k]) != 0) & (keys_at <= q_first + BQ - 1)
        every = ((key_any[k] & ~query_all) == 0) & (keys_at + BK - 1 <= q_first)
        flags[step, k] = jnp.where(some, jnp.where(every, 2, 1), 0)


def tables(parents, lengths, group_tokens, planes):
    seg_count = parents.shape[1]
    early = (planes - 1) * group_tokens
    steps = group_tokens // BQ
    blocks = planes * group_tokens // BK
    i32 = lambda *shape: jax.ShapeDtypeStruct(shape, jnp.int32)
    smem = pl.BlockSpec(memory_space=pltpu.SMEM)
    return pl.pallas_call(
        partial(tables_body, group_tokens, early, seg_count),
        grid=(steps,),
        in_specs=[smem, smem],
        out_specs=[
            pl.BlockSpec((BQ, 1), lambda i: (i, 0)),
            pl.BlockSpec((BQ, 1), lambda i: (i, 0)),
            pl.BlockSpec((1, BQ), lambda i: (0, i)),
            pl.BlockSpec((1, 1, BK), lambda i: (i, 0, 0)),
            pl.BlockSpec((BK, 1), lambda i: (i, 0)),
            smem,
        ],
        out_shape=[
            i32(group_tokens, 1),
            i32(group_tokens, 1),
            i32(1, group_tokens),
            i32(blocks, 1, BK),
            i32(blocks * BK, 1),
            i32(steps, blocks),
        ],
        scratch_shapes=[pltpu.SMEM((blocks,), jnp.int32)],
        cost_estimate=QUICK,
        name="tables",
    )(parents, lengths)


def inner(left, right):
    return dg(left, right, TN)


def after(value, *others):
    return lax.optimization_barrier((value,) + others)[0]


def per_device(
    layer_in,
    out_grad,
    parents,
    lengths,
    attn_gain,
    mlp_gain,
    query_norm_gain,
    key_gain,
    query_weight,
    key_matrix,
    value_matrix,
    headgate_weight,
    output_weight,
    gate_weight,
    up_weight,
    down_weight,
):
    data_count = lax.axis_size("dp")
    model_count = lax.axis_size("mp")
    share, width = layer_in.shape
    rows_here = query_weight.shape[0]
    group_tokens = share * model_count * GROUP
    seg_count = parents.shape[1]
    far = [[member + GROUP * plane for plane in range(data_count // GROUP)] for member in range(GROUP)]
    planes = TREE_TOKENS // group_tokens

    gates = headgate_weight.shape[1] // GROUP
    pieces_gates = jnp.pad(
        headgate_weight.reshape(rows_here, GROUP, gates), ((0, 0), (0, 0), (0, HEAD_SIZE - gates))
    ).reshape(rows_here, GROUP * HEAD_SIZE)

    def far_gather(mine):
        return lax.all_gather(
            mine.reshape(GROUP * rows_here, -1), "dp", axis=0, tiled=True, axis_index_groups=far
        )

    def far_scatter(grad):
        mine = lax.psum_scatter(grad, "dp", scatter_dimension=0, tiled=True, axis_index_groups=far)
        return mine.reshape(GROUP, rows_here, -1)

    sizes = [attn_gain.shape[0], mlp_gain.shape[0], query_norm_gain.shape[0], key_gain.shape[0]]
    cuts = [sum(sizes[:i]) for i in range(5)]
    tile = (8, 128)
    spare = tile[0] * tile[1] - cuts[4]
    gain_tile = jnp.pad(
        jnp.concatenate([attn_gain, mlp_gain, query_norm_gain, key_gain]).astype(f32), (0, spare)
    ).reshape(tile)
    mine_attn, all_gains = trade_group([query_weight, key_matrix, value_matrix, pieces_gates], 3, small=gain_tile)
    full_attn = far_gather(mine_attn)
    gains = all_gains.transpose(2, 1, 0, 3, 4).reshape(data_count * model_count, -1)
    gain_one, gain_two, gain_query, gain_key = [
        gains[:, cuts[i] : cuts[i + 1]].reshape(-1) for i in range(4)
    ]
    head_gains = jnp.stack([gain_query, gain_key])
    mine_out = trade_group([after(output_weight.T, all_gains)], 4)
    full_out = far_gather(mine_out)

    positions, query_column, query_line, key_lines, key_column, flags = tables(parents, lengths, group_tokens, planes)
    cosine, sine = rope_tables(positions, HEAD_SIZE)
    early = (planes - 1) * group_tokens
    key_cut = early // BK

    rows = layer_in.astype(f32)
    normed_one, norm_one_back = jax.vjp(row_norm, rows, gain_one)
    hidden_first = gather_group(after(normed_one.astype(bf), mine_out))
    q_width = query_weight.shape[1] // GROUP
    k_width = key_matrix.shape[1] // GROUP
    heads = q_width // HEAD_SIZE
    raw, query, pair = prepare(hidden_first, full_attn, cosine, sine, head_gains)
    mine_glu, pair_early = trade_group([gate_weight, up_weight], 5, pair)
    full_glu = far_gather(mine_glu)
    query = after(query, mine_glu)
    own = attend(True, flags[:, key_cut:], query, pair, query_column, key_lines[key_cut:])
    mine_down = trade_group([after(down_weight.T, own[0])], 6)
    full_down = far_gather(mine_down)
    grad_tokens, attn, mixed, lse = gather_attend(
        after(out_grad, mine_down), query, pair_early, query_column, key_lines[:key_cut], own[0], own[1], raw, 19
    )
    branch = product_reduce(mixed, full_out, 2)
    middle = rows + branch

    normed_two, norm_two_back = jax.vjp(row_norm, middle, gain_two)
    h_two, both_glu, hidden = gather_product(normed_two.astype(bf), full_glu, 14)
    units = full_down.shape[1]

    down_part = inner(grad_tokens, hidden).astype(bf)
    down_rows = far_scatter(down_part)
    grad_glu = hidden_back(after(grad_tokens, down_part), full_down, both_glu)
    grad_h_two, glu_part = product_reduce(grad_glu, full_glu, 15, h_two)
    glu_rows = far_scatter(glu_part)
    grad_mid_norm, gain_two_grad = norm_two_back(grad_h_two)
    grad_middle = out_grad.astype(f32) + grad_mid_norm

    grad_branch, grad_attn, grad_logit, delta = gather_product(grad_middle.astype(bf), full_out, 16, [attn, raw])
    query_grad, early_grad = attend_back(
        False, flags[:, :key_cut], query, grad_attn, pair_early, query_line, key_column[:early], lse, delta
    )
    query_grad, own_grad = attend_back(
        True, flags[:, key_cut:], query, grad_attn, pair, query_line, key_column[early:], lse, delta, query_grad
    )
    down_grad, out_part = trade_back([after(down_rows, own_grad)], ((units,),), 7, side=(grad_branch, mixed))
    out_rows = far_scatter(out_part)
    last_branch, returned = product_reduce(after(hidden, out_part), full_down, 18, pair=early_grad)
    layer_out = (middle + last_branch).astype(bf)
    grad_raw, head_gain_grads = prepare_back(raw, cosine, sine, head_gains, query_grad, own_grad, returned, grad_logit)
    grad_h_one, attn_part = product_reduce(grad_raw, full_attn, 17, hidden_first)
    attn_rows = far_scatter(attn_part)
    grad_in_norm, gain_one_grad = norm_one_back(grad_h_one)
    input_grad = (grad_middle + grad_in_norm).astype(bf)

    devices = data_count * model_count
    gain_parts = jnp.concatenate(
        [
            piece.reshape(devices, -1)
            for piece in (gain_one_grad, gain_two_grad, head_gain_grads[0], head_gain_grads[1], jnp.zeros((devices, spare), f32))
        ],
        axis=1,
    )
    gain_parts = gain_parts.reshape((data_count // GROUP, GROUP, model_count) + tile).transpose(2, 1, 0, 3, 4)
    gate_grad, up_grad, out_weight_grad, gain_sums = trade_back(
        [after(glu_rows, grad_h_one), out_rows], ((units, units), (q_width,)), 8, small=gain_parts
    )
    gain_sums = gain_sums.reshape(-1)
    q_grad, k_grad, v_grad, gates_grad = trade_back(
        [after(attn_rows, gain_sums)], ((q_width, k_width, k_width, HEAD_SIZE),), 10
    )
    gates_grad = gates_grad.reshape(rows_here, GROUP, HEAD_SIZE)[:, :, :heads].reshape(rows_here, -1)
    return (
        layer_out,
        input_grad,
        gain_sums[cuts[0] : cuts[1]],
        gain_sums[cuts[1] : cuts[2]],
        gain_sums[cuts[2] : cuts[3]],
        gain_sums[cuts[3] : cuts[4]],
        q_grad.astype(f32),
        k_grad.astype(f32),
        v_grad.astype(f32),
        gates_grad.astype(f32),
        out_weight_grad.astype(f32).T,
        gate_grad.astype(f32),
        up_grad.astype(f32),
        down_grad.astype(f32).T,
    )


def solution(mesh):
    in_specs = (
        P(("dp", "mp"), None),
        P(("dp", "mp"), None),
        P(),
        P(),
        P(("dp", "mp")),
        P(("dp", "mp")),
        P(("dp", "mp")),
        P(("dp", "mp")),
        P("dp", "mp"),
        P("dp", "mp"),
        P("dp", "mp"),
        P("dp", "mp"),
        P("mp", "dp"),
        P("dp", "mp"),
        P("dp", "mp"),
        P("mp", "dp"),
    )
    out_specs = (
        P(("dp", "mp"), None),
        P(("dp", "mp"), None),
        P(("dp", "mp")),
        P(("dp", "mp")),
        P(("dp", "mp")),
        P(("dp", "mp")),
        P("dp", "mp"),
        P("dp", "mp"),
        P("dp", "mp"),
        P("dp", "mp"),
        P("mp", "dp"),
        P("dp", "mp"),
        P("dp", "mp"),
        P("mp", "dp"),
    )
    return jax.shard_map(
        per_device, mesh=mesh, in_specs=in_specs, out_specs=out_specs, check_vma=False
    )
```

```python
from functools import partial

import jax
import jax.numpy as jnp
from jax import lax
from jax.experimental import pallas as pl
from jax.experimental.pallas import tpu as pltpu
from jax.sharding import PartitionSpec as P

HEAD_SIZE = 128
TREE_TOKENS = 4096
EPS = 1e-06
THETA = 1000000.0
f32 = jnp.float32
bf = jnp.bfloat16

LOG2E = 1.4426950408889634
SCORE_SCALE = HEAD_SIZE ** (-0.5)
BQ = 256
BK = 512
NT = (((1,), (1,)), ((), ()))
NN = (((1,), (0,)), ((), ()))
TN = (((0,), (0,)), ((), ()))


def dg(left, right, dims):
    return lax.dot_general(left, right, dims, preferred_element_type=f32)


def halves(ref, rows):
    return jnp.concatenate([ref[rows, :HEAD_SIZE], ref[rows, HEAD_SIZE:]], axis=0)


def as_rows(column):
    return jnp.broadcast_to(column, (column.shape[0], HEAD_SIZE)).T[0:1, :]


def attend_body(causal, last, flags, q_ref, kv_ref, qbit_ref, kbit_ref, *refs):
    if last:
        acc_in, tot_in, logit_ref, attn_ref, mixed_ref, lse_ref, acc, tot = refs
    else:
        acc_out, tot_out, acc, tot = refs
    qb = pl.program_id(0)
    bq = q_ref.shape[0]
    nk, _, bk = kbit_ref.shape
    q = halves(q_ref, slice(None))
    acc[...] = jnp.zeros_like(acc)
    tot[...] = jnp.zeros_like(tot)

    def step(kb, masked):
        rows = pl.ds(pl.multiple_of(kb * bk, bk), bk)
        s = dg(q, kv_ref[rows, :HEAD_SIZE], NT) * (LOG2E * SCORE_SCALE)
        if masked:
            seen = (qbit_ref[...] & kbit_ref[kb]) != 0
            if causal:
                at = lax.broadcasted_iota(jnp.int32, (bq, bk), 1) + kb * bk
                row = lax.broadcasted_iota(jnp.int32, (bq, bk), 0) + qb * bq
                seen = seen & (at <= row)
            s = jnp.where(jnp.concatenate([seen, seen], axis=0), s, -1e30)
        p = jnp.exp2(s)
        part = p[:, 0:128]
        for i in range(1, bk // 128):
            part = part + p[:, i * 128 : (i + 1) * 128]
        tot[...] += part
        acc[...] += dg(p.astype(bf), kv_ref[rows, HEAD_SIZE:], NN)

    def body(kb, _):
        flag = flags[qb, kb]
        pl.when(flag == 1)(lambda: step(kb, True))
        pl.when(flag == 2)(lambda: step(kb, False))
        return 0

    lax.fori_loop(0, nk, body, 0)
    total = jnp.sum(tot[...], axis=1, keepdims=True)
    if not last:
        acc_out[:, :HEAD_SIZE] = acc[:bq, :]
        acc_out[:, HEAD_SIZE:] = acc[bq:, :]
        tot_out[...] = jnp.concatenate([total[:bq], total[bq:]], axis=1)
    else:
        for h in range(2):
            rows = slice(h * bq, (h + 1) * bq)
            cols = slice(h * HEAD_SIZE, (h + 1) * HEAD_SIZE)
            sums = total[rows] + tot_in[:, h : h + 1]
            out = (acc[rows, :] + acc_in[:, cols]) / sums
            attn_ref[:, cols] = out
            mixed_ref[:, cols] = (out * jax.nn.sigmoid(logit_ref[:, h : h + 1])).astype(bf)
            lse_ref[h : h + 1, :] = as_rows(jnp.log2(sums))


def attend(causal, flags, q, kv, qbit, kbit, earlier=None):
    T = q.shape[0]
    N = kv.shape[0]
    nk = N // BK
    W = 2 * HEAD_SIZE
    blk = lambda w, j=0: pl.BlockSpec((BQ, w), lambda i, f: (i, j))
    last = earlier is not None
    in_specs = [
        blk(W),
        pl.BlockSpec((N, W), lambda i, f: (0, 0)),
        blk(1),
        pl.BlockSpec((nk, 1, BK), lambda i, f: (0, 0, 0)),
    ]
    if last:
        acc, tot, raw = earlier
        extra = [acc, tot, raw]
        in_specs += [blk(W), blk(2), blk(HEAD_SIZE, raw.shape[1] // HEAD_SIZE - 1)]
        out_specs = [blk(W), blk(W), pl.BlockSpec((2, BQ), lambda i, f: (0, i))]
        out_shape = [
            jax.ShapeDtypeStruct((T, W), f32),
            jax.ShapeDtypeStruct((T, W), bf),
            jax.ShapeDtypeStruct((2, T), f32),
        ]
    else:
        extra = []
        out_specs = [blk(W), blk(2)]
        out_shape = [jax.ShapeDtypeStruct((T, W), f32), jax.ShapeDtypeStruct((T, 2), f32)]
    return pl.pallas_call(
        partial(attend_body, causal, last),
        grid_spec=pltpu.PrefetchScalarGridSpec(
            num_scalar_prefetch=1,
            grid=(T // BQ,),
            in_specs=in_specs,
            out_specs=out_specs,
            scratch_shapes=[pltpu.VMEM((2 * BQ, HEAD_SIZE), f32), pltpu.VMEM((2 * BQ, HEAD_SIZE), f32)],
        ),
        out_shape=out_shape,
        cost_estimate=pl.CostEstimate(
            flops=(2 if causal else 4) * T * N * W, bytes_accessed=8 << 20, transcendentals=T * N * (1 if causal else 2)
        ),
        name="attend_own" if causal else "attend_earlier",
    )(flags, q, kv, qbit, kbit, *extra)


def attend_back_body(causal, flags, q_ref, g_ref, kv_ref, qbit_ref, kbit_ref, lse_ref, del_ref, *refs):
    if causal:
        dq_in, dq_ref, dkv_ref, dk_acc, dv_acc = refs
    else:
        dq_ref, dkv_ref, dk_acc, dv_acc = refs
    kb = pl.program_id(0)
    bk = kv_ref.shape[0]
    T = q_ref.shape[0]
    bq = BQ

    @pl.when(kb == 0)
    def _():
        if causal:
            dq_ref[...] = dq_in[...]
        else:
            dq_ref[...] = jnp.zeros_like(dq_ref)

    dk_acc[...] = jnp.zeros_like(dk_acc)
    dv_acc[...] = jnp.zeros_like(dv_acc)

    def line(ref, rows):
        return jnp.concatenate([ref[0:1, rows], ref[1:2, rows]], axis=1)

    def step(qb, masked):
        rows = pl.ds(pl.multiple_of(qb * bq, bq), bq)
        q = halves(q_ref, rows)
        g = halves(g_ref, rows)
        k = kv_ref[:, :HEAD_SIZE]
        s = dg(k, q, NT) * (LOG2E * SCORE_SCALE) - line(lse_ref, rows)
        if masked:
            seen = (kbit_ref[...] & qbit_ref[0:1, rows]) != 0
            if causal:
                at = lax.broadcasted_iota(jnp.int32, (bk, bq), 0) + kb * bk
                row = lax.broadcasted_iota(jnp.int32, (bk, bq), 1) + qb * bq
                seen = seen & (at <= row)
            s = jnp.where(jnp.concatenate([seen, seen], axis=1), s, -1e30)
        p = jnp.exp2(s)
        dv_acc[...] += dg(p.astype(bf), g, NN)
        dp = dg(kv_ref[:, HEAD_SIZE:], g, NT)
        ds = (p * (dp - line(del_ref, rows))).astype(bf)
        dk_acc[...] += dg(ds, q, NN)
        dq = dg(ds, k, TN)
        dq_ref[rows, :HEAD_SIZE] += dq[:bq]
        dq_ref[rows, HEAD_SIZE:] += dq[bq:]

    def body(qb, _):
        flag = flags[qb, kb]
        pl.when(flag == 1)(lambda: step(qb, True))
        pl.when(flag == 2)(lambda: step(qb, False))
        return 0

    lax.fori_loop(0, T // bq, body, 0)
    dkv_ref[:, :HEAD_SIZE] = (dk_acc[...] * SCORE_SCALE).astype(dkv_ref.dtype)
    dkv_ref[:, HEAD_SIZE:] = dv_acc[...].astype(dkv_ref.dtype)


def attend_back(causal, flags, q, g, kv, qbit, kbit, lse, delta, dq=None):
    T = q.shape[0]
    N = kv.shape[0]
    W = 2 * HEAD_SIZE
    whole = lambda *s: pl.BlockSpec(s, lambda i, f: (0,) * len(s))
    along = lambda w: pl.BlockSpec((BK, w), lambda i, f: (i, 0))
    in_specs = [whole(T, W), whole(T, W), along(W), whole(1, T), along(1), whole(2, T), whole(2, T)]
    extra = []
    if causal:
        in_specs.append(whole(T, W))
        extra = [dq]
    return pl.pallas_call(
        partial(attend_back_body, causal),
        grid_spec=pltpu.PrefetchScalarGridSpec(
            num_scalar_prefetch=1,
            grid=(N // BK,),
            in_specs=in_specs,
            out_specs=[whole(T, W), along(W)],
            scratch_shapes=[pltpu.VMEM((BK, HEAD_SIZE), f32), pltpu.VMEM((BK, HEAD_SIZE), f32)],
        ),
        out_shape=[jax.ShapeDtypeStruct((T, W), f32), jax.ShapeDtypeStruct((N, W), f32 if causal else bf)],
        cost_estimate=pl.CostEstimate(
            flops=(5 if causal else 10) * T * N * W, bytes_accessed=12 << 20, transcendentals=T * N * (1 if causal else 2)
        ),
        name="attend_own_back" if causal else "attend_earlier_back",
    )(flags, q, g, kv, qbit, kbit, lse, delta, *extra)


def turn(values):
    return pltpu.roll(values, HEAD_SIZE // 2, 1)


def prepare_body(x_ref, w_ref, cos_ref, sin_ref, gain_ref, raw_ref, q_ref, kv_ref):
    raw_ref[...] = dg(x_ref[...], w_ref[...], NN)
    for i in range(3):
        cols = slice(i * HEAD_SIZE, (i + 1) * HEAD_SIZE)
        u = raw_ref[:, cols]
        r = lax.rsqrt(jnp.mean(u * u, axis=-1, keepdims=True) + EPS)
        n = u * r * gain_ref[(1 if i == 2 else 0) : (2 if i == 2 else 1), :]
        out = (n * cos_ref[...] + turn(n) * sin_ref[...]).astype(bf)
        if i < 2:
            q_ref[:, cols] = out
        else:
            kv_ref[:, :HEAD_SIZE] = out
    kv_ref[:, HEAD_SIZE:] = raw_ref[:, 3 * HEAD_SIZE : 4 * HEAD_SIZE].astype(bf)


def prepare(x, w, cos, sin, gains):
    T, depth = x.shape
    width = w.shape[1]
    blk = lambda w: pl.BlockSpec((BQ, w), lambda i: (i, 0))
    whole = lambda *s: pl.BlockSpec(s, lambda i: (0, 0))
    pair = jax.ShapeDtypeStruct((T, 2 * HEAD_SIZE), bf)
    return pl.pallas_call(
        prepare_body,
        grid=(T // BQ,),
        in_specs=[blk(depth), whole(depth, width), blk(HEAD_SIZE), blk(HEAD_SIZE), whole(2, HEAD_SIZE)],
        out_specs=[blk(width), blk(2 * HEAD_SIZE), blk(2 * HEAD_SIZE)],
        out_shape=[jax.ShapeDtypeStruct((T, width), f32), pair, pair],
        cost_estimate=pl.CostEstimate(flops=2 * T * depth * width, bytes_accessed=T * 640 * 12, transcendentals=T),
        name="prepare_heads",
    )(x, w, cos, sin, gains)


def prepare_back_body(raw_ref, cos_ref, sin_ref, gain_ref, dq_ref, dkv_ref, back_ref, dlogit_ref, out_ref, sums_ref):
    @pl.when(pl.program_id(0) == 0)
    def _():
        sums_ref[...] = jnp.zeros_like(sums_ref)

    sent = lax.axis_index("dp") // GROUP % 2 == 0
    back = jnp.where(sent, back_ref[...].astype(f32), 0.0)
    for i in range(3):
        cols = slice(i * HEAD_SIZE, (i + 1) * HEAD_SIZE)
        if i < 2:
            w = dq_ref[:, cols] * SCORE_SCALE
        else:
            w = dkv_ref[:, :HEAD_SIZE] + back[:, :HEAD_SIZE]
        u = raw_ref[:, cols]
        j = 1 if i == 2 else 0
        r = lax.rsqrt(jnp.mean(u * u, axis=-1, keepdims=True) + EPS)
        w = w * cos_ref[...] + turn(w * sin_ref[...])
        sums_ref[j : j + 1, :] += jnp.sum(w * u * r, axis=0, keepdims=True)
        w = w * gain_ref[j : j + 1, :]
        out_ref[:, cols] = (r * w - u * (r * r * r * jnp.mean(w * u, axis=-1, keepdims=True))).astype(bf)
    out_ref[:, 3 * HEAD_SIZE : 4 * HEAD_SIZE] = (dkv_ref[:, HEAD_SIZE:] + back[:, HEAD_SIZE:]).astype(bf)
    out_ref[:, 4 * HEAD_SIZE :] = dlogit_ref[...]


def prepare_back(raw, cos, sin, gains, dq, dkv, back, dlogit):
    T, width = raw.shape
    W = 2 * HEAD_SIZE
    blk = lambda w: pl.BlockSpec((BQ, w), lambda i: (i, 0))
    flat = pl.BlockSpec((2, HEAD_SIZE), lambda i: (0, 0))
    return pl.pallas_call(
        prepare_back_body,
        grid=(T // BQ,),
        in_specs=[blk(width), blk(HEAD_SIZE), blk(HEAD_SIZE), flat, blk(W), blk(W), blk(W), blk(HEAD_SIZE)],
        out_specs=[blk(width), flat],
        out_shape=[jax.ShapeDtypeStruct((T, width), bf), jax.ShapeDtypeStruct((2, HEAD_SIZE), f32)],
        cost_estimate=pl.CostEstimate(flops=T * 8000, bytes_accessed=T * 640 * 10, transcendentals=T),
        name="prepare_heads_back",
    )(raw, cos, sin, gains, dq, dkv, back, dlogit)


def gate_back_rows(grad_mixed, attn_ref, logit_ref, ga_ref, dlogit_ref, del_ref):
    lanes = lax.broadcasted_iota(jnp.int32, dlogit_ref.shape, 1)
    grads = jnp.zeros(dlogit_ref.shape, f32)
    for h in range(2):
        cols = slice(h * HEAD_SIZE, (h + 1) * HEAD_SIZE)
        g = jax.nn.sigmoid(logit_ref[:, h : h + 1])
        gm = grad_mixed[:, cols]
        at = attn_ref[:, cols]
        ga = (gm * g).astype(bf)
        ga_ref[:, cols] = ga
        slope = jnp.sum(gm * at, axis=-1, keepdims=True) * (g * (1 - g))
        grads = jnp.where(lanes == h, slope, grads)
        del_ref[h : h + 1, :] = as_rows(jnp.sum(ga.astype(f32) * at, axis=-1, keepdims=True))
    dlogit_ref[...] = grads.astype(bf)


def hidden_back_body(dout_ref, down_ref, both_ref, out_ref):
    units = down_ref.shape[1]
    chunk = 256
    for j in range(units // chunk):
        left = slice(j * chunk, (j + 1) * chunk)
        right = slice(units + j * chunk, units + (j + 1) * chunk)
        grad = dg(dout_ref[...], down_ref[:, left], NN)
        gate = both_ref[:, left]
        s = jax.nn.sigmoid(gate)
        out_ref[:, left] = (grad * both_ref[:, right] * s * (1 + gate * (1 - s))).astype(bf)
        out_ref[:, right] = (grad * (gate * s)).astype(bf)


def hidden_back(dout, down, both):
    T, width = dout.shape
    units = down.shape[1]
    blk = lambda w: pl.BlockSpec((2 * BQ, w), lambda i: (i, 0))
    return pl.pallas_call(
        hidden_back_body,
        grid=(T // (2 * BQ),),
        in_specs=[blk(width), pl.BlockSpec((width, units), lambda i: (0, 0)), blk(2 * units)],
        out_specs=blk(2 * units),
        out_shape=jax.ShapeDtypeStruct((T, 2 * units), bf),
        cost_estimate=pl.CostEstimate(flops=2 * T * width * units, bytes_accessed=T * units * 30, transcendentals=T * units),
        name="hidden_back",
    )(dout, down, both)


GROUP = 4
MESH = pl.DeviceIdType.MESH
QUICK = pl.CostEstimate(flops=0, bytes_accessed=1 << 16, transcendentals=0)

def places():
    dp = lax.axis_index("dp"); c = lax.axis_index("mp")
    t = dp % GROUP
    base = dp - t
    tx = t + 1 - 2 * (t % 2)
    ty = t + 2 - 4 * (t // 2)
    td = 3 - t
    return base, t, tx, ty, td, c

def greet(devices):
    barrier = pltpu.get_barrier_semaphore()
    for device in devices:
        pl.semaphore_signal(barrier, inc=1, device_id=device, device_id_type=MESH)
    pl.semaphore_wait(barrier, len(devices))

def gather_steps(x_ref, out_ref, send, recv, local):
    base, t, tx, ty, td, c = places()
    share = x_ref.shape[0]
    half = share // 2
    xdev, ydev, mate = (base + tx, c), (base + ty, c), (base + t, 1 - c)
    greet([xdev, ydev, mate])

    def spot(who, part=None):
        start = (2 * who + c) * share
        if part is None:
            return out_ref.at[pl.ds(pl.multiple_of(start, share), share)]
        return out_ref.at[pl.ds(pl.multiple_of(start + part * half, half), half)]

    def copy(kind, src, dst, device):
        one = pltpu.make_async_remote_copy(
            src_ref=src, dst_ref=dst, send_sem=send.at[kind], recv_sem=recv.at[kind], device_id=device, device_id_type=MESH
        )
        one.start()
        return one

    own = pltpu.make_async_copy(x_ref, spot(t), local)
    own.start()
    mine = [x_ref.at[pl.ds(0, half)], x_ref.at[pl.ds(half, half)]]
    k = {}
    k[2] = copy(2, mine[0], spot(t, 0), ydev)
    k[1] = copy(1, mine[1], spot(t, 1), xdev)
    k[3] = copy(3, mine[1], spot(t, 1), ydev)
    k[0] = copy(0, mine[0], spot(t, 0), xdev)
    k[6] = copy(6, x_ref, spot(t), mate)
    yield
    k[2].wait_recv()
    k[4] = copy(4, spot(ty, 0), spot(ty, 0), xdev)
    k[9] = copy(9, spot(ty, 0), spot(ty, 0), mate)
    k[1].wait_recv()
    k[5] = copy(5, spot(tx, 1), spot(tx, 1), ydev)
    k[8] = copy(8, spot(tx, 1), spot(tx, 1), mate)
    yield
    k[0].wait_recv()
    k[7] = copy(7, spot(tx, 0), spot(tx, 0), mate)
    k[3].wait_recv()
    k[10] = copy(10, spot(ty, 1), spot(ty, 1), mate)
    k[4].wait_recv()
    k[11] = copy(11, spot(td, 0), spot(td, 0), mate)
    k[5].wait_recv()
    k[12] = copy(12, spot(td, 1), spot(td, 1), mate)
    for kind in range(6, 13):
        k[kind].wait_recv()
    for kind in range(13):
        k[kind].wait_send()
    own.wait()
    yield


def gather_body(x_ref, out_ref, send, recv, local):
    for _ in gather_steps(x_ref, out_ref, send, recv, local):
        pass


def gather_sems():
    return [pltpu.SemaphoreType.DMA((13,)), pltpu.SemaphoreType.DMA((13,)), pltpu.SemaphoreType.DMA]


def gather_group(x):
    share, width = x.shape
    return pl.pallas_call(
        gather_body,
        out_shape=jax.ShapeDtypeStruct((share * GROUP * 2, width), x.dtype),
        in_specs=[pl.BlockSpec(memory_space=pltpu.VMEM)],
        out_specs=pl.BlockSpec(memory_space=pl.ANY),
        scratch_shapes=gather_sems(),
        compiler_params=pltpu.CompilerParams(collective_id=1, has_side_effects=True),
        cost_estimate=QUICK,
        name="gather_group",
    )(x)


def gather_attend_body(
    x_ref, q_ref, kv_ref, qbit_ref, kbit_ref, acc_in, tot_in, raw_ref, out_ref, attn_ref, mixed_ref, lse_ref,
    acc, tot, logit, fetch, send, recv, local
):
    edge = raw_ref.shape[1] - HEAD_SIZE
    logits = pltpu.make_async_copy(raw_ref.at[:, pl.ds(edge, HEAD_SIZE)], logit, fetch)
    logits.start()
    steps = gather_steps(x_ref, out_ref, send, recv, local)
    next(steps)
    logits.wait()
    nk, _, bk = kbit_ref.shape

    def block(qb, _):
        here = pl.ds(pl.multiple_of(qb * BQ, BQ), BQ)
        q = halves(q_ref, here)
        acc[...] = jnp.zeros_like(acc)
        tot[...] = jnp.zeros_like(tot)

        def step(kb, _):
            rows = pl.ds(pl.multiple_of(kb * bk, bk), bk)
            s = dg(q, kv_ref[rows, :HEAD_SIZE], NT) * (LOG2E * SCORE_SCALE)
            seen = (qbit_ref[here, :] & kbit_ref[kb]) != 0
            p = jnp.exp2(jnp.where(jnp.concatenate([seen, seen], axis=0), s, -1e30))
            part = p[:, 0:128]
            for i in range(1, bk // 128):
                part = part + p[:, i * 128 : (i + 1) * 128]
            tot[...] += part
            acc[...] += dg(p.astype(bf), kv_ref[rows, HEAD_SIZE:], NN)
            return 0

        lax.fori_loop(0, nk, step, 0)
        total = jnp.sum(tot[...], axis=1, keepdims=True)
        for h in range(2):
            rows = slice(h * BQ, (h + 1) * BQ)
            cols = slice(h * HEAD_SIZE, (h + 1) * HEAD_SIZE)
            sums = total[rows] + tot_in[here, h : h + 1]
            out = (acc[rows, :] + acc_in[here, cols]) / sums
            attn_ref[here, cols] = out
            mixed_ref[here, cols] = (out * jax.nn.sigmoid(logit[here, h : h + 1])).astype(bf)
            lse_ref[h : h + 1, here] = as_rows(jnp.log2(sums))
        return 0

    blocks = q_ref.shape[0] // BQ
    lax.fori_loop(0, 3 * blocks // 8, block, 0)
    next(steps)
    lax.fori_loop(3 * blocks // 8, blocks, block, 0)
    next(steps)


def gather_attend(x, q, kv, qbit, kbit, acc, tot, raw, key):
    share, width = x.shape
    T, W = q.shape
    vmem = pl.BlockSpec(memory_space=pltpu.VMEM)
    anywhere = pl.BlockSpec(memory_space=pl.ANY)
    shape = jax.ShapeDtypeStruct
    return pl.pallas_call(
        gather_attend_body,
        out_shape=[shape((share * GROUP * 2, width), bf), shape((T, W), f32), shape((T, W), bf), shape((2, T), f32)],
        in_specs=[vmem] * 7 + [anywhere],
        out_specs=[anywhere] + [vmem] * 3,
        scratch_shapes=[
            pltpu.VMEM((2 * BQ, HEAD_SIZE), f32),
            pltpu.VMEM((2 * BQ, HEAD_SIZE), f32),
            pltpu.VMEM((T, HEAD_SIZE), f32),
            pltpu.SemaphoreType.DMA,
        ]
        + gather_sems(),
        compiler_params=pltpu.CompilerParams(collective_id=key, has_side_effects=True, vmem_limit_bytes=40 << 20),
        cost_estimate=QUICK,
        name="gather_attend",
    )(x, q, kv, qbit, kbit, acc, tot, raw)


def own_back(q_ref, g_ref, kv_ref, qbit_ref, kbit_ref, lse_ref, del_ref, dq_in, dq_ref, dkv_ref, dk_acc, dv_acc):
    dq_ref[...] = dq_in[...]

    def line(ref, rows):
        return jnp.concatenate([ref[0:1, rows], ref[1:2, rows]], axis=1)

    def keys(kb, _):
        here = pl.ds(pl.multiple_of(kb * BK, BK), BK)
        dk_acc[...] = jnp.zeros_like(dk_acc)
        dv_acc[...] = jnp.zeros_like(dv_acc)

        def step(qb, _):
            rows = pl.ds(pl.multiple_of(qb * BQ, BQ), BQ)
            q = halves(q_ref, rows)
            g = halves(g_ref, rows)
            k = kv_ref[here, :HEAD_SIZE]
            s = dg(k, q, NT) * (LOG2E * SCORE_SCALE) - line(lse_ref, rows)
            at = lax.broadcasted_iota(jnp.int32, (BK, BQ), 0) + kb * BK
            row = lax.broadcasted_iota(jnp.int32, (BK, BQ), 1) + qb * BQ
            seen = ((kbit_ref[here, :] & qbit_ref[0:1, rows]) != 0) & (at <= row)
            p = jnp.exp2(jnp.where(jnp.concatenate([seen, seen], axis=1), s, -1e30))
            dv_acc[...] += dg(p.astype(bf), g, NN)
            dp = dg(kv_ref[here, HEAD_SIZE:], g, NT)
            ds = (p * (dp - line(del_ref, rows))).astype(bf)
            dk_acc[...] += dg(ds, q, NN)
            dq = dg(ds, k, TN)
            dq_ref[rows, :HEAD_SIZE] += dq[:BQ]
            dq_ref[rows, HEAD_SIZE:] += dq[BQ:]
            return 0

        lax.fori_loop(kb * (BK // BQ), q_ref.shape[0] // BQ, step, 0)
        dkv_ref[here, :HEAD_SIZE] = dk_acc[...] * SCORE_SCALE
        dkv_ref[here, HEAD_SIZE:] = dv_acc[...]
        return 0

    lax.fori_loop(0, kv_ref.shape[0] // BK, keys, 0)


def reduce_body(side, back, left_ref, right_ref, *refs):
    if side:
        tall_ref, out_ref, grad_ref, tall, grad, refs = *refs[:5], refs[5:]
    elif back:
        pair_ref, q_ref, g_ref, kv_ref, qbit_ref, kbit_ref, lse_ref, del_ref, dq_in, refs = *refs[:9], refs[9:]
        out_ref, pair_out, dq_ref, dkv_ref, dk_acc, dv_acc, refs = *refs[:6], refs[6:]
    else:
        out_ref, refs = refs[0], refs[1:]
    left, right, fars, near, mates, sums, xin, yin, zin, turned, fetch, send, recv = refs
    base, t, tx, ty, td, c = places()
    share = out_ref.shape[0]
    half = share // 2
    chunk = right.shape[0] // 4
    xdev, ydev, mate = (base + tx, c), (base + ty, c), (base + t, 1 - c)
    order = [td, tx, ty, t]
    lefts, rights, talls = [], [], []
    for i, who in enumerate(order):
        for j, core in enumerate((1 - c, c)):
            rows = pl.ds(pl.multiple_of((2 * who + core) * share, share), share)
            n = 2 * i + j
            place = pl.ds(n * share, share)
            lefts.append(pltpu.make_async_copy(left_ref.at[rows], left.at[place], fetch.at[n]))
            if side:
                talls.append(pltpu.make_async_copy(tall_ref.at[rows], tall.at[place], fetch.at[12 + n]))
    for j in range(4):
        rows = pl.ds(j * chunk, chunk)
        rights.append(pltpu.make_async_copy(right_ref.at[rows], right.at[rows], fetch.at[8 + j]))
    for one in lefts[:2] + rights + lefts[2:] + talls:
        one.start()
    friends = [xdev, ydev, mate]
    if back:
        late = lax.axis_index("dp") // GROUP % 2
        friends.append((lax.axis_index("dp") + (GROUP - 2 * GROUP * late), c))
    greet(friends)
    if back:
        pair = pltpu.make_async_remote_copy(
            src_ref=pair_ref,
            dst_ref=pair_out,
            send_sem=send.at[10],
            recv_sem=recv.at[10],
            device_id=friends[-1],
            device_id_type=MESH,
        )
        keep = pltpu.make_async_copy(pair_ref, pair_out, fetch.at[12])

        @pl.when(late == 1)
        def _():
            pair.start()
            keep.start()

    def copy(kind, src, dst, device):
        return pltpu.make_async_remote_copy(
            src_ref=src, dst_ref=dst, send_sem=send.at[kind], recv_sem=recv.at[kind], device_id=device, device_id_type=MESH
        )

    def product(n, dst):
        lefts[n].wait()

        def go(j, _):
            rows = pl.ds(pl.multiple_of(j * chunk, chunk), chunk)
            dst[:, rows] = dg(left[n * share : (n + 1) * share, :], right[rows, :], NT).astype(dst.dtype)
            return 0

        if n == 0:
            for j in range(4):
                rights[j].wait()
                go(j, 0)
        else:
            lax.fori_loop(0, 4, go, 0)

    def add(dst, one, two):
        step = 16

        def go(i, _):
            rows = pl.ds(pl.multiple_of(i * step, step), step)
            dst[rows, :] = (one[rows, :].astype(f32) + two[rows, :].astype(f32)).astype(dst.dtype)
            return 0

        lax.fori_loop(0, dst.shape[0] // step, go, 0)

    A, B = pl.ds(0, half), pl.ds(half, half)
    over, k = [], {}

    def join(i):
        over[i].wait_recv()
        add(sums.at[i], near.at[i], mates.at[i])
        if i == 0:
            k[4] = copy(4, sums.at[0, A], xin.at[1], xdev)
            k[5] = copy(5, sums.at[0, B], yin.at[1], ydev)
            k[4].start()
            k[5].start()
        if i == 1:
            k[6] = copy(6, sums.at[1, A], xin.at[0], xdev)
            k[6].start()
        if i == 2:
            k[7] = copy(7, sums.at[2, B], yin.at[0], ydev)
            k[7].start()

    for i in range(4):
        product(2 * i, fars.at[i])
        over.append(copy(i, fars.at[i], mates.at[i], mate))
        over[i].start()
        product(2 * i + 1, near.at[i])
        if i:
            join(i - 1)
    join(3)
    k[4].wait_recv()
    add(turned.at[0], sums.at[2, A], xin.at[1])
    k[8] = copy(8, turned.at[0], zin.at[0], ydev)
    k[8].start()
    k[5].wait_recv()
    add(turned.at[1], sums.at[1, B], yin.at[1])
    k[9] = copy(9, turned.at[1], zin.at[1], xdev)
    k[9].start()
    if side:
        for one in talls:
            one.wait()

        def inner_product(j, _):
            cols = pl.ds(pl.multiple_of(j * 256, 256), 256)
            grad[cols, :] = dg(tall[:, cols], left[...], TN).astype(bf)
            return 0

        lax.fori_loop(0, tall.shape[1] // 256, inner_product, 0)
        put = pltpu.make_async_copy(grad, grad_ref, fetch.at[20])
        put.start()
    if back:
        own_back(q_ref, g_ref, kv_ref, qbit_ref, kbit_ref, lse_ref, del_ref, dq_in, dq_ref, dkv_ref, dk_acc, dv_acc)
    k[6].wait_recv()
    add(out_ref.at[A], sums.at[3, A], xin.at[0])
    k[7].wait_recv()
    add(out_ref.at[B], sums.at[3, B], yin.at[0])
    k[8].wait_recv()
    add(out_ref.at[A], out_ref.at[A], zin.at[0])
    k[9].wait_recv()
    add(out_ref.at[B], out_ref.at[B], zin.at[1])
    for i in range(4):
        over[i].wait_send()
    for kind in range(4, 10):
        k[kind].wait_send()
    if side:
        put.wait()
    if back:

        @pl.when(late == 1)
        def _():
            pair.wait_send()
            keep.wait()

        @pl.when(late == 0)
        def _():
            pair.wait_recv()


def product_reduce(left, right, key, tall=None, back=()):
    rows, depth = left.shape
    side = tall is not None
    width = right.shape[0]
    share = rows // (2 * GROUP)
    half = share // 2
    block = lambda n, r: pltpu.VMEM((n, r, width), bf)
    anywhere = pl.BlockSpec(memory_space=pl.ANY)
    outs, out_specs = [jax.ShapeDtypeStruct((share, width), f32)], [pl.BlockSpec(memory_space=pltpu.VMEM)]
    ins, extra = [left, right], []
    if side:
        ins.append(tall)
        outs.append(jax.ShapeDtypeStruct((tall.shape[1], depth), bf))
        out_specs.append(anywhere)
        extra = [pltpu.VMEM(tall.shape, bf), pltpu.VMEM((tall.shape[1], depth), bf)]
    in_specs = [anywhere] * len(ins)
    if back:
        ins += back
        in_specs += [pl.BlockSpec(memory_space=pltpu.VMEM)] * len(back)
        pair, dq = back[0], back[-1]
        outs += [jax.ShapeDtypeStruct(pair.shape, bf)] + [jax.ShapeDtypeStruct(dq.shape, f32)] * 2
        out_specs += [anywhere] + [pl.BlockSpec(memory_space=pltpu.VMEM)] * 2
        extra = [pltpu.VMEM((BK, HEAD_SIZE), f32), pltpu.VMEM((BK, HEAD_SIZE), f32)]
    result = pl.pallas_call(
        partial(reduce_body, side, bool(back)),
        out_shape=outs,
        in_specs=in_specs,
        out_specs=out_specs,
        scratch_shapes=extra
        + [
            pltpu.VMEM((rows, depth), bf),
            pltpu.VMEM((width, depth), bf),
            block(4, share),
            block(4, share),
            block(4, share),
            block(4, share),
            block(2, half),
            block(2, half),
            block(2, half),
            block(2, half),
            pltpu.SemaphoreType.DMA((21,)),
            pltpu.SemaphoreType.DMA((11,)),
            pltpu.SemaphoreType.DMA((11,)),
        ],
        compiler_params=pltpu.CompilerParams(collective_id=key, has_side_effects=True, vmem_limit_bytes=60 << 20),
        cost_estimate=QUICK,
        name="product_reduce",
    )(*ins)
    return result if side or back else result[0]


def gather_product_body(glu, x_ref, w_ref, *refs):
    if glu:
        full_ref, y_ref, hidden_ref, hs, ys, refs = *refs[:5], refs[5:]
    else:
        attn_ref, raw_ref, full_ref, ga_ref, dlogit_ref, del_ref, attn, logit, gs, ds, es, refs = *refs[:11], refs[11:]
    buf, w, fetch, put_x, put_y, send, recv = refs
    base, t, tx, ty, td, c = places()
    share = x_ref.shape[0]
    half = share // 2
    width = w.shape[1]
    xdev, ydev, mate = (base + tx, c), (base + ty, c), (base + t, 1 - c)
    weights = [pltpu.make_async_copy(w_ref, w, fetch.at[0])]
    if not glu:
        edge = raw_ref.shape[1] - HEAD_SIZE
        weights.append(pltpu.make_async_copy(attn_ref, attn, fetch.at[1]))
        weights.append(pltpu.make_async_copy(raw_ref.at[:, pl.ds(edge, HEAD_SIZE)], logit, fetch.at[2]))
    for one in weights:
        one.start()
    greet([xdev, ydev, mate])

    def unit(who, core):
        return pl.ds(pl.multiple_of((2 * who + core) * share, share), share)

    def spot(who, part):
        start = (2 * who + c) * share + part * half
        return buf.at[pl.ds(pl.multiple_of(start, half), half)]

    def copy(kind, src, dst, device):
        one = pltpu.make_async_remote_copy(
            src_ref=src, dst_ref=dst, send_sem=send.at[kind], recv_sem=recv.at[kind], device_id=device, device_id_type=MESH
        )
        one.start()
        return one

    mine = [x_ref.at[pl.ds(0, half)], x_ref.at[pl.ds(half, half)]]
    k, puts = {}, []
    k[2] = copy(2, mine[0], spot(t, 0), ydev)
    k[1] = copy(1, mine[1], spot(t, 1), xdev)
    k[3] = copy(3, mine[1], spot(t, 1), ydev)
    k[0] = copy(0, mine[0], spot(t, 0), xdev)
    k[6] = copy(6, x_ref, buf.at[unit(t, c)], mate)
    for one in weights:
        one.wait()

    def work(n, src, who, core):
        rows = unit(who, core)
        slot = n % 2
        one = pltpu.make_async_copy(src, full_ref.at[rows], put_x.at[n])
        one.start()
        if n >= 2:
            for old in puts[n - 2][1:]:
                old.wait()
        if glu:
            chunk = 256

            def go(j, _):
                left = pl.ds(pl.multiple_of(j * chunk, chunk), chunk)
                right = pl.ds(pl.multiple_of(width // 2 + j * chunk, chunk), chunk)
                gate = dg(src[...], w[:, left], NN)
                up = dg(src[...], w[:, right], NN)
                ys[slot, :, left] = gate
                ys[slot, :, right] = up
                hs[slot, :, left] = (gate * jax.nn.sigmoid(gate) * up).astype(bf)
                return 0

            lax.fori_loop(0, width // 2 // chunk, go, 0)
            outs = [
                one,
                pltpu.make_async_copy(ys.at[slot], y_ref.at[rows], put_y.at[n]),
                pltpu.make_async_copy(hs.at[slot], hidden_ref.at[rows], put_y.at[8 + n]),
            ]
        else:
            gm = dg(src[...], w[...], NN)
            gate_back_rows(gm, attn.at[rows], logit.at[rows], gs.at[slot], ds.at[slot], es.at[slot])
            outs = [
                one,
                pltpu.make_async_copy(gs.at[slot], ga_ref.at[rows], put_y.at[n]),
                pltpu.make_async_copy(ds.at[slot], dlogit_ref.at[rows], put_y.at[8 + n]),
                pltpu.make_async_copy(es.at[slot], del_ref.at[:, rows], put_y.at[16 + n]),
            ]
        for out in outs[1:]:
            out.start()
        puts.append(outs)

    def landed(who, core):
        return buf.at[unit(who, core)]

    work(0, x_ref, t, c)
    k[6].wait_recv()
    work(1, landed(t, 1 - c), t, 1 - c)
    k[2].wait_recv()
    k[4] = copy(4, spot(ty, 0), spot(ty, 0), xdev)
    k[9] = copy(9, spot(ty, 0), spot(ty, 0), mate)
    k[1].wait_recv()
    k[5] = copy(5, spot(tx, 1), spot(tx, 1), ydev)
    k[8] = copy(8, spot(tx, 1), spot(tx, 1), mate)
    k[0].wait_recv()
    k[7] = copy(7, spot(tx, 0), spot(tx, 0), mate)
    k[3].wait_recv()
    k[10] = copy(10, spot(ty, 1), spot(ty, 1), mate)
    work(2, landed(tx, c), tx, c)
    work(3, landed(ty, c), ty, c)
    k[7].wait_recv()
    k[8].wait_recv()
    work(4, landed(tx, 1 - c), tx, 1 - c)
    k[9].wait_recv()
    k[10].wait_recv()
    work(5, landed(ty, 1 - c), ty, 1 - c)
    k[4].wait_recv()
    k[11] = copy(11, spot(td, 0), spot(td, 0), mate)
    k[5].wait_recv()
    k[12] = copy(12, spot(td, 1), spot(td, 1), mate)
    work(6, landed(td, c), td, c)
    k[11].wait_recv()
    k[12].wait_recv()
    work(7, landed(td, 1 - c), td, 1 - c)
    for kind in range(13):
        k[kind].wait_send()
    for n, outs in enumerate(puts):
        outs[0].wait()
        if n >= 6:
            for out in outs[1:]:
                out.wait()


def gather_product(x, w, key, gated=None):
    share, depth = x.shape
    width = w.shape[1]
    rows = share * GROUP * 2
    anywhere = pl.BlockSpec(memory_space=pl.ANY)
    shape = jax.ShapeDtypeStruct
    if gated is None:
        gated = []
        outs = [shape((rows, width), f32), shape((rows, width // 2), bf)]
        extra = [pltpu.VMEM((2, share, width // 2), bf), pltpu.VMEM((2, share, width), f32)]
    else:
        outs = [shape((rows, width), bf), shape((rows, HEAD_SIZE), bf), shape((2, rows), f32)]
        extra = [
            pltpu.VMEM((rows, width), f32),
            pltpu.VMEM((rows, HEAD_SIZE), f32),
            pltpu.VMEM((2, share, width), bf),
            pltpu.VMEM((2, share, HEAD_SIZE), bf),
            pltpu.VMEM((2, 2, share), f32),
        ]
    outs = [shape((rows, depth), bf)] + outs
    return pl.pallas_call(
        partial(gather_product_body, not gated),
        out_shape=outs,
        in_specs=[pl.BlockSpec(memory_space=pltpu.VMEM)] + [anywhere] * (1 + len(gated)),
        out_specs=[anywhere] * len(outs),
        scratch_shapes=extra
        + [
            pltpu.VMEM((rows, depth), bf),
            pltpu.VMEM((depth, width), bf),
            pltpu.SemaphoreType.DMA((3,)),
            pltpu.SemaphoreType.DMA((8,)),
            pltpu.SemaphoreType.DMA((24,)),
            pltpu.SemaphoreType.DMA((13,)),
            pltpu.SemaphoreType.DMA((13,)),
        ],
        compiler_params=pltpu.CompilerParams(collective_id=key, has_side_effects=True, vmem_limit_bytes=48 << 20),
        cost_estimate=QUICK,
        name="gather_product",
    )(x, w, *gated)


def far_places():
    dp = lax.axis_index("dp")
    return dp // GROUP, lax.axis_size("dp") // GROUP


def far_friends():
    base, t, tx, ty, td, c = places()
    r, count = far_places()
    return [((r + i) % count * GROUP + t, c) for i in range(1, count)] + [(base + t, 1 - c)]


def small_copy(send, recv):
    def copy(kind, src, dst, device):
        one = pltpu.make_async_remote_copy(
            src_ref=src, dst_ref=dst, send_sem=send.at[kind], recv_sem=recv.at[kind], device_id=device, device_id_type=MESH
        )
        one.start()
        return one

    return copy


def spread(x_ref, out_ref, send, recv, local):
    base, t, tx, ty, td, c = places()
    r, count = far_places()
    copy = small_copy(send, recv)
    own = pltpu.make_async_copy(x_ref, out_ref.at[c, t, r], local)
    own.start()
    others = [(r + i) % count for i in range(1, count)]
    stage = [copy(i, x_ref, out_ref.at[c, t, r], (z * GROUP + t, c)) for i, z in enumerate(others)]
    own.wait()
    for one in stage:
        one.wait()
    stage = [copy(count - 1 + i, out_ref.at[c, t], out_ref.at[c, t], (base + who, c)) for i, who in enumerate([td, tx, ty])]
    yield
    for one in stage:
        one.wait()
    copy(count + 2, out_ref.at[c], out_ref.at[c], (base + t, 1 - c)).wait()
    yield


def collect(x_ref, out_ref, one_in, one_sum, two_in, two_sum, far_in, send, recv):
    base, t, tx, ty, td, c = places()
    r, count = far_places()
    copy = small_copy(send, recv)
    copy(0, x_ref.at[1 - c], one_in, (base + t, 1 - c)).wait()
    one_sum[...] = x_ref[c] + one_in[...]
    stage = [copy(1 + i, one_sum.at[who], two_in.at[i], (base + who, c)) for i, who in enumerate([td, tx, ty])]
    yield
    for one in stage:
        one.wait()
    two_sum[...] = one_sum[t] + two_in[0] + two_in[1] + two_in[2]
    others = [(r + i) % count for i in range(1, count)]
    stage = [copy(4 + i, two_sum.at[z], far_in.at[i], (z * GROUP + t, c)) for i, z in enumerate(others)]
    for one in stage:
        one.wait()
    total = two_sum[r]
    for i in range(count - 1):
        total = total + far_in[i]
    out_ref[...] = total
    yield


def small_scratch(tile, inward):
    count = lax.axis_size("dp") // GROUP
    sems = [pltpu.SemaphoreType.DMA((count + 3,)), pltpu.SemaphoreType.DMA((count + 3,))]
    if inward:
        return sems + [pltpu.SemaphoreType.DMA]
    shapes = [(GROUP, count), (GROUP, count), (3, count), (count,), (count - 1,)]
    return [pltpu.VMEM(shape + tile, f32) for shape in shapes] + sems


def trade_body(inward, widths, sender, side, small, *refs):
    base, t, tx, ty, td, c = places()
    partners = [td, tx, ty]
    friends = [(base + who, c) for who in partners]
    flat = [(i, sum(ws[:j]), w) for i, ws in enumerate(widths) for j, w in enumerate(ws)]
    count = len(flat)
    packed, loose = len(widths), count
    ins, refs = refs[: loose if inward else packed], refs[loose if inward else packed :]
    if sender is not None:
        pair_ref, refs = refs[0], refs[1:]
    if side:
        tall_ref, wide_ref, refs = *refs[:2], refs[2:]
    if small:
        small_ref, refs = refs[0], refs[1:]
    outs, refs = refs[: packed if inward else loose], refs[packed if inward else loose :]
    if sender is not None:
        pair_out, refs = refs[0], refs[1:]
    if side:
        grad_ref, refs = refs[0], refs[1:]
    if small:
        small_out, refs = refs[0], refs[1:]
    if side:
        tall, wide, grad, fetch, refs = *refs[:4], refs[4:]
    send, recv, local, *rest = refs
    if small:
        friends += far_friends()
    if sender is not None:
        late = lax.axis_index("dp") // GROUP % 2
        friends.append((lax.axis_index("dp") + (GROUP - 2 * GROUP * late), c))
    greet(friends)

    def block(ref, i, who):
        array, start, width = flat[i]
        return ref[array].at[who, :, pl.ds(start, width)]

    def column(ref, i, who):
        width = flat[i][2]
        return ref[i].at[:, pl.ds(pl.multiple_of(who * width, width), width)]

    if small:
        steps = (spread if inward else collect)(small_ref, small_out, *rest)
        next(steps)
    source, target = (column, block) if inward else (block, column)
    copies = []
    for j, who in enumerate(partners):
        for i in range(count):
            kind = j * count + i
            one = pltpu.make_async_remote_copy(
                src_ref=source(ins, i, who),
                dst_ref=target(outs, i, t),
                send_sem=send.at[kind],
                recv_sem=recv.at[kind],
                device_id=(base + who, c),
                device_id_type=MESH,
            )
            one.start()
            copies.append(one)
    if sender is not None:
        pair = pltpu.make_async_remote_copy(
            src_ref=pair_ref,
            dst_ref=pair_out,
            send_sem=send.at[3 * count],
            recv_sem=recv.at[3 * count],
            device_id=friends[-1],
            device_id_type=MESH,
        )
        keep = pltpu.make_async_copy(pair_ref, pair_out, local.at[count])

        @pl.when(late == sender)
        def _():
            pair.start()
            keep.start()

    owns = [pltpu.make_async_copy(source(ins, i, t), target(outs, i, t), local.at[i]) for i in range(count)]
    for own in owns:
        own.start()
    if side:
        loads = [pltpu.make_async_copy(tall_ref, tall, fetch.at[0]), pltpu.make_async_copy(wide_ref, wide, fetch.at[1])]
        for one in loads:
            one.start()
        for one in loads:
            one.wait()

        def inner_product(j, _):
            cols = pl.ds(pl.multiple_of(j * 256, 256), 256)
            grad[cols, :] = dg(tall[:, cols], wide[...], TN).astype(bf)
            return 0

        lax.fori_loop(0, tall.shape[1] // 256, inner_product, 0)
        put = pltpu.make_async_copy(grad, grad_ref, fetch.at[2])
        put.start()
    if small:
        next(steps)
    for one in copies:
        one.wait()
    for own in owns:
        own.wait()
    if side:
        put.wait()
    if sender is not None:

        @pl.when(late == sender)
        def _():
            pair.wait_send()
            keep.wait()

        @pl.when(late == 1 - sender)
        def _():
            pair.wait_recv()


def trade_call(inward, ins, outs, widths, key, pair=None, sender=None, side=(), small=None):
    vmem = pl.BlockSpec(memory_space=pltpu.VMEM)
    anywhere = pl.BlockSpec(memory_space=pl.ANY)
    count = sum(len(ws) for ws in widths)
    scratch = []
    if sender is not None:
        ins = list(ins) + [pair]
        outs = outs + [jax.ShapeDtypeStruct(pair.shape, bf)]
    if side:
        tall, wide = side
        grad = (tall.shape[1], wide.shape[1])
        outs = outs + [jax.ShapeDtypeStruct(grad, bf)]
        scratch = [pltpu.VMEM(tall.shape, bf), pltpu.VMEM(wide.shape, bf), pltpu.VMEM(grad, bf), pltpu.SemaphoreType.DMA((3,))]
    smalls = [] if small is None else [small]
    out_specs = [anywhere] * len(outs) + [vmem] * len(smalls)
    rest = []
    if smalls:
        tile = small.shape[-2:]
        result = (2, GROUP, lax.axis_size("dp") // GROUP) + tile if inward else tile
        outs = outs + [jax.ShapeDtypeStruct(result, f32)]
        rest = small_scratch(tile, inward)
    return pl.pallas_call(
        partial(trade_body, inward, widths, sender, bool(side), bool(smalls)),
        out_shape=outs,
        in_specs=[vmem] * len(ins) + [anywhere] * len(side) + [vmem] * len(smalls),
        out_specs=out_specs,
        scratch_shapes=scratch
        + [
            pltpu.SemaphoreType.DMA((3 * count + 1,)),
            pltpu.SemaphoreType.DMA((3 * count + 1,)),
            pltpu.SemaphoreType.DMA((count + 1,)),
        ]
        + rest,
        compiler_params=pltpu.CompilerParams(collective_id=key, has_side_effects=True),
        cost_estimate=QUICK,
        name="trade_group",
    )(*ins, *side, *smalls)


def trade_group(weights, key, pair=None, small=None):
    rows = weights[0].shape[0]
    widths = (tuple(w.shape[1] // GROUP for w in weights),)
    outs = [jax.ShapeDtypeStruct((GROUP, rows, sum(widths[0])), bf)]
    if pair is None:
        result = trade_call(True, weights, outs, widths, key, small=small)
        return result[0] if small is None else result
    return trade_call(True, weights, outs, widths, key, pair, 0)


def trade_back(grads, widths, key, pair=None, side=(), small=None):
    rows = grads[0].shape[1]
    outs = [jax.ShapeDtypeStruct((rows, GROUP * w), bf) for ws in widths for w in ws]
    return trade_call(False, grads, outs, widths, key, pair, None if pair is None else 1, side, small)


def row_norm(values, gain):
    scale = lax.rsqrt(jnp.mean(values * values, axis=-1, keepdims=True) + EPS)
    return values * scale * gain


def rope_tables(positions, width):
    half = width // 2
    lanes = jnp.arange(width, dtype=jnp.int32)
    freqs = THETA ** (-((lanes % half).astype(f32) / half))
    angle = positions.astype(f32) * freqs[None, :]
    return jnp.cos(angle), jnp.sin(angle) * jnp.where(lanes < half, -1.0, 1.0)[None, :]


def tables_body(group_tokens, early, seg_count, parents, lengths, pos_ref, qcol_ref, qline_ref, kline_ref, kcol_ref, flags, key_any):
    step = pl.program_id(0)
    first = lax.axis_index("dp") // GROUP * group_tokens
    tree = first // TREE_TOKENS
    begin = first - tree * TREE_TOKENS
    size = [lengths[tree, seg] for seg in range(seg_count)]
    starts, bits, depth = [jnp.int32(0)], [jnp.int32(1)], [jnp.int32(0)]
    for seg in range(1, seg_count):
        starts.append(starts[-1] + size[seg - 1])
        parent = parents[tree, seg]
        above, deep = bits[0], depth[0] + size[0]
        for p in range(1, seg):
            above = jnp.where(parent == p, bits[p], above)
            deep = jnp.where(parent == p, depth[p] + size[p], deep)
        bits.append(above | (1 << seg))
        depth.append(deep)
    powers = [jnp.int32(1 << seg) for seg in range(seg_count)]

    def by_segment(offsets, values):
        out = jnp.zeros_like(offsets) + values[0]
        for start, value in zip(starts[1:], values[1:]):
            out = jnp.where(offsets >= start, value, out)
        return out

    q_first = begin + step * BQ
    k_first = begin - early + step * BK
    column = lax.broadcasted_iota(jnp.int32, (BQ, 1), 0) + q_first
    pos_ref[...] = by_segment(column, [d - s for d, s in zip(depth, starts)]) + column
    qcol_ref[...] = by_segment(column, bits)
    qline_ref[...] = by_segment(lax.broadcasted_iota(jnp.int32, (1, BQ), 1) + q_first, bits)
    column = lax.broadcasted_iota(jnp.int32, (BK, 1), 0) + k_first
    kcol_ref[...] = jnp.where(column >= 0, by_segment(column, powers), 0)
    line = lax.broadcasted_iota(jnp.int32, (1, BK), 1) + k_first
    kline_ref[0] = jnp.where(line >= 0, by_segment(line, powers), 0)

    def touches(begins, seg, span):
        return (starts[seg] <= begins + span - 1) & (starts[seg] + size[seg] > begins)

    @pl.when(step == 0)
    def _():
        for k in range(key_any.shape[0]):
            seen = jnp.int32(0)
            for seg in range(seg_count):
                seen = jnp.where(touches(begin - early + k * BK, seg, BK), seen | powers[seg], seen)
            key_any[k] = seen

    query_any, query_all = jnp.int32(0), jnp.int32(-1)
    for seg in range(seg_count):
        inside = touches(q_first, seg, BQ)
        query_any = jnp.where(inside, query_any | bits[seg], query_any)
        query_all = jnp.where(inside, query_all & bits[seg], query_all)
    for k in range(key_any.shape[0]):
        keys_at = begin - early + k * BK
        some = ((query_any & key_any[k]) != 0) & (keys_at <= q_first + BQ - 1)
        every = ((key_any[k] & ~query_all) == 0) & (keys_at + BK - 1 <= q_first)
        flags[step, k] = jnp.where(some, jnp.where(every, 2, 1), 0)


def tables(parents, lengths, group_tokens, planes):
    seg_count = parents.shape[1]
    early = (planes - 1) * group_tokens
    steps = group_tokens // BQ
    blocks = planes * group_tokens // BK
    i32 = lambda *shape: jax.ShapeDtypeStruct(shape, jnp.int32)
    smem = pl.BlockSpec(memory_space=pltpu.SMEM)
    return pl.pallas_call(
        partial(tables_body, group_tokens, early, seg_count),
        grid=(steps,),
        in_specs=[smem, smem],
        out_specs=[
            pl.BlockSpec((BQ, 1), lambda i: (i, 0)),
            pl.BlockSpec((BQ, 1), lambda i: (i, 0)),
            pl.BlockSpec((1, BQ), lambda i: (0, i)),
            pl.BlockSpec((1, 1, BK), lambda i: (i, 0, 0)),
            pl.BlockSpec((BK, 1), lambda i: (i, 0)),
            smem,
        ],
        out_shape=[
            i32(group_tokens, 1),
            i32(group_tokens, 1),
            i32(1, group_tokens),
            i32(blocks, 1, BK),
            i32(blocks * BK, 1),
            i32(steps, blocks),
        ],
        scratch_shapes=[pltpu.SMEM((blocks,), jnp.int32)],
        cost_estimate=QUICK,
        name="tables",
    )(parents, lengths)


def inner(left, right):
    return dg(left, right, TN)


def after(value, *others):
    return lax.optimization_barrier((value,) + others)[0]


def per_device(
    layer_in,
    out_grad,
    parents,
    lengths,
    attn_gain,
    mlp_gain,
    query_norm_gain,
    key_gain,
    query_weight,
    key_matrix,
    value_matrix,
    headgate_weight,
    output_weight,
    gate_weight,
    up_weight,
    down_weight,
):
    data_count = lax.axis_size("dp")
    model_count = lax.axis_size("mp")
    share, width = layer_in.shape
    rows_here = query_weight.shape[0]
    group_tokens = share * model_count * GROUP
    seg_count = parents.shape[1]
    far = [[member + GROUP * plane for plane in range(data_count // GROUP)] for member in range(GROUP)]
    planes = TREE_TOKENS // group_tokens

    gates = headgate_weight.shape[1] // GROUP
    pieces_gates = jnp.pad(
        headgate_weight.reshape(rows_here, GROUP, gates), ((0, 0), (0, 0), (0, HEAD_SIZE - gates))
    ).reshape(rows_here, GROUP * HEAD_SIZE)

    def far_gather(mine):
        return lax.all_gather(
            mine.reshape(GROUP * rows_here, -1), "dp", axis=0, tiled=True, axis_index_groups=far
        )

    def far_scatter(grad):
        mine = lax.psum_scatter(grad, "dp", scatter_dimension=0, tiled=True, axis_index_groups=far)
        return mine.reshape(GROUP, rows_here, -1)

    sizes = [attn_gain.shape[0], mlp_gain.shape[0], query_norm_gain.shape[0], key_gain.shape[0]]
    cuts = [sum(sizes[:i]) for i in range(5)]
    tile = (8, 128)
    spare = tile[0] * tile[1] - cuts[4]
    gain_tile = jnp.pad(
        jnp.concatenate([attn_gain, mlp_gain, query_norm_gain, key_gain]).astype(f32), (0, spare)
    ).reshape(tile)
    mine_attn, all_gains = trade_group([query_weight, key_matrix, value_matrix, pieces_gates], 3, small=gain_tile)
    full_attn = far_gather(mine_attn)
    gains = all_gains.transpose(2, 1, 0, 3, 4).reshape(data_count * model_count, -1)
    gain_one, gain_two, gain_query, gain_key = [
        gains[:, cuts[i] : cuts[i + 1]].reshape(-1) for i in range(4)
    ]
    head_gains = jnp.stack([gain_query, gain_key])
    mine_out = trade_group([after(output_weight.T, all_gains)], 4)
    full_out = far_gather(mine_out)

    positions, query_column, query_line, key_lines, key_column, flags = tables(parents, lengths, group_tokens, planes)
    cosine, sine = rope_tables(positions, HEAD_SIZE)
    early = (planes - 1) * group_tokens
    key_cut = early // BK

    rows = layer_in.astype(f32)
    normed_one, norm_one_back = jax.vjp(row_norm, rows, gain_one)
    hidden_first = gather_group(after(normed_one.astype(bf), mine_out))
    q_width = query_weight.shape[1] // GROUP
    k_width = key_matrix.shape[1] // GROUP
    heads = q_width // HEAD_SIZE
    raw, query, pair = prepare(hidden_first, full_attn, cosine, sine, head_gains)
    mine_glu, pair_early = trade_group([gate_weight, up_weight], 5, pair)
    full_glu = far_gather(mine_glu)
    query = after(query, mine_glu)
    own = attend(True, flags[:, key_cut:], query, pair, query_column, key_lines[key_cut:])
    mine_down = trade_group([after(down_weight.T, own[0])], 6)
    full_down = far_gather(mine_down)
    grad_tokens, attn, mixed, lse = gather_attend(
        after(out_grad, mine_down), query, pair_early, query_column, key_lines[:key_cut], own[0], own[1], raw, 19
    )
    branch = product_reduce(mixed, full_out, 2)
    middle = rows + branch

    normed_two, norm_two_back = jax.vjp(row_norm, middle, gain_two)
    h_two, both_glu, hidden = gather_product(normed_two.astype(bf), full_glu, 14)
    units = full_down.shape[1]

    down_part = inner(grad_tokens, hidden).astype(bf)
    down_rows = far_scatter(down_part)
    grad_glu = hidden_back(after(grad_tokens, down_part), full_down, both_glu)
    grad_h_two, glu_part = product_reduce(grad_glu, full_glu, 15, h_two)
    glu_rows = far_scatter(glu_part)
    grad_mid_norm, gain_two_grad = norm_two_back(grad_h_two)
    grad_middle = out_grad.astype(f32) + grad_mid_norm

    grad_branch, grad_attn, grad_logit, delta = gather_product(grad_middle.astype(bf), full_out, 16, [attn, raw])
    query_grad, early_grad = attend_back(
        False, flags[:, :key_cut], query, grad_attn, pair_early, query_line, key_column[:early], lse, delta
    )
    down_grad, out_part = trade_back([after(down_rows, early_grad)], ((units,),), 7, side=(grad_branch, mixed))
    out_rows = far_scatter(out_part)
    back = [early_grad, query, grad_attn, pair, query_line, key_column[early:], lse, delta, query_grad]
    last_branch, returned, query_grad, own_grad = product_reduce(after(hidden, out_part), full_down, 18, back=back)
    layer_out = (middle + last_branch).astype(bf)
    grad_raw, head_gain_grads = prepare_back(raw, cosine, sine, head_gains, query_grad, own_grad, returned, grad_logit)
    grad_h_one, attn_part = product_reduce(grad_raw, full_attn, 17, hidden_first)
    attn_rows = far_scatter(attn_part)
    grad_in_norm, gain_one_grad = norm_one_back(grad_h_one)
    input_grad = (grad_middle + grad_in_norm).astype(bf)

    devices = data_count * model_count
    gain_parts = jnp.concatenate(
        [
            piece.reshape(devices, -1)
            for piece in (gain_one_grad, gain_two_grad, head_gain_grads[0], head_gain_grads[1], jnp.zeros((devices, spare), f32))
        ],
        axis=1,
    )
    gain_parts = gain_parts.reshape((data_count // GROUP, GROUP, model_count) + tile).transpose(2, 1, 0, 3, 4)
    gate_grad, up_grad, out_weight_grad, gain_sums = trade_back(
        [after(glu_rows, grad_h_one), out_rows], ((units, units), (q_width,)), 8, small=gain_parts
    )
    gain_sums = gain_sums.reshape(-1)
    q_grad, k_grad, v_grad, gates_grad = trade_back(
        [after(attn_rows, gain_sums)], ((q_width, k_width, k_width, HEAD_SIZE),), 10
    )
    gates_grad = gates_grad.reshape(rows_here, GROUP, HEAD_SIZE)[:, :, :heads].reshape(rows_here, -1)
    return (
        layer_out,
        input_grad,
        gain_sums[cuts[0] : cuts[1]],
        gain_sums[cuts[1] : cuts[2]],
        gain_sums[cuts[2] : cuts[3]],
        gain_sums[cuts[3] : cuts[4]],
        q_grad.astype(f32),
        k_grad.astype(f32),
        v_grad.astype(f32),
        gates_grad.astype(f32),
        out_weight_grad.astype(f32).T,
        gate_grad.astype(f32),
        up_grad.astype(f32),
        down_grad.astype(f32).T,
    )


def solution(mesh):
    in_specs = (
        P(("dp", "mp"), None),
        P(("dp", "mp"), None),
        P(),
        P(),
        P(("dp", "mp")),
        P(("dp", "mp")),
        P(("dp", "mp")),
        P(("dp", "mp")),
        P("dp", "mp"),
        P("dp", "mp"),
        P("dp", "mp"),
        P("dp", "mp"),
        P("mp", "dp"),
        P("dp", "mp"),
        P("dp", "mp"),
        P("mp", "dp"),
    )
    out_specs = (
        P(("dp", "mp"), None),
        P(("dp", "mp"), None),
        P(("dp", "mp")),
        P(("dp", "mp")),
        P(("dp", "mp")),
        P(("dp", "mp")),
        P("dp", "mp"),
        P("dp", "mp"),
        P("dp", "mp"),
        P("dp", "mp"),
        P("mp", "dp"),
        P("dp", "mp"),
        P("dp", "mp"),
        P("mp", "dp"),
    )
    return jax.shard_map(
        per_device, mesh=mesh, in_specs=in_specs, out_specs=out_specs, check_vma=False
    )
```
